32 devices in a mesh: wide: 8 (over z, x), narrow: 4 (over y, core).
Axes of the slice: x: 2, y: 2, z: 4, core: 2. Of those that a mesh axis runs over, the one named last changes fastest.
Arguments:
- byte_values: int32 [32, 2048], P(('wide', 'narrow')), may hold values from 0 to 255, as said below
- row_lengths: int32 [32], P(('wide', 'narrow')), may hold values from 512 to 2048, as said below
- embedding: bfloat16 [256, 768], P('wide'), may hold values from -6 to 6
- conv_kernel: bfloat16 [4, 768], P(None, 'wide'), may hold values from -3 to 3
- score_vector: bfloat16 [768], P('wide'), may hold values from -0.4375 to 0.4375
- attn_gain: bfloat16 [768], P('wide'), may hold values from 0.5 to 1.5
- query_weight: bfloat16 [768, 768], P('wide'), may hold values from -0.21875 to 0.21875
- key_weight: bfloat16 [768, 768], P('wide'), may hold values from -0.21875 to 0.21875
- value_weight: bfloat16 [768, 768], P('wide'), may hold values from -0.21875 to 0.21875
- output_weight: bfloat16 [768, 768], P('wide'), may hold values from -3.5 to 3.5
- ffn_gain: bfloat16 [768], P('wide'), may hold values from 0.5 to 1.5
- gate_weight: bfloat16 [768, 2048], P('wide'), may hold values from -0.21875 to 0.21875
- up_weight: bfloat16 [768, 2048], P('wide'), may hold values from -0.21875 to 0.21875
- down_weight: bfloat16 [2048, 768], P('wide'), may hold values from -0.125 to 0.125
- cotangent: float32 [32, 1024, 768], P(('wide', 'narrow')), may hold values from -6 to 6
Outputs:
- layer_out: float32 [32, 1024, 768], P(('wide', 'narrow'))
- entropy: float32 [], replicated
- grad_embedding: float32 [256, 768], P('wide')
- grad_conv: float32 [4, 768], P(None, 'wide')
- grad_score: float32 [768], P('wide')
- grad_attn_gain: float32 [768], P('wide')
- grad_query: float32 [768, 768], P('wide')
- grad_key: float32 [768, 768], P('wide')
- grad_value: float32 [768, 768], P('wide')
- grad_output: float32 [768, 768], P('wide')
- grad_ffn_gain: float32 [768], P('wide')
- grad_gate: float32 [768, 2048], P('wide')
- grad_up: float32 [768, 2048], P('wide')
- grad_down: float32 [2048, 768], P('wide')
The draws below stay inside these ranges and needn't reach their ends.
Inputs may be any that keep to these rules, and one draw needn't show every extreme that they name: `row_lengths`: each row's length is 2048, 1024 or 512; about a third of the rows have 2048, four ninths 2048 / 2, two ninths 2048 / 4. `byte_values`: row r holds at most 2 ** (8 r // 32) distinct byte values.
All inputs are finite; a program needn't handle non-finite values.
Results may differ from the reference program's by a relative error of at most 0.018.
Values may be sent and summed in bfloat16 or wider, within the bound.
A program may use at most 384 MiB of HBM per device.

```python
import jax
import jax.numpy as jnp
from jax import lax

D = 768
HEADS = 12
FF = 2048
VOCAB = 256
MAXBLOCK = 4
KERNEL = 4
LB = 2048
ROWS = 32
POOLED_TOKENS = 1024


def draw_row_lengths(key, part):
    ordering = jax.random.permutation(jax.random.fold_in(key, 7), ROWS)
    category = ordering * 36 // ROWS
    return jnp.where(category < 12, LB, jnp.where(category < 28, LB // 2, LB // 4)).astype(jnp.int32)


def draw_byte_values(key, part):
    row_index = jnp.arange(ROWS, dtype=jnp.int32)
    alphabet = jnp.left_shift(jnp.int32(1), 8 * row_index // ROWS)
    offsets = jax.random.randint(jax.random.fold_in(key, 11), (ROWS,), 0, VOCAB, dtype=jnp.int32)
    raw_values = jax.random.randint(jax.random.fold_in(key, 13), (ROWS, LB), 0, VOCAB, dtype=jnp.int32)
    return (raw_values % alphabet[:, None] + offsets[:, None]) % VOCAB


def block_scale(key, extent, cuts, least, top_value):
    def one(dim, parts):
        draws = jax.random.uniform(jax.random.fold_in(jax.random.fold_in(key, 6), dim), (parts,), jnp.float32, least / len(cuts), top_value / len(cuts))
        return jnp.repeat(jnp.exp(draws), extent[dim] // parts).reshape((-1,) + (1,) * (len(extent) - dim - 1))

    factor_of = one(*cuts[0])
    for cut in cuts[1:]:
        factor_of = factor_of * one(*cut)
    return factor_of


def bell_draw(rng, dims, width, most, shards=(), kind=jnp.bfloat16):
    factor_of = block_scale(rng, dims, shards, -0.22, 0.18) if shards else 1.0
    values = jax.random.normal(rng, dims, jnp.float32) * width * factor_of
    return jnp.minimum(jnp.maximum(values, -most), most).astype(kind)


def setup_inputs(seed: int = 0) -> dict:
    streams_of = jax.random.split(jax.random.key(seed), 16)
    byte_values = draw_byte_values(jax.random.fold_in(streams_of[15], 71), 0)
    row_lengths = draw_row_lengths(jax.random.fold_in(streams_of[15], 71), 0)
    embedding = bell_draw(streams_of[2], (VOCAB, D), 1.0, 6.0, ((0, 8),))
    conv_kernel = bell_draw(streams_of[3], (KERNEL, D), 0.5, 3.0, ((1, 8),))
    score_vector = bell_draw(streams_of[4], (D,), (D // 4) ** -0.5, 0.4375, ((0, 8),))
    attn_gain = jnp.clip(1.0 + 0.1 * jax.random.normal(streams_of[5], (D,), jnp.float32), 0.5, 1.5).astype(jnp.bfloat16)
    query_weight = bell_draw(streams_of[6], (D, D), D ** -0.5, 0.21875, ((0, 8),))
    key_weight = bell_draw(streams_of[7], (D, D), D ** -0.5, 0.21875, ((0, 8),))
    value_weight = bell_draw(streams_of[8], (D, D), D ** -0.5, 0.21875, ((0, 8),))
    output_weight = bell_draw(streams_of[9], (D, D), (max(D * 4 // POOLED_TOKENS, 1)) ** -0.5, 3.5, ((0, 8),))
    ffn_gain = jnp.clip(1.0 + 0.1 * jax.random.normal(streams_of[10], (D,), jnp.float32), 0.5, 1.5).astype(jnp.bfloat16)
    gate_weight = bell_draw(streams_of[11], (D, FF), D ** -0.5, 0.21875, ((0, 8),))
    up_weight = bell_draw(streams_of[12], (D, FF), D ** -0.5, 0.21875, ((0, 8),))
    down_weight = bell_draw(streams_of[13], (FF, D), FF ** -0.5, 0.125, ((0, 8),))
    cotangent = bell_draw(streams_of[14], (ROWS, POOLED_TOKENS, D), 1.0, 6.0, ((0, 32),), jnp.float32)
    return {"byte_values": byte_values, "row_lengths": row_lengths, "embedding": embedding, "conv_kernel": conv_kernel, "score_vector": score_vector, "attn_gain": attn_gain, "query_weight": query_weight, "key_weight": key_weight, "value_weight": value_weight, "output_weight": output_weight, "ffn_gain": ffn_gain, "gate_weight": gate_weight, "up_weight": up_weight, "down_weight": down_weight, "cotangent": cotangent}


@jax.custom_vjp
def low(v):
    return lax.optimization_barrier(v.astype(jnp.bfloat16)).astype(jnp.float32)

@jax.custom_vjp
def low_back(v):
    return v

def low_keep(v):
    return (low(v), None)

def low_pass(kept, grad):
    return (grad,)

def back_keep(v):
    return (v, None)

def back_low(kept, grad):
    return (low(grad),)
low.defvjp(low_keep, low_pass)
low_back.defvjp(back_keep, back_low)
EPS = 1e-06
ENT_WEIGHT = 1.0
EXACT_MATMUL = lax.Precision.HIGHEST

def careful_matmul(left, right):
    return jnp.dot(left, right, precision=EXACT_MATMUL, preferred_element_type=jnp.float32)

def rms_norm(values, gain):
    return values * lax.rsqrt(lax.optimization_barrier(jnp.mean(values * values, axis=-1, keepdims=True)) + EPS) * gain

def pool_size(values, byte_valid_mask, block_len):
    positions = values.shape[-2]
    blocks = -(-positions // block_len)
    surplus = blocks * block_len - positions
    leading = values.shape[:-2]
    spread = [(0, 0)] * len(leading)
    padded = jnp.pad(values, spread + [(0, surplus), (0, 0)])
    block_sums = padded.reshape(leading + (blocks, block_len, values.shape[-1])).sum(axis=-2)
    counts = jnp.pad(byte_valid_mask, spread + [(0, surplus)]).reshape(leading + (blocks, block_len)).sum(axis=-1)
    averages = block_sums / jnp.maximum(counts, 1.0)[..., None]
    return jnp.repeat(averages, block_len, axis=-2)[..., :positions, :]

def gbst_block(byte_embeddings, byte_valid_mask, tok_mask, kernel, scorer):
    positions = byte_embeddings.shape[-2]
    taps = kernel.shape[0]
    spread = [(0, 0)] * (byte_embeddings.ndim - 2)
    padded = jnp.pad(byte_embeddings, spread + [(1, taps - 2), (0, 0)])
    convolved = kernel[0] * padded[..., 0:positions, :]
    for offset in range(1, taps):
        convolved = convolved + kernel[offset] * padded[..., offset:offset + positions, :]
    convolved = convolved * byte_valid_mask[..., None]
    pooled_all = [pool_size(convolved, byte_valid_mask, block_len) for block_len in range(1, MAXBLOCK + 1)]
    scores = jnp.stack([jnp.einsum('...ld,d->...l', pooled, scorer, precision=EXACT_MATMUL) for pooled in pooled_all])
    highest = lax.optimization_barrier(jnp.max(scores, axis=0))
    exponent = jnp.exp(scores - highest)
    totals = lax.optimization_barrier(jnp.sum(exponent, axis=0))
    chance = exponent / totals
    log_total = highest + jnp.log(totals)
    block_mixture = chance[0][..., None] * pooled_all[0]
    for index in range(1, MAXBLOCK):
        block_mixture = block_mixture + chance[index][..., None] * pooled_all[index]
    entropy_sum = jnp.sum(byte_valid_mask * (log_total - lax.optimization_barrier(jnp.sum(chance * scores, axis=0))))
    paired = block_mixture.reshape(block_mixture.shape[:-2] + (positions // 2, 2, block_mixture.shape[-1]))
    started = (paired[..., 0, :] + paired[..., 1, :]) * 0.5 * tok_mask[..., None]
    return (started, entropy_sum)

def gated_gelu(gate_in, up_in):
    return jax.nn.gelu(gate_in, approximate=True) * up_in

def layer_row(params, row_bytes, row_length):
    embedding, conv_kernel, score_vector, attn_gain, query_weight, key_weight, value_weight, output_weight, ffn_gain, gate_weight, up_weight, down_weight = params
    positions = row_bytes.shape[0]
    tokens = positions // 2
    byte_valid_mask = (jnp.arange(positions) < row_length).astype(jnp.float32)
    keep = 2 * jnp.arange(tokens) < row_length
    tok_mask = keep.astype(jnp.float32)
    byte_embeddings = jnp.take(embedding, row_bytes, axis=0) * byte_valid_mask[:, None]
    started, entropy_sum = gbst_block(byte_embeddings, byte_valid_mask, tok_mask, conv_kernel, score_vector)
    head_dim = query_weight.shape[0] // HEADS
    scale = head_dim ** (-0.5)
    normed = low(rms_norm(started, attn_gain))

    def project(weight):
        return low_back(low(careful_matmul(normed, weight))).reshape(tokens, HEADS, head_dim)
    queries = project(query_weight)
    keys = project(key_weight)
    values = project(value_weight)
    scores = low_back(jnp.einsum('qhd,khd->hqk', queries, keys, precision=EXACT_MATMUL) * scale)
    scores = jnp.where(keep[None, None, :], scores, -1e+30)
    highest = lax.optimization_barrier(jnp.max(scores, axis=-1, keepdims=True))
    exponent = jnp.exp(scores - highest)
    chance = exponent / lax.optimization_barrier(jnp.sum(exponent, axis=-1, keepdims=True))
    context = low_back(low(jnp.einsum('hqk,khd->qhd', low(chance), values, precision=EXACT_MATMUL)))
    context = context.reshape(tokens, HEADS * head_dim)
    middle = started + low_back(careful_matmul(context, output_weight))
    normed_two = low(rms_norm(middle, ffn_gain))
    gate_in = low_back(careful_matmul(normed_two, gate_weight))
    up_in = low_back(careful_matmul(normed_two, up_weight))
    hidden = low(gated_gelu(gate_in, up_in))
    return (middle + low_back(careful_matmul(hidden, down_weight)), entropy_sum)

def reference(byte_values, row_lengths, embedding, conv_kernel, score_vector, attn_gain, query_weight, key_weight, value_weight, output_weight, ffn_gain, gate_weight, up_weight, down_weight, cotangent):
    params = tuple((weight.astype(jnp.float32) for weight in (embedding, conv_kernel, score_vector, attn_gain, query_weight, key_weight, value_weight, output_weight, ffn_gain, gate_weight, up_weight, down_weight)))
    count = jnp.sum(row_lengths).astype(jnp.float32)

    def forward(weights):

        def per_row(running, inputs):
            row_bytes, row_length = inputs
            result, entropy_sum = layer_row(weights, row_bytes, row_length)
            return (running + entropy_sum, result)
        total, results = lax.scan(jax.checkpoint(per_row), jnp.float32(0.0), (byte_values, row_lengths))
        return (results, total / count)
    (layer_out, entropy), backward = jax.vjp(forward, params)
    grads, = backward((cotangent.astype(jnp.float32), jnp.float32(ENT_WEIGHT)))
    return (layer_out, entropy, grads[0], grads[1], grads[2], grads[3], grads[4], grads[5], grads[6], grads[7], grads[8], grads[9], grads[10], grads[11])
```

```python
import functools
import jax
import jax.numpy as jnp
from jax import lax
from jax.experimental import pallas as pl
from jax.experimental.pallas import tpu as pltpu
from jax.sharding import PartitionSpec as P

F32 = jnp.float32
BF16 = jnp.bfloat16
EPS = 1e-06
HEADS = 12
ENT_WEIGHT = 1.0
PERIOD = 12
GROUPS = 176
HIGH = lax.Precision.HIGHEST
VM = pl.BlockSpec(memory_space=pltpu.VMEM)
SM = pl.BlockSpec(memory_space=pltpu.SMEM)


def dot(a, b, dims=((1,), (0,)), precision=None):
    return lax.dot_general(a, b, (dims, ((), ())), precision=precision, preferred_element_type=F32)


def same_block(size):
    r = lax.broadcasted_iota(jnp.int32, (128, 128), 0)
    c = lax.broadcasted_iota(jnp.int32, (128, 128), 1)
    return jnp.where((r // size == c // size) & (r < PERIOD) & (c < PERIOD), 1.0, 0.0).astype(F32)


def block_sum(x, size):
    return dot(x, same_block(size), precision=HIGH)


def lane_scalars(csum, length):
    i = lax.broadcasted_iota(jnp.int32, (GROUPS, 128), 0)
    k = lax.broadcasted_iota(jnp.int32, (GROUPS, 128), 1)
    mask = jnp.where((PERIOD * i + k < length) & (k < PERIOD), 1.0, 0.0).astype(F32)
    tok = block_sum(jnp.where(k % 2 == 0, mask, 0.0), 2)
    inv = [jnp.ones_like(mask)] + [1.0 / jnp.maximum(block_sum(mask, b), 1.0) for b in (2, 3, 4)]
    scores = [csum] + [block_sum(csum, b) * inv[b - 1] for b in (2, 3, 4)]
    top = functools.reduce(jnp.maximum, scores)
    ex = [jnp.exp(s - top) for s in scores]
    total = ex[0] + ex[1] + ex[2] + ex[3]
    rec = 1.0 / total
    chance = [e * rec for e in ex]
    mean = sum(c * s for c, s in zip(chance, scores))
    ent = mask * (top + jnp.log(total) - mean)
    alpha = [c * v for c, v in zip(chance, inv)]
    return mask, tok, inv, scores, chance, mean, ent, alpha


def gbst_fwd_body(len_ref, bcol_ref, emb_ref, ck_ref, sc_ref, start_ref, conv_ref, csum_ref, ent_ref,
                  table, onehot, planes, coef, tiles):
    length = len_ref[0, 0]
    emb = emb_ref[...].astype(F32)
    for j in range(4):
        table[pl.ds(256 * j, 256), :] = (emb * ck_ref[pl.ds(j, 1), :].astype(F32)).astype(BF16)
    vocab = lax.broadcasted_iota(jnp.int32, (GROUPS, 256), 1)
    for k in range(PERIOD + 3):
        onehot[:, pl.ds(256 * k, 256)] = jnp.where(bcol_ref[:, k:k + 1] == vocab, 1.0, 0.0).astype(BF16)
    csum_ref[...] = jnp.zeros_like(csum_ref)
    s = sc_ref[...].astype(F32)
    rows = lax.broadcasted_iota(jnp.int32, (GROUPS, 1), 0)
    lane = lax.broadcasted_iota(jnp.int32, (GROUPS, 128), 1)

    def plane(k, _):
        lhs = onehot[:, pl.ds(pl.multiple_of(256 * k, 256), 1024)]
        out = dot(lhs, table[...])
        out = jnp.where(PERIOD * rows + k < length, out, 0.0)
        planes[k] = out
        conv_ref[k] = out.astype(BF16)
        c = jnp.sum(out * s, axis=1, keepdims=True)
        csum_ref[...] = jnp.where(lane == k, c, csum_ref[...])
        return 0

    lax.fori_loop(0, PERIOD, plane, 0)
    mask, tok, inv, scores, chance, mean, ent, alpha = lane_scalars(csum_ref[...], length)
    ent_ref[...] = jnp.sum(jnp.sum(ent, axis=0, keepdims=True), axis=1, keepdims=True) + jnp.zeros((8, 128), F32)
    half = 0.5 * tok
    coef[0] = (alpha[0] + block_sum(alpha[1], 2)) * half
    coef[1] = alpha[2] * half
    coef[2] = block_sum(alpha[2], 2) * half
    coef[3] = block_sum(alpha[3], 2) * half

    def rowblock(ib, _):
        r0 = pl.multiple_of(ib * 16, 16)
        rs = pl.ds(r0, 16)
        ce, c3, c3p, c4p = [coef[n, rs, :] for n in range(4)]
        for lt in range(6):
            ls = pl.ds(128 * lt, 128)
            p = [planes[k, rs, ls] for k in range(PERIOD)]
            pair = [p[2 * m] + p[2 * m + 1] for m in range(6)]
            quad = [pair[2 * y] + pair[2 * y + 1] for y in range(3)]
            tri = [p[3 * x] + p[3 * x + 1] + p[3 * x + 2] for x in range(4)]
            for m in range(6):
                a, b = 2 * m, 2 * m + 1
                out = ce[:, a:a + 1] * p[a] + ce[:, b:b + 1] * p[b] + c4p[:, a:a + 1] * quad[m // 2]
                if a // 3 == b // 3:
                    out = out + c3p[:, a:a + 1] * tri[a // 3]
                else:
                    out = out + c3[:, a:a + 1] * tri[a // 3] + c3[:, b:b + 1] * tri[b // 3]
                tiles[lt, pl.ds(6 * r0 + m, 16, stride=6), :] = out
        return 0

    lax.fori_loop(0, GROUPS // 16, rowblock, 0)
    for lt in range(6):
        start_ref[:, pl.ds(128 * lt, 128)] = tiles[lt, pl.ds(0, start_ref.shape[0]), :]


def gbst_fwd(length, bcol, emb, ck, sc):
    return pl.pallas_call(
        gbst_fwd_body,
        out_shape=(jax.ShapeDtypeStruct((1024, 768), F32),
                   jax.ShapeDtypeStruct((PERIOD, GROUPS, 768), BF16),
                   jax.ShapeDtypeStruct((GROUPS, 128), F32),
                   jax.ShapeDtypeStruct((8, 128), F32)),
        in_specs=[SM, VM, VM, VM, VM],
        out_specs=(VM, VM, VM, VM),
        scratch_shapes=[pltpu.VMEM((1024, 768), BF16), pltpu.VMEM((GROUPS, 256 * 15), BF16),
                        pltpu.VMEM((PERIOD, GROUPS, 768), F32), pltpu.VMEM((4, GROUPS, 128), F32),
                        pltpu.VMEM((6, 6 * GROUPS, 128), F32)],
        compiler_params=pltpu.CompilerParams(vmem_limit_bytes=60 << 20),
        name="gbst_fwd",
    )(length, bcol, emb, ck, sc)


def gbst_bwd_body(len_ref, invc_ref, brow_ref, emb_ref, ck_ref, sc_ref, dstart_ref, conv_ref, csum_ref,
                  gemb_ref, gconv_ref, gscore_ref, dm, dots, coef, dconv, onehot, tiles):
    for lt in range(6):
        tiles[lt, pl.ds(0, 1024), :] = dstart_ref[:, pl.ds(128 * lt, 128)]
        tiles[lt, pl.ds(1024, 6 * GROUPS - 1024), :] = jnp.zeros((6 * GROUPS - 1024, 128), F32)
    length = len_ref[0, 0]
    invc = invc_ref[0, 0]
    mask, tok, inv, scores, chance, mean, ent, alpha = lane_scalars(csum_ref[...], length)
    half = 0.5 * tok
    coef[0] = half
    lane16 = lax.broadcasted_iota(jnp.int32, (16, 128), 1)

    def first(ib, _):
        r0 = pl.multiple_of(ib * 16, 16)
        rs = pl.ds(r0, 16)
        h = coef[0, rs, :]
        acc = [jnp.zeros((16, 128), F32) for _ in range(26)]
        for lt in range(6):
            ls = pl.ds(128 * lt, 128)
            p = [conv_ref[k, rs, ls].astype(F32) for k in range(PERIOD)]
            quad = [(p[4 * y] + p[4 * y + 1]) + (p[4 * y + 2] + p[4 * y + 3]) for y in range(3)]
            tri = [p[3 * x] + p[3 * x + 1] + p[3 * x + 2] for x in range(4)]
            n = 0
            for m in range(6):
                d = tiles[lt, pl.ds(6 * r0 + m, 16, stride=6), :] * h[:, 2 * m:2 * m + 1]
                dm[m, rs, ls] = d
                for q in terms(m, p, quad, tri):
                    acc[n] = acc[n] + d * q
                    n += 1
        g1 = jnp.zeros((16, 128), F32)
        g3 = jnp.zeros((16, 128), F32)
        g4 = jnp.zeros((16, 128), F32)
        n = 0
        for m in range(6):
            a, b = 2 * m, 2 * m + 1
            v = [jnp.sum(acc[n + q], axis=1, keepdims=True) for q in range(len(TERMS[m]))]
            n += len(TERMS[m])
            g1 = jnp.where(lane16 == a, v[0], jnp.where(lane16 == b, v[1], g1))
            g4 = jnp.where((lane16 == a) | (lane16 == b), v[2], g4)
            g3 = jnp.where(lane16 == a, v[3], jnp.where(lane16 == b, v[-1], g3))
        dots[0, rs, :] = g1
        dots[1, rs, :] = g3
        dots[2, rs, :] = g4
        return 0

    lax.fori_loop(0, GROUPS // 16, first, 0)
    g1 = dots[0]
    dch = [g1, block_sum(g1, 2) * inv[1], dots[1] * inv[2], dots[2] * inv[3]]
    dmean = sum(c * d for c, d in zip(chance, dch))
    dsc = [c * (d - dmean) - invc * mask * c * (s - mean) for c, d, s in zip(chance, dch, scores)]
    w = dsc[0] + sum(block_sum(dsc[b - 1], b) * inv[b - 1] for b in (2, 3, 4))
    coef[0] = (alpha[0] + block_sum(alpha[1], 2)) * mask
    coef[1] = alpha[2]
    coef[2] = block_sum(alpha[2], 2)
    coef[3] = block_sum(alpha[3], 2)
    coef[4] = w * mask
    coef[5] = mask
    s = sc_ref[...].astype(F32)
    gscore_ref[...] = jnp.zeros_like(gscore_ref)
    dconv[pl.ds(PERIOD * GROUPS, 2304 - PERIOD * GROUPS), :] = jnp.zeros((2304 - PERIOD * GROUPS, 768), BF16)

    def second(ib, _):
        r0 = pl.multiple_of(ib * 16, 16)
        rs = pl.ds(r0, 16)
        ce, c3, c3p, c4p, cw, mk = [coef[n, rs, :] for n in range(6)]
        for lt in range(6):
            ls = pl.ds(128 * lt, 128)
            d = [dm[m, rs, ls] for m in range(6)]
            tri = [c3p[:, 0:1] * d[0] + c3[:, 2:3] * d[1], c3[:, 3:4] * d[1] + c3p[:, 4:5] * d[2],
                   c3p[:, 6:7] * d[3] + c3[:, 8:9] * d[4], c3[:, 9:10] * d[4] + c3p[:, 10:11] * d[5]]
            quad = [c4p[:, 4 * y:4 * y + 1] * d[2 * y] + c4p[:, 4 * y + 2:4 * y + 3] * d[2 * y + 1] for y in range(3)]
            st = s[:, 128 * lt:128 * lt + 128]
            gs = jnp.zeros((16, 128), F32)
            for k in range(PERIOD):
                wk = cw[:, k:k + 1]
                out = ce[:, k:k + 1] * d[k // 2] + mk[:, k:k + 1] * (tri[k // 3] + quad[k // 4]) + wk * st
                gs = gs + wk * conv_ref[k, rs, ls].astype(F32)
                dconv[pl.ds(pl.multiple_of(GROUPS * k + r0, 16), 16), ls] = out.astype(BF16)
            gscore_ref[:, ls] += gs[:8] + gs[8:]
        return 0

    lax.fori_loop(0, GROUPS // 16, second, 0)
    vocab = lax.broadcasted_iota(jnp.int32, (256, 2304), 0)
    emb = emb_ref[...].astype(F32)
    for j in range(4):
        onehot[...] = jnp.where(brow_ref[pl.ds(j, 1), :] == vocab, 1.0, 0.0).astype(BF16)
        g = dot(onehot[...], dconv[...])
        gconv_ref[pl.ds(j, 1), :] = jnp.sum(g * emb, axis=0, keepdims=True)
        part = g * ck_ref[pl.ds(j, 1), :].astype(F32)
        gemb_ref[...] = part if j == 0 else gemb_ref[...] + part


TERMS = {m: (1, 1, 4, 3) if (2 * m) // 3 == (2 * m + 1) // 3 else (1, 1, 4, 3, 3) for m in range(6)}


def terms(m, p, quad, tri):
    a, b = 2 * m, 2 * m + 1
    out = [p[a], p[b], quad[m // 2], tri[a // 3]]
    if a // 3 != b // 3:
        out.append(tri[b // 3])
    return out


def gbst_bwd(length, invc, brow, emb, ck, sc, dstart, conv, csum):
    return pl.pallas_call(
        gbst_bwd_body,
        out_shape=(jax.ShapeDtypeStruct((256, 768), F32),
                   jax.ShapeDtypeStruct((8, 768), F32),
                   jax.ShapeDtypeStruct((8, 768), F32)),
        in_specs=[SM, SM] + [VM] * 7,
        out_specs=(VM, VM, VM),
        scratch_shapes=[pltpu.VMEM((6, GROUPS, 768), F32), pltpu.VMEM((3, GROUPS, 128), F32),
                        pltpu.VMEM((6, GROUPS, 128), F32), pltpu.VMEM((2304, 768), BF16),
                        pltpu.VMEM((256, 2304), BF16), pltpu.VMEM((6, 6 * GROUPS, 128), F32)],
        compiler_params=pltpu.CompilerParams(vmem_limit_bytes=60 << 20),
        name="gbst_bwd",
    )(length, invc, brow, emb, ck, sc, dstart, conv, csum)


def byte_planes(byte_values, length):
    positions = byte_values.shape[0]
    real = jnp.where(jnp.arange(positions) < length, byte_values, -1)
    ext = jnp.pad(real, (1, PERIOD * (GROUPS + 2) - positions - 1), constant_values=-1)
    cols = ext.reshape(GROUPS + 2, PERIOD)
    wide = jnp.concatenate([cols[:GROUPS], cols[1:GROUPS + 1, :4]], axis=1)
    rows = wide.T
    brow = jnp.stack([jnp.pad(rows[j:j + PERIOD].reshape(-1), (0, 2304 - PERIOD * GROUPS), constant_values=-1)
                      for j in range(4)])
    return wide, brow

TOK = 1024
BLK = 256
NEG = -1e30


def rms_parts(x):
    return lax.rsqrt(jnp.mean(x * x, axis=1, keepdims=True) + EPS)


def head_lanes(h2, rows, dtype=BF16):
    lane = lax.broadcasted_iota(jnp.int32, (rows, 128), 1)
    return jnp.where(lane // 64 == h2, 1.0, 0.0).astype(dtype)


def split3(x):
    hi = x.astype(BF16).astype(F32)
    mid = (x - hi).astype(BF16).astype(F32)
    return hi, mid, x - hi - mid


def att_fwd_body(len_ref, start_ref, gain_ref, wq_ref, wk_ref, wv_ref, wo_ref,
                 qs_ref, k_ref, v_ref, ctx_ref, qx_ref, normed_ref, middle_ref,
                 kx, vext, kext, qxf):
    length = len_ref[0, 0]
    g = gain_ref[...].astype(F32)

    def project(r, _):
        rs = pl.ds(pl.multiple_of(r * BLK, BLK), BLK)
        x = start_ref[rs, :]
        n = (x * rms_parts(x) * g).astype(BF16)
        normed_ref[rs, :] = n
        qs_ref[rs, :] = (dot(n, wq_ref[...]).astype(BF16).astype(F32) * 0.125).astype(BF16)
        k_ref[rs, :] = dot(n, wk_ref[...]).astype(BF16)
        v_ref[rs, :] = dot(n, wv_ref[...]).astype(BF16)
        return 0

    lax.fori_loop(0, TOK // BLK, project, 0)
    lane = lax.broadcasted_iota(jnp.int32, (TOK, 128), 1)
    row = lax.broadcasted_iota(jnp.int32, (TOK, 128), 0)
    keep = 2 * row < length
    kx[...] = jnp.where((lane == 0) & ~keep, NEG, 0.0).astype(BF16)
    ones = jnp.where(keep, 1.0, 0.0).astype(BF16)
    for h2 in range(2):
        vext[h2, :, pl.ds(128, 128)] = ones
        kext[h2, :, pl.ds(128, 128)] = kx[...]
    qxf[...] = jnp.where(lane == 0, 1.0, 0.0).astype(F32)
    lane_b = lax.broadcasted_iota(jnp.int32, (BLK, 128), 1)
    first = jnp.where(lane_b == 0, 1.0, 0.0).astype(BF16)

    def pair(p, _):
        ls = pl.ds(pl.multiple_of(p * 128, 128), 128)
        for h2 in range(2):
            hm = head_lanes(h2, TOK)
            vext[h2, :, pl.ds(0, 128)] = v_ref[:, ls] * hm
            kext[h2, :, pl.ds(0, 128)] = k_ref[:, ls] * hm

        def qblock(r, _):
            rs = pl.ds(pl.multiple_of(r * BLK, BLK), BLK)
            q = jnp.concatenate([qs_ref[rs, ls], first], axis=1)
            out = jnp.zeros((BLK, 128), F32)
            upd = qxf[rs, :]
            for h2 in range(2):
                s = dot(q, kext[h2], ((1,), (1,)))
                m = jnp.max(s, axis=1, keepdims=True)
                e = jnp.exp(s - m).astype(BF16)
                c = dot(e, vext[h2])
                total = c[:, 128:]
                out = out + c[:, :128] * (1.0 / total)
                hi, mid, lo = split3(-(m + jnp.log(total)))
                base = 1 + 3 * (2 * p + h2)
                upd = jnp.where(lane_b == base, hi, jnp.where(lane_b == base + 1, mid,
                                jnp.where(lane_b == base + 2, lo, upd)))
            qxf[rs, :] = upd
            ctx_ref[rs, ls] = out.astype(BF16)
            return 0

        lax.fori_loop(0, TOK // BLK, qblock, 0)
        return 0

    lax.fori_loop(0, HEADS // 2, pair, 0)
    qx_ref[...] = qxf[...].astype(BF16)

    def outproj(r, _):
        rs = pl.ds(pl.multiple_of(r * BLK, BLK), BLK)
        middle_ref[rs, :] = start_ref[rs, :] + dot(ctx_ref[rs, :], wo_ref[...])
        return 0

    lax.fori_loop(0, TOK // BLK, outproj, 0)


def att_fwd(length, start, gain, wq, wk, wv, wo):
    b = jax.ShapeDtypeStruct((TOK, 768), BF16)
    return pl.pallas_call(
        att_fwd_body,
        out_shape=(b, b, b, b, jax.ShapeDtypeStruct((TOK, 128), BF16), b, jax.ShapeDtypeStruct((TOK, 768), F32)),
        in_specs=[SM] + [VM] * 6,
        out_specs=(VM,) * 7,
        scratch_shapes=[pltpu.VMEM((TOK, 128), BF16), pltpu.VMEM((2, TOK, 256), BF16),
                        pltpu.VMEM((2, TOK, 256), BF16), pltpu.VMEM((TOK, 128), F32)],
        compiler_params=pltpu.CompilerParams(vmem_limit_bytes=60 << 20),
        name="att_fwd",
    )(length, start, gain, wq, wk, wv, wo)


def att_bwd_body(len_ref, dmid_ref, start_ref, gain_ref, qs_ref, k_ref, v_ref, ctx_ref, qx_ref, normed_ref,
                 wq_ref, wk_ref, wv_ref, wo_ref,
                 gq_ref, gk_ref, gv_ref, go_ref, dstart_ref, ggain_ref,
                 dctx, dx, dq, dk, dv, dqt, qcat, ocat, low):
    length = len_ref[0, 0]
    low[...] = dmid_ref[...].astype(BF16)
    lane_s = lax.broadcasted_iota(jnp.int32, (768, 128), 1)
    row_s = lax.broadcasted_iota(jnp.int32, (768, 128), 0)
    sel = jnp.where(lane_s // 3 == row_s // 64, 1.0, 0.0).astype(BF16)
    lane_b = lax.broadcasted_iota(jnp.int32, (BLK, 128), 1)

    def head(r, _):
        rs = pl.ds(pl.multiple_of(r * BLK, BLK), BLK)
        d = dot(low[rs, :], wo_ref[...], ((1,), (1,))).astype(BF16)
        dctx[rs, :] = d
        prod = d.astype(F32) * ctx_ref[rs, :].astype(F32)
        hi = prod.astype(BF16)
        delta = dot(hi, sel) + dot((prod - hi.astype(F32)).astype(BF16), sel)
        a, b, c = split3(-delta)
        dx[rs, :] = jnp.where(lane_b % 3 == 0, a, jnp.where(lane_b % 3 == 1, b, c)).astype(BF16)
        return 0

    lax.fori_loop(0, TOK // BLK, head, 0)

    def gout(c, _):
        cs = pl.ds(pl.multiple_of(c * BLK, BLK), BLK)
        go_ref[cs, :] = dot(ctx_ref[:, cs], low[...], ((0,), (0,))).astype(BF16)
        return 0

    lax.fori_loop(0, 3, gout, 0)
    qcat[:, pl.ds(128, 128)] = qx_ref[...]
    ocat[:, pl.ds(128, 128)] = dx[...]
    row_b = lax.broadcasted_iota(jnp.int32, (BLK, 128), 0)

    def pair(p, _):
        ls = pl.ds(pl.multiple_of(p * 128, 128), 128)
        qcat[:, pl.ds(0, 128)] = qs_ref[:, ls]
        ocat[:, pl.ds(0, 128)] = dctx[:, ls]
        dqt[...] = jnp.zeros_like(dqt)

        def kblock(r, _):
            rs = pl.ds(pl.multiple_of(r * BLK, BLK), BLK)
            bias = jnp.where((lane_b == 0) & (2 * (row_b + r * BLK) >= length), NEG, 0.0)
            dvb = jnp.zeros((BLK, 128), F32)
            dkb = jnp.zeros((BLK, 128), F32)
            dqb = dqt[...]
            for h2 in range(2):
                hm = head_lanes(h2, BLK)
                hd = 3 * (2 * p + h2)
                km = k_ref[rs, ls] * hm
                vm = v_ref[rs, ls] * hm
                kxl = jnp.where((lane_b > hd) & (lane_b <= hd + 3), 1.0, bias).astype(BF16)
                vxl = jnp.where((lane_b >= hd) & (lane_b < hd + 3), 1.0, 0.0).astype(BF16)
                st = dot(jnp.concatenate([km, kxl], axis=1), qcat[...], ((1,), (1,)))
                dp = dot(jnp.concatenate([vm, vxl], axis=1), ocat[...], ((1,), (1,)))
                prob = jnp.exp(st)
                dsc = (prob * dp).astype(BF16)
                dvb = dvb + dot(prob.astype(BF16), ocat[:, pl.ds(0, 128)]) * hm.astype(F32)
                dkb = dkb + dot(dsc, qcat[:, pl.ds(0, 128)]) * hm.astype(F32)
                dqb = dqb + dot(km, dsc, ((0,), (0,)))
            dv[rs, ls] = dvb.astype(BF16)
            dk[rs, ls] = dkb.astype(BF16)
            dqt[...] = dqb
            return 0

        lax.fori_loop(0, TOK // BLK, kblock, 0)
        dq[:, ls] = (dqt[...].T * 0.125).astype(BF16)
        return 0

    lax.fori_loop(0, HEADS // 2, pair, 0)

    def wgrad(c, _):
        cs = pl.ds(pl.multiple_of(c * BLK, BLK), BLK)
        n = normed_ref[:, cs]
        gq_ref[cs, :] = dot(n, dq[...], ((0,), (0,))).astype(BF16)
        gk_ref[cs, :] = dot(n, dk[...], ((0,), (0,))).astype(BF16)
        gv_ref[cs, :] = dot(n, dv[...], ((0,), (0,))).astype(BF16)
        return 0

    lax.fori_loop(0, 3, wgrad, 0)
    ggain_ref[...] = jnp.zeros_like(ggain_ref)
    g = gain_ref[...].astype(F32)

    def tail(r, _):
        rs = pl.ds(pl.multiple_of(r * BLK, BLK), BLK)
        d = (dot(dq[rs, :], wq_ref[...], ((1,), (1,))) + dot(dk[rs, :], wk_ref[...], ((1,), (1,)))
             + dot(dv[rs, :], wv_ref[...], ((1,), (1,))))
        dxv, gg = rms_back(start_ref[rs, :], g, d)
        dstart_ref[rs, :] = dmid_ref[rs, :] + dxv
        ggain_ref[...] += gg
        return 0

    lax.fori_loop(0, TOK // BLK, tail, 0)


def rms_back(x, g, d):
    s = rms_parts(x)
    xn = x * s
    dxn = d * xn
    gg = jnp.sum(dxn.reshape(x.shape[0] // 8, 8, x.shape[1]), axis=0)
    return s * (d * g - xn * jnp.mean(dxn * g, axis=1, keepdims=True)), gg


def att_bwd(length, dmid, start, gain, qs, k, v, ctx, qx, normed, wq, wk, wv, wo):
    w = jax.ShapeDtypeStruct((768, 768), BF16)
    act = pltpu.VMEM((TOK, 768), BF16)
    return pl.pallas_call(
        att_bwd_body,
        out_shape=(w, w, w, w, jax.ShapeDtypeStruct((TOK, 768), F32), jax.ShapeDtypeStruct((8, 768), F32)),
        in_specs=[SM] + [VM] * 13,
        out_specs=(VM,) * 6,
        scratch_shapes=[act, pltpu.VMEM((TOK, 128), BF16), act, act, act, pltpu.VMEM((128, TOK), F32),
                        pltpu.VMEM((TOK, 256), BF16), pltpu.VMEM((TOK, 256), BF16), act],
        compiler_params=pltpu.CompilerParams(vmem_limit_bytes=60 << 20),
        name="att_bwd",
    )(length, dmid, start, gain, qs, k, v, ctx, qx, normed, wq, wk, wv, wo)


C0 = 0.7978845608028654
C1 = 0.044715


def ffn_body(middle_ref, gain_ref, cot_ref, wg_ref, wu_ref, wd_ref,
             out_ref, gg_ref, gu_ref, gd_ref, dmid_ref, ggain_ref,
             n2, n2t, top, dn2, hid, dg, du):
    f = pl.program_id(0)
    g2 = gain_ref[...].astype(F32)

    @pl.when(f == 0)
    def _():
        def prep(r, _):
            rs = pl.ds(pl.multiple_of(r * BLK, BLK), BLK)
            x = middle_ref[rs, :]
            n = x * rms_parts(x) * g2
            n2[rs, :] = n.astype(BF16)
            n2t[:, rs] = n.T.astype(BF16)
            top[rs, :] = cot_ref[rs, :].astype(BF16)
            out_ref[rs, :] = x
            dn2[rs, :] = jnp.zeros((BLK, 768), F32)
            return 0
        lax.fori_loop(0, TOK // BLK, prep, 0)

    def rows(r, _):
        rs = pl.ds(pl.multiple_of(r * BLK, BLK), BLK)
        n = n2[rs, :]
        v = dot(n, wg_ref[...])
        u = dot(n, wu_ref[...])
        dh = dot(top[rs, :], wd_ref[...], ((1,), (1,)))
        v2 = v * v
        t = jnp.tanh(v * (C0 + (C0 * C1) * v2))
        hp = 0.5 + 0.5 * t
        gelu = v * hp
        slope = hp + (0.5 * v) * (1.0 - t * t) * (C0 + (3.0 * C0 * C1) * v2)
        h = (gelu * u).astype(BF16)
        hid[rs, :] = h
        a = (dh * u * slope).astype(BF16)
        b = (dh * gelu).astype(BF16)
        dg[rs, :] = a
        du[rs, :] = b
        out_ref[rs, :] += dot(h, wd_ref[...])
        dn2[rs, :] += dot(a, wg_ref[...], ((1,), (1,))) + dot(b, wu_ref[...], ((1,), (1,)))
        return 0

    lax.fori_loop(0, TOK // BLK, rows, 0)
    gg_ref[...] = dot(n2t[...], dg[...]).astype(BF16)
    gu_ref[...] = dot(n2t[...], du[...]).astype(BF16)
    gd_ref[...] = dot(hid[...], top[...], ((0,), (0,))).astype(BF16)

    @pl.when(f == pl.num_programs(0) - 1)
    def _():
        ggain_ref[...] = jnp.zeros_like(ggain_ref)

        def fin(r, _):
            rs = pl.ds(pl.multiple_of(r * BLK, BLK), BLK)
            dxv, gg = rms_back(middle_ref[rs, :], g2, dn2[rs, :])
            dmid_ref[rs, :] = cot_ref[rs, :] + dxv
            ggain_ref[...] += gg
            return 0
        lax.fori_loop(0, TOK // BLK, fin, 0)


def ffn(middle, gain, cot, wg, wu, wd):
    ff = wg.shape[1]
    whole = lambda *s: pl.BlockSpec(s, lambda f: (0, 0), pipeline_mode=pl.Buffered(1))
    act = jax.ShapeDtypeStruct((TOK, 768), F32)
    wide = pl.BlockSpec((768, BLK), lambda f: (0, f))
    tall = pl.BlockSpec((BLK, 768), lambda f: (f, 0))
    return pl.pallas_call(
        ffn_body,
        grid=(ff // BLK,),
        out_shape=(act, jax.ShapeDtypeStruct((768, ff), BF16), jax.ShapeDtypeStruct((768, ff), BF16),
                   jax.ShapeDtypeStruct((ff, 768), BF16), act, jax.ShapeDtypeStruct((8, 768), F32)),
        in_specs=[whole(TOK, 768), whole(1, 768), whole(TOK, 768), wide, wide, tall],
        out_specs=(whole(TOK, 768), wide, wide, tall, whole(TOK, 768), whole(8, 768)),
        scratch_shapes=[pltpu.VMEM((TOK, 768), BF16), pltpu.VMEM((768, TOK), BF16), pltpu.VMEM((TOK, 768), BF16),
                        pltpu.VMEM((TOK, 768), F32)] + [pltpu.VMEM((TOK, BLK), BF16)] * 3,
        compiler_params=pltpu.CompilerParams(vmem_limit_bytes=60 << 20),
        name="ffn",
    )(middle, gain, cot, wg, wu, wd)


def body(
    byte_values, row_lengths, embedding, conv_kernel, score_vector, attn_gain, query_weight, key_weight,
    value_weight, output_weight, ffn_gain, gate_weight, up_weight, down_weight, cotangent,
):
    gather = lambda x, axis=0: lax.all_gather(x, "wide", axis=axis, tiled=True)
    emb, ck = gather(embedding), gather(conv_kernel, 1)
    sc, g1, g2 = [gather(x).reshape(1, 768) for x in (score_vector, attn_gain, ffn_gain)]
    wq, wk, wv, wo = [gather(w) for w in (query_weight, key_weight, value_weight, output_weight)]
    wg, wu, wd = [gather(w) for w in (gate_weight, up_weight, down_weight)]
    length = row_lengths.reshape(1, 1)
    bcol, brow = byte_planes(byte_values[0], row_lengths[0])
    start, conv, csum, ent = gbst_fwd(length, bcol, emb, ck, sc)
    count, entropy_total = lax.psum((row_lengths[0].astype(F32), ent[0, 0]), ("wide", "narrow"))
    entropy = entropy_total / count
    qs, k, v, ctx, qx, normed, middle = att_fwd(length, start, g1, wq, wk, wv, wo)
    out, gg, gu, gd, dmid, gg2 = ffn(middle, g2, cotangent[0], wg, wu, wd)
    gq, gk, gv, go, dstart, gg1 = att_bwd(length, dmid, start, g1, qs, k, v, ctx, qx, normed, wq, wk, wv, wo)
    ge, gc, gs = gbst_bwd(length, (ENT_WEIGHT / count).reshape(1, 1), brow, emb, ck, sc, dstart, conv, csum)

    def scatter(x, axis=0):
        part = lax.psum_scatter(x.astype(BF16), "wide", scatter_dimension=axis, tiled=True)
        return lax.psum(part, "narrow").astype(F32)

    return (out[None], entropy, scatter(ge), scatter(gc[:4], 1), scatter(gs.sum(0)), scatter(gg1.sum(0)),
            scatter(gq), scatter(gk), scatter(gv), scatter(go), scatter(gg2.sum(0)),
            scatter(gg), scatter(gu), scatter(gd))


def solution(mesh):
    both = ("wide", "narrow")
    row, flat = P("wide", None), P("wide")
    return jax.shard_map(
        body,
        mesh=mesh,
        in_specs=(P(both, None), P(both), row, P(None, "wide"), flat, flat, row, row, row, row, flat,
                  row, row, row, P(both, None, None)),
        out_specs=(P(both, None, None), P(), row, P(None, "wide"), flat, flat, row, row, row, row, flat,
                   row, row, row),
        check_vma=False,
    )
```

```python
import functools
import jax
import jax.numpy as jnp
from jax import lax
from jax.experimental import pallas as pl
from jax.experimental.pallas import tpu as pltpu
from jax.sharding import PartitionSpec as P

F32 = jnp.float32
BF16 = jnp.bfloat16
EPS = 1e-06
HEADS = 12
ENT_WEIGHT = 1.0
PERIOD = 12
GROUPS = 176
HIGH = lax.Precision.HIGHEST
VM = pl.BlockSpec(memory_space=pltpu.VMEM)
SM = pl.BlockSpec(memory_space=pltpu.SMEM)


def dot(a, b, dims=((1,), (0,)), precision=None):
    return lax.dot_general(a, b, (dims, ((), ())), precision=precision, preferred_element_type=F32)


def same_block(size):
    r = lax.broadcasted_iota(jnp.int32, (128, 128), 0)
    c = lax.broadcasted_iota(jnp.int32, (128, 128), 1)
    return jnp.where((r // size == c // size) & (r < PERIOD) & (c < PERIOD), 1.0, 0.0).astype(F32)


def block_sum(x, size):
    return dot(x, same_block(size), precision=HIGH)


def lane_scalars(csum, length):
    i = lax.broadcasted_iota(jnp.int32, (GROUPS, 128), 0)
    k = lax.broadcasted_iota(jnp.int32, (GROUPS, 128), 1)
    mask = jnp.where((PERIOD * i + k < length) & (k < PERIOD), 1.0, 0.0).astype(F32)
    tok = block_sum(jnp.where(k % 2 == 0, mask, 0.0), 2)
    inv = [jnp.ones_like(mask)] + [1.0 / jnp.maximum(block_sum(mask, b), 1.0) for b in (2, 3, 4)]
    scores = [csum] + [block_sum(csum, b) * inv[b - 1] for b in (2, 3, 4)]
    top = functools.reduce(jnp.maximum, scores)
    ex = [jnp.exp(s - top) for s in scores]
    total = ex[0] + ex[1] + ex[2] + ex[3]
    rec = 1.0 / total
    chance = [e * rec for e in ex]
    mean = sum(c * s for c, s in zip(chance, scores))
    ent = mask * (top + jnp.log(total) - mean)
    alpha = [c * v for c, v in zip(chance, inv)]
    return mask, tok, inv, scores, chance, mean, ent, alpha


def gbst_fwd_body(tick, params, len_ref, bcol_ref, start_ref, conv_ref, csum_ref, ent_ref,
                  table, onehot, planes, coef, tiles):
    length = len_ref[0, 0]
    vocab = lax.broadcasted_iota(jnp.int32, (GROUPS, 256), 1)
    for k in range(PERIOD + 3):
        onehot[:, pl.ds(256 * k, 256)] = jnp.where(bcol_ref[:, k:k + 1] == vocab, 1.0, 0.0).astype(BF16)
    csum_ref[...] = jnp.zeros_like(csum_ref)
    tick("onehot", 0)
    emb, small = params()
    for j in range(4):
        table[pl.ds(256 * j, 256), :] = (emb * small[j:j + 1]).astype(BF16)
    s = small[4:5]
    tick("table", 0)
    rows = lax.broadcasted_iota(jnp.int32, (GROUPS, 1), 0)
    lane = lax.broadcasted_iota(jnp.int32, (GROUPS, 128), 1)

    def plane(k, _):
        tick("plane", k)
        lhs = onehot[:, pl.ds(pl.multiple_of(256 * k, 256), 1024)]
        out = dot(lhs, table[...])
        out = jnp.where(PERIOD * rows + k < length, out, 0.0)
        planes[k] = out
        conv_ref[k] = out.astype(BF16)
        c = jnp.sum(out * s, axis=1, keepdims=True)
        csum_ref[...] = jnp.where(lane == k, c, csum_ref[...])
        return 0

    lax.fori_loop(0, PERIOD, plane, 0)
    mask, tok, inv, scores, chance, mean, ent, alpha = lane_scalars(csum_ref[...], length)
    ent_ref[...] = jnp.sum(jnp.sum(ent, axis=0, keepdims=True), axis=1, keepdims=True) + jnp.zeros((8, 128), F32)
    half = 0.5 * tok
    coef[0] = (alpha[0] + block_sum(alpha[1], 2)) * half
    coef[1] = alpha[2] * half
    coef[2] = block_sum(alpha[2], 2) * half
    coef[3] = block_sum(alpha[3], 2) * half

    def rowblock(ib, _):
        tick("rows", ib)
        r0 = pl.multiple_of(ib * 16, 16)
        rs = pl.ds(r0, 16)
        ce, c3, c3p, c4p = [coef[n, rs, :] for n in range(4)]
        for lt in range(6):
            ls = pl.ds(128 * lt, 128)
            p = [planes[k, rs, ls] for k in range(PERIOD)]
            pair = [p[2 * m] + p[2 * m + 1] for m in range(6)]
            quad = [pair[2 * y] + pair[2 * y + 1] for y in range(3)]
            tri = [p[3 * x] + p[3 * x + 1] + p[3 * x + 2] for x in range(4)]
            for m in range(6):
                a, b = 2 * m, 2 * m + 1
                out = ce[:, a:a + 1] * p[a] + ce[:, b:b + 1] * p[b] + c4p[:, a:a + 1] * quad[m // 2]
                if a // 3 == b // 3:
                    out = out + c3p[:, a:a + 1] * tri[a // 3]
                else:
                    out = out + c3[:, a:a + 1] * tri[a // 3] + c3[:, b:b + 1] * tri[b // 3]
                tiles[lt, pl.ds(6 * r0 + m, 16, stride=6), :] = out
        return 0

    lax.fori_loop(0, GROUPS // 16, rowblock, 0)
    for lt in range(6):
        start_ref[:, pl.ds(128 * lt, 128)] = tiles[lt, pl.ds(0, start_ref.shape[0]), :]


def gbst_bwd_body(len_ref, invc_ref, brow_ref, emb_ref, ck_ref, sc_ref, dstart_ref, conv_ref, csum_ref,
                  gemb_ref, gconv_ref, gscore_ref, dm, dots, coef, dconv, onehot, tiles):
    for lt in range(6):
        tiles[lt, pl.ds(0, 1024), :] = dstart_ref[:, pl.ds(128 * lt, 128)]
        tiles[lt, pl.ds(1024, 6 * GROUPS - 1024), :] = jnp.zeros((6 * GROUPS - 1024, 128), F32)
    length = len_ref[0, 0]
    invc = invc_ref[0, 0]
    mask, tok, inv, scores, chance, mean, ent, alpha = lane_scalars(csum_ref[...], length)
    half = 0.5 * tok
    coef[0] = half
    lane16 = lax.broadcasted_iota(jnp.int32, (16, 128), 1)

    def first(ib, _):
        r0 = pl.multiple_of(ib * 16, 16)
        rs = pl.ds(r0, 16)
        h = coef[0, rs, :]
        acc = [jnp.zeros((16, 128), F32) for _ in range(26)]
        for lt in range(6):
            ls = pl.ds(128 * lt, 128)
            p = [conv_ref[k, rs, ls].astype(F32) for k in range(PERIOD)]
            quad = [(p[4 * y] + p[4 * y + 1]) + (p[4 * y + 2] + p[4 * y + 3]) for y in range(3)]
            tri = [p[3 * x] + p[3 * x + 1] + p[3 * x + 2] for x in range(4)]
            n = 0
            for m in range(6):
                d = tiles[lt, pl.ds(6 * r0 + m, 16, stride=6), :] * h[:, 2 * m:2 * m + 1]
                dm[m, rs, ls] = d
                for q in terms(m, p, quad, tri):
                    acc[n] = acc[n] + d * q
                    n += 1
        g1 = jnp.zeros((16, 128), F32)
        g3 = jnp.zeros((16, 128), F32)
        g4 = jnp.zeros((16, 128), F32)
        n = 0
        for m in range(6):
            a, b = 2 * m, 2 * m + 1
            v = [jnp.sum(acc[n + q], axis=1, keepdims=True) for q in range(len(TERMS[m]))]
            n += len(TERMS[m])
            g1 = jnp.where(lane16 == a, v[0], jnp.where(lane16 == b, v[1], g1))
            g4 = jnp.where((lane16 == a) | (lane16 == b), v[2], g4)
            g3 = jnp.where(lane16 == a, v[3], jnp.where(lane16 == b, v[-1], g3))
        dots[0, rs, :] = g1
        dots[1, rs, :] = g3
        dots[2, rs, :] = g4
        return 0

    lax.fori_loop(0, GROUPS // 16, first, 0)
    g1 = dots[0]
    dch = [g1, block_sum(g1, 2) * inv[1], dots[1] * inv[2], dots[2] * inv[3]]
    dmean = sum(c * d for c, d in zip(chance, dch))
    dsc = [c * (d - dmean) - invc * mask * c * (s - mean) for c, d, s in zip(chance, dch, scores)]
    w = dsc[0] + sum(block_sum(dsc[b - 1], b) * inv[b - 1] for b in (2, 3, 4))
    coef[0] = (alpha[0] + block_sum(alpha[1], 2)) * mask
    coef[1] = alpha[2]
    coef[2] = block_sum(alpha[2], 2)
    coef[3] = block_sum(alpha[3], 2)
    coef[4] = w * mask
    coef[5] = mask
    s = sc_ref[...].astype(F32)
    gscore_ref[...] = jnp.zeros_like(gscore_ref)
    dconv[pl.ds(PERIOD * GROUPS, 2304 - PERIOD * GROUPS), :] = jnp.zeros((2304 - PERIOD * GROUPS, 768), BF16)

    def second(ib, _):
        r0 = pl.multiple_of(ib * 16, 16)
        rs = pl.ds(r0, 16)
        ce, c3, c3p, c4p, cw, mk = [coef[n, rs, :] for n in range(6)]
        for lt in range(6):
            ls = pl.ds(128 * lt, 128)
            d = [dm[m, rs, ls] for m in range(6)]
            tri = [c3p[:, 0:1] * d[0] + c3[:, 2:3] * d[1], c3[:, 3:4] * d[1] + c3p[:, 4:5] * d[2],
                   c3p[:, 6:7] * d[3] + c3[:, 8:9] * d[4], c3[:, 9:10] * d[4] + c3p[:, 10:11] * d[5]]
            quad = [c4p[:, 4 * y:4 * y + 1] * d[2 * y] + c4p[:, 4 * y + 2:4 * y + 3] * d[2 * y + 1] for y in range(3)]
            st = s[:, 128 * lt:128 * lt + 128]
            gs = jnp.zeros((16, 128), F32)
            for k in range(PERIOD):
                wk = cw[:, k:k + 1]
                out = ce[:, k:k + 1] * d[k // 2] + mk[:, k:k + 1] * (tri[k // 3] + quad[k // 4]) + wk * st
                gs = gs + wk * conv_ref[k, rs, ls].astype(F32)
                dconv[pl.ds(pl.multiple_of(GROUPS * k + r0, 16), 16), ls] = out.astype(BF16)
            gscore_ref[:, ls] += gs[:8] + gs[8:]
        return 0

    lax.fori_loop(0, GROUPS // 16, second, 0)
    vocab = lax.broadcasted_iota(jnp.int32, (256, 2304), 0)
    emb = emb_ref[...].astype(F32)
    for j in range(4):
        onehot[...] = jnp.where(brow_ref[pl.ds(j, 1), :] == vocab, 1.0, 0.0).astype(BF16)
        g = dot(onehot[...], dconv[...])
        gconv_ref[pl.ds(j, 1), :] = jnp.sum(g * emb, axis=0, keepdims=True)
        part = g * ck_ref[pl.ds(j, 1), :].astype(F32)
        gemb_ref[...] = part if j == 0 else gemb_ref[...] + part


TERMS = {m: (1, 1, 4, 3) if (2 * m) // 3 == (2 * m + 1) // 3 else (1, 1, 4, 3, 3) for m in range(6)}


def terms(m, p, quad, tri):
    a, b = 2 * m, 2 * m + 1
    out = [p[a], p[b], quad[m // 2], tri[a // 3]]
    if a // 3 != b // 3:
        out.append(tri[b // 3])
    return out


def gbst_bwd(length, invc, brow, emb, ck, sc, dstart, conv, csum):
    return pl.pallas_call(
        gbst_bwd_body,
        out_shape=(jax.ShapeDtypeStruct((256, 768), F32),
                   jax.ShapeDtypeStruct((8, 768), F32),
                   jax.ShapeDtypeStruct((8, 768), F32)),
        in_specs=[SM, SM] + [VM] * 7,
        out_specs=(VM, VM, VM),
        scratch_shapes=[pltpu.VMEM((6, GROUPS, 768), F32), pltpu.VMEM((3, GROUPS, 128), F32),
                        pltpu.VMEM((6, GROUPS, 128), F32), pltpu.VMEM((2304, 768), BF16),
                        pltpu.VMEM((256, 2304), BF16), pltpu.VMEM((6, 6 * GROUPS, 128), F32)],
        compiler_params=pltpu.CompilerParams(vmem_limit_bytes=60 << 20),
        name="gbst_bwd",
    )(length, invc, brow, emb, ck, sc, dstart, conv, csum)


def byte_planes(byte_values, length):
    positions = byte_values.shape[0]
    real = jnp.where(jnp.arange(positions) < length, byte_values, -1)
    ext = jnp.pad(real, (1, PERIOD * (GROUPS + 2) - positions - 1), constant_values=-1)
    cols = ext.reshape(GROUPS + 2, PERIOD)
    wide = jnp.concatenate([cols[:GROUPS], cols[1:GROUPS + 1, :4]], axis=1)
    rows = wide.T
    brow = jnp.stack([jnp.pad(rows[j:j + PERIOD].reshape(-1), (0, 2304 - PERIOD * GROUPS), constant_values=-1)
                      for j in range(4)])
    return wide, brow

TOK = 1024
BLK = 256
NEG = -1e30


def rms_parts(x):
    return lax.rsqrt(jnp.mean(x * x, axis=1, keepdims=True) + EPS)


def head_lanes(h2, rows, dtype=BF16):
    lane = lax.broadcasted_iota(jnp.int32, (rows, 128), 1)
    return jnp.where(lane // 64 == h2, 1.0, 0.0).astype(dtype)


def split3(x):
    hi = x.astype(BF16).astype(F32)
    mid = (x - hi).astype(BF16).astype(F32)
    return hi, mid, x - hi - mid


def att_fwd_body(tick, len_ref, start_ref, gain, wq_ref, wk_ref, wv_ref, wo_ref,
                 qs_ref, k_ref, v_ref, ctx_ref, qx_ref, normed_ref, middle_ref,
                 kx, vext, kext, qxf):
    length = len_ref[0, 0]
    g = gain
    tick("project", 0)

    def project(r, _):
        rs = pl.ds(pl.multiple_of(r * BLK, BLK), BLK)
        x = start_ref[rs, :]
        n = (x * rms_parts(x) * g).astype(BF16)
        normed_ref[rs, :] = n
        qs_ref[rs, :] = (dot(n, wq_ref[...]).astype(BF16).astype(F32) * 0.125).astype(BF16)
        k_ref[rs, :] = dot(n, wk_ref[...]).astype(BF16)
        v_ref[rs, :] = dot(n, wv_ref[...]).astype(BF16)
        return 0

    lax.fori_loop(0, TOK // BLK, project, 0)
    lane = lax.broadcasted_iota(jnp.int32, (TOK, 128), 1)
    row = lax.broadcasted_iota(jnp.int32, (TOK, 128), 0)
    keep = 2 * row < length
    kx[...] = jnp.where((lane == 0) & ~keep, NEG, 0.0).astype(BF16)
    ones = jnp.where(keep, 1.0, 0.0).astype(BF16)
    for h2 in range(2):
        vext[h2, :, pl.ds(128, 128)] = ones
        kext[h2, :, pl.ds(128, 128)] = kx[...]
    qxf[...] = jnp.where(lane == 0, 1.0, 0.0).astype(F32)
    lane_b = lax.broadcasted_iota(jnp.int32, (BLK, 128), 1)
    first = jnp.where(lane_b == 0, 1.0, 0.0).astype(BF16)

    def pair(p, _):
        ls = pl.ds(pl.multiple_of(p * 128, 128), 128)
        for h2 in range(2):
            hm = head_lanes(h2, TOK)
            vext[h2, :, pl.ds(0, 128)] = v_ref[:, ls] * hm
            kext[h2, :, pl.ds(0, 128)] = k_ref[:, ls] * hm

        def qblock(r, _):
            tick("att", 4 * p + r)
            rs = pl.ds(pl.multiple_of(r * BLK, BLK), BLK)
            q = jnp.concatenate([qs_ref[rs, ls], first], axis=1)
            out = jnp.zeros((BLK, 128), F32)
            upd = qxf[rs, :]
            for h2 in range(2):
                s = dot(q, kext[h2], ((1,), (1,)))
                m = jnp.max(s, axis=1, keepdims=True)
                e = jnp.exp(s - m).astype(BF16)
                c = dot(e, vext[h2])
                total = c[:, 128:]
                out = out + c[:, :128] * (1.0 / total)
                hi, mid, lo = split3(-(m + jnp.log(total)))
                base = 1 + 3 * (2 * p + h2)
                upd = jnp.where(lane_b == base, hi, jnp.where(lane_b == base + 1, mid,
                                jnp.where(lane_b == base + 2, lo, upd)))
            qxf[rs, :] = upd
            ctx_ref[rs, ls] = out.astype(BF16)
            return 0

        lax.fori_loop(0, TOK // BLK, qblock, 0)
        return 0

    lax.fori_loop(0, HEADS // 2, pair, 0)
    qx_ref[...] = qxf[...].astype(BF16)

    tick("outproj", 0)

    def outproj(r, _):
        rs = pl.ds(pl.multiple_of(r * BLK, BLK), BLK)
        middle_ref[rs, :] = start_ref[rs, :] + dot(ctx_ref[rs, :], wo_ref[...])
        return 0

    lax.fori_loop(0, TOK // BLK, outproj, 0)


def att_bwd_body(len_ref, dmid_ref, start_ref, gain_ref, qs_ref, k_ref, v_ref, ctx_ref, qx_ref, normed_ref,
                 wq_ref, wk_ref, wv_ref, wo_ref,
                 gq_ref, gk_ref, gv_ref, go_ref, dstart_ref, ggain_ref,
                 dctx, dx, dq, dk, dv, dqt, qcat, ocat, low):
    length = len_ref[0, 0]
    low[...] = dmid_ref[...].astype(BF16)
    lane_s = lax.broadcasted_iota(jnp.int32, (768, 128), 1)
    row_s = lax.broadcasted_iota(jnp.int32, (768, 128), 0)
    sel = jnp.where(lane_s // 3 == row_s // 64, 1.0, 0.0).astype(BF16)
    lane_b = lax.broadcasted_iota(jnp.int32, (BLK, 128), 1)

    def head(r, _):
        rs = pl.ds(pl.multiple_of(r * BLK, BLK), BLK)
        d = dot(low[rs, :], wo_ref[...], ((1,), (1,))).astype(BF16)
        dctx[rs, :] = d
        prod = d.astype(F32) * ctx_ref[rs, :].astype(F32)
        hi = prod.astype(BF16)
        delta = dot(hi, sel) + dot((prod - hi.astype(F32)).astype(BF16), sel)
        a, b, c = split3(-delta)
        dx[rs, :] = jnp.where(lane_b % 3 == 0, a, jnp.where(lane_b % 3 == 1, b, c)).astype(BF16)
        return 0

    lax.fori_loop(0, TOK // BLK, head, 0)

    def gout(c, _):
        cs = pl.ds(pl.multiple_of(c * BLK, BLK), BLK)
        go_ref[cs, :] = dot(ctx_ref[:, cs], low[...], ((0,), (0,))).astype(BF16)
        return 0

    lax.fori_loop(0, 3, gout, 0)
    qcat[:, pl.ds(128, 128)] = qx_ref[...]
    ocat[:, pl.ds(128, 128)] = dx[...]
    row_b = lax.broadcasted_iota(jnp.int32, (BLK, 128), 0)

    def pair(p, _):
        ls = pl.ds(pl.multiple_of(p * 128, 128), 128)
        qcat[:, pl.ds(0, 128)] = qs_ref[:, ls]
        ocat[:, pl.ds(0, 128)] = dctx[:, ls]
        dqt[...] = jnp.zeros_like(dqt)

        def kblock(r, _):
            rs = pl.ds(pl.multiple_of(r * BLK, BLK), BLK)
            bias = jnp.where((lane_b == 0) & (2 * (row_b + r * BLK) >= length), NEG, 0.0)
            dvb = jnp.zeros((BLK, 128), F32)
            dkb = jnp.zeros((BLK, 128), F32)
            dqb = dqt[...]
            for h2 in range(2):
                hm = head_lanes(h2, BLK)
                hd = 3 * (2 * p + h2)
                km = k_ref[rs, ls] * hm
                vm = v_ref[rs, ls] * hm
                kxl = jnp.where((lane_b > hd) & (lane_b <= hd + 3), 1.0, bias).astype(BF16)
                vxl = jnp.where((lane_b >= hd) & (lane_b < hd + 3), 1.0, 0.0).astype(BF16)
                st = dot(jnp.concatenate([km, kxl], axis=1), qcat[...], ((1,), (1,)))
                dp = dot(jnp.concatenate([vm, vxl], axis=1), ocat[...], ((1,), (1,)))
                prob = jnp.exp(st)
                dsc = (prob * dp).astype(BF16)
                dvb = dvb + dot(prob.astype(BF16), ocat[:, pl.ds(0, 128)]) * hm.astype(F32)
                dkb = dkb + dot(dsc, qcat[:, pl.ds(0, 128)]) * hm.astype(F32)
                dqb = dqb + dot(km, dsc, ((0,), (0,)))
            dv[rs, ls] = dvb.astype(BF16)
            dk[rs, ls] = dkb.astype(BF16)
            dqt[...] = dqb
            return 0

        lax.fori_loop(0, TOK // BLK, kblock, 0)
        dq[:, ls] = (dqt[...].T * 0.125).astype(BF16)
        return 0

    lax.fori_loop(0, HEADS // 2, pair, 0)

    def wgrad(c, _):
        cs = pl.ds(pl.multiple_of(c * BLK, BLK), BLK)
        n = normed_ref[:, cs]
        gq_ref[cs, :] = dot(n, dq[...], ((0,), (0,))).astype(BF16)
        gk_ref[cs, :] = dot(n, dk[...], ((0,), (0,))).astype(BF16)
        gv_ref[cs, :] = dot(n, dv[...], ((0,), (0,))).astype(BF16)
        return 0

    lax.fori_loop(0, 3, wgrad, 0)
    ggain_ref[...] = jnp.zeros_like(ggain_ref)
    g = gain_ref[...].astype(F32)

    def tail(r, _):
        rs = pl.ds(pl.multiple_of(r * BLK, BLK), BLK)
        d = (dot(dq[rs, :], wq_ref[...], ((1,), (1,))) + dot(dk[rs, :], wk_ref[...], ((1,), (1,)))
             + dot(dv[rs, :], wv_ref[...], ((1,), (1,))))
        dxv, gg = rms_back(start_ref[rs, :], g, d)
        dstart_ref[rs, :] = dmid_ref[rs, :] + dxv
        ggain_ref[...] += gg
        return 0

    lax.fori_loop(0, TOK // BLK, tail, 0)


def rms_back(x, g, d):
    s = rms_parts(x)
    xn = x * s
    dxn = d * xn
    gg = jnp.sum(dxn.reshape(x.shape[0] // 8, 8, x.shape[1]), axis=0)
    return s * (d * g - xn * jnp.mean(dxn * g, axis=1, keepdims=True)), gg


def att_bwd(length, dmid, start, gain, qs, k, v, ctx, qx, normed, wq, wk, wv, wo):
    w = jax.ShapeDtypeStruct((768, 768), BF16)
    act = pltpu.VMEM((TOK, 768), BF16)
    return pl.pallas_call(
        att_bwd_body,
        out_shape=(w, w, w, w, jax.ShapeDtypeStruct((TOK, 768), F32), jax.ShapeDtypeStruct((8, 768), F32)),
        in_specs=[SM] + [VM] * 13,
        out_specs=(VM,) * 6,
        scratch_shapes=[act, pltpu.VMEM((TOK, 128), BF16), act, act, act, pltpu.VMEM((128, TOK), F32),
                        pltpu.VMEM((TOK, 256), BF16), pltpu.VMEM((TOK, 256), BF16), act],
        compiler_params=pltpu.CompilerParams(vmem_limit_bytes=60 << 20),
        name="att_bwd",
    )(length, dmid, start, gain, qs, k, v, ctx, qx, normed, wq, wk, wv, wo)


C0 = 0.7978845608028654
C1 = 0.044715


def ffn_body(middle_ref, gain_ref, cot_ref, wg_ref, wu_ref, wd_ref,
             out_ref, gg_ref, gu_ref, gd_ref, dmid_ref, ggain_ref,
             n2, n2t, top, dn2, hid, dg, du):
    f = pl.program_id(0)
    g2 = gain_ref[...].astype(F32)

    @pl.when(f == 0)
    def _():
        def prep(r, _):
            rs = pl.ds(pl.multiple_of(r * BLK, BLK), BLK)
            x = middle_ref[rs, :]
            n = x * rms_parts(x) * g2
            n2[rs, :] = n.astype(BF16)
            n2t[:, rs] = n.T.astype(BF16)
            top[rs, :] = cot_ref[rs, :].astype(BF16)
            out_ref[rs, :] = x
            dn2[rs, :] = jnp.zeros((BLK, 768), F32)
            return 0
        lax.fori_loop(0, TOK // BLK, prep, 0)

    def rows(r, _):
        rs = pl.ds(pl.multiple_of(r * BLK, BLK), BLK)
        n = n2[rs, :]
        v = dot(n, wg_ref[...])
        u = dot(n, wu_ref[...])
        dh = dot(top[rs, :], wd_ref[...], ((1,), (1,)))
        v2 = v * v
        t = jnp.tanh(v * (C0 + (C0 * C1) * v2))
        hp = 0.5 + 0.5 * t
        gelu = v * hp
        slope = hp + (0.5 * v) * (1.0 - t * t) * (C0 + (3.0 * C0 * C1) * v2)
        h = (gelu * u).astype(BF16)
        hid[rs, :] = h
        a = (dh * u * slope).astype(BF16)
        b = (dh * gelu).astype(BF16)
        dg[rs, :] = a
        du[rs, :] = b
        out_ref[rs, :] += dot(h, wd_ref[...])
        dn2[rs, :] += dot(a, wg_ref[...], ((1,), (1,))) + dot(b, wu_ref[...], ((1,), (1,)))
        return 0

    lax.fori_loop(0, TOK // BLK, rows, 0)
    gg_ref[...] = dot(n2t[...], dg[...]).astype(BF16)
    gu_ref[...] = dot(n2t[...], du[...]).astype(BF16)
    gd_ref[...] = dot(hid[...], top[...], ((0,), (0,))).astype(BF16)

    @pl.when(f == pl.num_programs(0) - 1)
    def _():
        ggain_ref[...] = jnp.zeros_like(ggain_ref)

        def fin(r, _):
            rs = pl.ds(pl.multiple_of(r * BLK, BLK), BLK)
            dxv, gg = rms_back(middle_ref[rs, :], g2, dn2[rs, :])
            dmid_ref[rs, :] = cot_ref[rs, :] + dxv
            ggain_ref[...] += gg
            return 0
        lax.fori_loop(0, TOK // BLK, fin, 0)


def ffn(middle, gain, cot, wg, wu, wd):
    ff = wg.shape[1]
    whole = lambda *s: pl.BlockSpec(s, lambda f: (0, 0), pipeline_mode=pl.Buffered(1))
    act = jax.ShapeDtypeStruct((TOK, 768), F32)
    wide = pl.BlockSpec((768, BLK), lambda f: (0, f))
    tall = pl.BlockSpec((BLK, 768), lambda f: (f, 0))
    return pl.pallas_call(
        ffn_body,
        grid=(ff // BLK,),
        out_shape=(act, jax.ShapeDtypeStruct((768, ff), BF16), jax.ShapeDtypeStruct((768, ff), BF16),
                   jax.ShapeDtypeStruct((ff, 768), BF16), act, jax.ShapeDtypeStruct((8, 768), F32)),
        in_specs=[whole(TOK, 768), whole(1, 768), whole(TOK, 768), wide, wide, tall],
        out_specs=(whole(TOK, 768), wide, wide, tall, whole(TOK, 768), whole(8, 768)),
        scratch_shapes=[pltpu.VMEM((TOK, 768), BF16), pltpu.VMEM((768, TOK), BF16), pltpu.VMEM((TOK, 768), BF16),
                        pltpu.VMEM((TOK, 768), F32)] + [pltpu.VMEM((TOK, BLK), BF16)] * 3,
        compiler_params=pltpu.CompilerParams(vmem_limit_bytes=60 << 20),
        name="ffn",
    )(middle, gain, cot, wg, wu, wd)

MESH = pl.DeviceIdType.MESH
HB = pl.BlockSpec(memory_space=pl.ANY)


def bit_of(v, b):
    return (v // (1 << b)) % 2


def flip(v, b):
    return v + (1 - 2 * bit_of(v, b)) * (1 << b)


def with_bits(v, bits, e):
    for i, b in enumerate(bits):
        v = v + (((e >> i) & 1) - bit_of(v, b)) * (1 << b)
    return v


def here():
    return lax.axis_index("wide"), lax.axis_index("narrow")


def greet(wide, direct):
    w, n = here()
    sem = pltpu.get_barrier_semaphore()
    peers = [(lax.rem(w + d, wide), n) for d in range(1, wide)] if direct else [
        (flip(w, b), n) for b in range(wide.bit_length() - 1)]
    peers = peers + [(w, flip(n, 0)), (w, flip(n, 1))]
    for p in peers:
        pl.semaphore_signal(sem, inc=1, device_id=p, device_id_type=MESH)
    pl.semaphore_wait(sem, len(peers))


class Ticker:
    def __init__(self):
        self.todo = {}

    def add(self, name, index, fn):
        self.todo.setdefault((name, index), []).append(fn)

    def __call__(self, name, index):
        for (loop, at), fns in self.todo.items():
            if loop == name:
                if isinstance(index, int):
                    if at == index:
                        for fn in fns:
                            fn()
                else:
                    @pl.when(index == at)
                    def _(fns=fns):
                        for fn in fns:
                            fn()


def wide_order(order, wide):
    bits = wide.bit_length() - 1
    return order if bits == len(order) else tuple(range(bits - 1, -1, -1))


class Gather:
    def __init__(self, index, shard, out, region, order, split, sems):
        self.a, self.shard, self.out = index, shard, out
        self.row, self.nrow, self.col, self.ncol = region
        self.wide = out.shape[0]
        self.order = wide_order(order, self.wide)
        self.split = None
        if split:
            if self.ncol % 512 == 0:
                self.split = "col"
            elif self.nrow % 16 == 0:
                self.split = "row"
        self.send, self.recv, self.local = sems
        self.stages = len(self.order) + (2 if self.split else 1)

    def part(self, ref, quarter=True):
        _, n = here()
        half = self.ncol // 2
        col, ncol = self.col + bit_of(n, 0) * half, half
        row, nrow = self.row, self.nrow
        if self.split == "col" and quarter:
            ncol = half // 2
            col = col + bit_of(n, 1) * ncol
        rs = pl.ds(row, nrow)
        if self.split == "row" and quarter:
            nrow = nrow // 2
            rs = pl.ds(pl.multiple_of(row + bit_of(n, 1) * nrow, 8), nrow)
        lead = (slice(None),) * (len(ref.shape) - 2)
        return ref.at[lead + (rs, pl.ds(pl.multiple_of(col, 128), ncol))]

    def copy(self, src, dst, slot, device):
        return pltpu.make_async_remote_copy(src, dst, self.send.at[self.a, slot], self.recv.at[self.a, slot],
                                            device_id=device, device_id_type=MESH)

    def copies(self, i):
        w, n = here()
        if i < len(self.order):
            dev = (flip(w, self.order[i]), n)
            out = []
            for e in range(1 << i):
                blk = with_bits(w, self.order[:i], e)
                dst = self.part(self.out.at[blk])
                src = self.part(self.shard) if i == 0 else dst
                out.append(self.copy(src, dst, (1 << i) - 1 + e, dev))
            return out
        if self.split and i == len(self.order):
            ref = self.part(self.out)
            return [self.copy(ref, ref, self.wide - 1, (w, flip(n, 1)))]
        ref = self.part(self.out, quarter=False)
        return [self.copy(ref, ref, self.wide, (w, flip(n, 0)))]

    def own(self):
        w, _ = here()
        return pltpu.make_async_copy(self.part(self.shard), self.part(self.out.at[w]), self.local.at[self.a])

    def start(self, i):
        if i == 0:
            self.own().start()
        else:
            self.finish(i - 1)
            if i == 1:
                self.own().wait()
        for c in self.copies(i):
            c.start()

    def finish(self, i):
        for c in self.copies(i):
            c.wait_recv()

    def drain(self):
        for i in range(self.stages):
            for c in self.copies(i):
                c.wait_send()


class Total:
    def __init__(self, acc, slots, send, recv, wide, narrow):
        self.acc, self.slots, self.send, self.recv = acc, slots, send, recv
        self.bits = [("w", b) for b in range(wide.bit_length() - 1)] + [("n", b) for b in range(narrow.bit_length() - 1)]
        self.stages = len(self.bits)

    def copy(self, i):
        w, n = here()
        axis, b = self.bits[i]
        dev = (flip(w, b), n) if axis == "w" else (w, flip(n, b))
        return pltpu.make_async_remote_copy(self.acc.at[i], self.slots.at[i], self.send.at[i], self.recv.at[i],
                                            device_id=dev, device_id_type=MESH)

    def start(self, i):
        if i > 0:
            self.finish(i - 1)
        self.copy(i).start()

    def finish(self, i):
        self.copy(i).wait()
        self.acc[i + 1] = self.acc[i] + self.slots[i]


GATHERS = (
    (0, 0, (2, 1, 0), True), (1, 0, (2, 1, 0), True), (2, 0, (1, 2, 0), False), (3, 0, (0, 2, 1), False),
    (4, 0, (0, 1, 2), True), (4, 1, (1, 2, 0), False), (5, 0, (2, 1, 0), True), (5, 1, (2, 1, 0), False),
    (6, 0, (2, 0, 1), False), (6, 1, (2, 0, 1), True),
)
GATHER_PLAN = {
    ("begin", 0): [(0, 0), (1, 0), (2, 0), (9, 0)],
    ("onehot", 0): [(0, 1), (4, 0), (1, 1), (2, 1), (6, 0)],
    ("table", 0): [(0, 2), (8, 0), (7, 0)],
    ("plane", 2): [(9, 1), (4, 1), (1, 2)],
    ("plane", 5): [(5, 0), (3, 0)],
    ("plane", 8): [(0, 3), (2, 2)],
    ("rows", 0): [(9, 2), (1, 3)],
    ("rows", 4): [(0, 4), (6, 1)],
    ("rows", 8): [(4, 2), (2, 3), (1, 4)],
    ("att", 0): [(9, 3), (8, 1), (7, 1), (5, 1), (3, 1), (6, 2)],
    ("att", 2): [(4, 3)],
    ("att", 4): [(9, 4), (8, 2)],
    ("att", 6): [(6, 3), (7, 2)],
    ("att", 9): [(4, 4), (5, 2)],
    ("att", 11): [(7, 3), (3, 2)],
    ("att", 14): [(8, 3), (6, 4)],
    ("att", 17): [(5, 3), (3, 3)],
}


def chunk_region(weight, chunk, rows, cols):
    if weight < 4:
        return (0, rows, 0, cols)
    if weight < 6:
        return (0, rows, chunk * (cols // 2), cols // 2)
    return (chunk * (rows // 2), rows // 2, 0, cols)


def front_body(wide, narrow, len_ref, bcol_ref, emb_ref, small_ref,
               sq, sk, sv, so, sg, su, sd,
               oq, ok, ov, oo, og, ou, od,
               start_ref, conv_ref, csum_ref, tot_ref, smallall_ref, emball_ref,
               qs_ref, k_ref, v_ref, ctx_ref, qx_ref, normed_ref, middle_ref,
               table, onehot, planes, coef, tiles, ent, kx, vext, kext, qxf, vq, vk, vv, vo,
               embs, smalls, tacc, tslots,
               gsend, grecv, glocal, psend, precv, tsend, trecv, wsem):
    w, n = here()
    embs[w] = emb_ref[...]
    smalls[w] = small_ref[...]
    greet(wide, True)
    shards, outs = (sq, sk, sv, so, sg, su, sd), (oq, ok, ov, oo, og, ou, od)
    gathers = [Gather(i, shards[a], outs[a], chunk_region(a, c, *shards[a].shape), order, split, (gsend, grecv, glocal))
               for i, (a, c, order, split) in enumerate(GATHERS)]
    tick = Ticker()
    started = [0] * len(gathers)

    half = emb_ref.shape[1] // 2
    hcols = pl.ds(pl.multiple_of(bit_of(n, 0) * half, 128), half)
    small_copies, emb_copies = [], []
    for d in range(1, wide):
        peer = (lax.rem(w + d, wide), n)
        emb_copies.append(pltpu.make_async_remote_copy(
            emb_ref.at[:, hcols], embs.at[w, :, hcols], psend.at[0, d], precv.at[0, d], device_id=peer, device_id_type=MESH))
        small_copies.append(pltpu.make_async_remote_copy(
            small_ref, smalls.at[w], psend.at[1, d], precv.at[1, d], device_id=peer, device_id_type=MESH))
    for c in emb_copies + small_copies:
        c.start()
    swap = pltpu.make_async_remote_copy(embs.at[:, :, hcols], embs.at[:, :, hcols], psend.at[0, 0], precv.at[0, 0],
                                        device_id=(w, flip(n, 0)), device_id_type=MESH)

    def params():
        for c in emb_copies:
            c.wait_recv()
        swap.start()
        for c in small_copies:
            c.wait_recv()
        per = 768 // wide
        l = lax.broadcasted_iota(jnp.int32, (128, 768), 0)
        c = lax.broadcasted_iota(jnp.int32, (128, 768), 1)
        small = sum(dot(smalls[i].astype(BF16), jnp.where((c == per * i + l) & (l < per), 1.0, 0.0).astype(BF16))
                    for i in range(wide))
        smallall_ref[...] = small
        swap.wait()
        emb = embs[...].astype(F32).reshape(256, 768)
        emball_ref[...] = emb.astype(BF16)
        return emb, small

    for (loop, at), stages in GATHER_PLAN.items():
        for g, s in stages:
            if s < gathers[g].stages:
                tick.add(loop, at, functools.partial(gathers[g].start, s))
                started[g] = s + 1
    weights = list(zip((0, 1, 2), outs[:3], (vq, vk, vv)))

    def load(ws, sem0):
        copies = []
        for j, (_, src, dst) in enumerate(ws):
            r = src.shape[1]
            for i in range(wide):
                copies.append(pltpu.make_async_copy(src.at[i], dst.at[pl.ds(r * i, r)], wsem.at[sem0 + j, i]))
        return copies

    def ready(ids):
        for g in ids:
            for s in range(started[g], gathers[g].stages):
                gathers[g].start(s)
            gathers[g].finish(gathers[g].stages - 1)

    def qkv_ready():
        ready((0, 1, 2))
        cs = load(weights, 0)
        for c in cs:
            c.start()
        for c in cs:
            c.wait()

    tick.add("project", 0, qkv_ready)
    total = Total(tacc, tslots, tsend, trecv, wide, narrow)

    def total_begin():
        lane = lax.broadcasted_iota(jnp.int32, (8, 128), 1)
        tacc[0] = jnp.where(lane == 0, len_ref[0, 0].astype(F32), jnp.where(lane == 1, ent[...], 0.0))
        total.start(0)

    tick.add("att", 1, total_begin)
    for i in range(1, total.stages):
        tick.add("att", 1 + 2 * i, functools.partial(total.start, i))

    def out_ready():
        total.finish(total.stages - 1)
        tot_ref[...] = tacc[total.stages]
        ready((3,))
        cs = load([(3, outs[3], vo)], 3)
        for c in cs:
            c.start()
        for c in cs:
            c.wait()

    tick.add("outproj", 0, out_ready)
    tick("begin", 0)
    gbst_fwd_body(tick, params, len_ref, bcol_ref, start_ref, conv_ref, csum_ref, ent, table, onehot, planes, coef, tiles)
    att_fwd_body(tick, len_ref, start_ref, smallall_ref[pl.ds(5, 1), :], vq, vk, vv, vo,
                 qs_ref, k_ref, v_ref, ctx_ref, qx_ref, normed_ref, middle_ref, kx, vext, kext, qxf)
    ready(range(4, len(gathers)))
    for c in emb_copies + small_copies:
        c.wait_send()
    for g in gathers:
        g.drain()


def front(wide, narrow, length, bcol, emb, small, shards):
    b = jax.ShapeDtypeStruct((TOK, 768), BF16)
    f = jax.ShapeDtypeStruct((TOK, 768), F32)
    gathered = tuple(jax.ShapeDtypeStruct((wide,) + s.shape, s.dtype) for s in shards)
    sq = pltpu.VMEM((768, 768), BF16)
    ng = len(GATHERS)
    dma = pltpu.SemaphoreType.DMA
    stages = (wide * narrow).bit_length() - 1
    return pl.pallas_call(
        functools.partial(front_body, wide, narrow),
        out_shape=gathered + (
            f, jax.ShapeDtypeStruct((PERIOD, GROUPS, 768), BF16), jax.ShapeDtypeStruct((GROUPS, 128), F32),
            jax.ShapeDtypeStruct((8, 128), F32), jax.ShapeDtypeStruct((8, 768), F32), jax.ShapeDtypeStruct((256, 768), BF16),
            b, b, b, b, jax.ShapeDtypeStruct((TOK, 128), BF16), b, f),
        in_specs=[SM, VM, VM, VM] + [HB] * 7,
        out_specs=(HB,) * 7 + (VM,) * 13,
        scratch_shapes=[
            pltpu.VMEM((1024, 768), BF16), pltpu.VMEM((GROUPS, 256 * 15), BF16), pltpu.VMEM((PERIOD, GROUPS, 768), F32),
            pltpu.VMEM((4, GROUPS, 128), F32), pltpu.VMEM((6, 6 * GROUPS, 128), F32), pltpu.VMEM((8, 128), F32),
            pltpu.VMEM((TOK, 128), BF16), pltpu.VMEM((2, TOK, 256), BF16), pltpu.VMEM((2, TOK, 256), BF16),
            pltpu.VMEM((TOK, 128), F32), sq, sq, sq, sq,
            pltpu.VMEM((wide,) + emb.shape, BF16), pltpu.VMEM((wide, 8, 128), F32),
            pltpu.VMEM((stages + 1, 8, 128), F32), pltpu.VMEM((stages, 8, 128), F32),
            dma((ng, wide + 1)), dma((ng, wide + 1)), dma((ng,)), dma((2, wide)), dma((2, wide)), dma((stages,)), dma((stages,)),
            dma((4, wide))],
        compiler_params=pltpu.CompilerParams(vmem_limit_bytes=60 << 20, collective_id=0, has_side_effects=True),
        name="front",
    )(length, bcol, emb, small, *shards)


def body(
    wide, narrow,
    byte_values, row_lengths, embedding, conv_kernel, score_vector, attn_gain, query_weight, key_weight,
    value_weight, output_weight, ffn_gain, gate_weight, up_weight, down_weight, cotangent,
):
    length = row_lengths.reshape(1, 1)
    bcol, brow = byte_planes(byte_values[0], row_lengths[0])
    small = jnp.concatenate([conv_kernel, score_vector[None], attn_gain[None], ffn_gain[None]], axis=0).astype(F32)
    small = jnp.pad(small, ((0, 8 - small.shape[0]), (0, 128 - small.shape[1])))
    shards = (query_weight, key_weight, value_weight, output_weight, gate_weight, up_weight, down_weight)
    got = front(wide, narrow, length, bcol, embedding, small, shards)
    wq, wk, wv, wo, wg, wu, wd = [x.reshape(-1, x.shape[-1]) for x in got[:7]]
    start, conv, csum, tot, smallall, emb, qs, k, v, ctx, qx, normed, middle = got[7:]
    count, entropy_total = tot[0, 0], tot[0, 1]
    entropy = entropy_total / count
    ck, sc, g1, g2 = smallall[:4], smallall[4:5], smallall[5:6], smallall[6:7]
    out, gg, gu, gd, dmid, gg2 = ffn(middle, g2, cotangent[0], wg, wu, wd)
    gq, gk, gv, go, dstart, gg1 = att_bwd(length, dmid, start, g1, qs, k, v, ctx, qx, normed, wq, wk, wv, wo)
    ge, gc, gs = gbst_bwd(length, (ENT_WEIGHT / count).reshape(1, 1), brow, emb, ck, sc, dstart, conv, csum)

    def scatter(x, axis=0):
        part = lax.psum_scatter(x.astype(BF16), "wide", scatter_dimension=axis, tiled=True)
        return lax.psum(part, "narrow").astype(F32)

    return (out[None], entropy, scatter(ge), scatter(gc[:4], 1), scatter(gs.sum(0)), scatter(gg1.sum(0)),
            scatter(gq), scatter(gk), scatter(gv), scatter(go), scatter(gg2.sum(0)),
            scatter(gg), scatter(gu), scatter(gd))


def solution(mesh):
    both = ("wide", "narrow")
    row, flat = P("wide", None), P("wide")
    return jax.shard_map(
        functools.partial(body, mesh.shape["wide"], mesh.shape["narrow"]),
        mesh=mesh,
        in_specs=(P(both, None), P(both), row, P(None, "wide"), flat, flat, row, row, row, row, flat,
                  row, row, row, P(both, None, None)),
        out_specs=(P(both, None, None), P(), row, P(None, "wide"), flat, flat, row, row, row, row, flat,
                   row, row, row),
        check_vma=False,
    )
```

```python
import functools
import jax
import jax.numpy as jnp
from jax import lax
from jax.experimental import pallas as pl
from jax.experimental.pallas import tpu as pltpu
from jax.sharding import PartitionSpec as P

F32 = jnp.float32
BF16 = jnp.bfloat16
EPS = 1e-06
HEADS = 12
ENT_WEIGHT = 1.0
PERIOD = 12
GROUPS = 176
HIGH = lax.Precision.HIGHEST
VM = pl.BlockSpec(memory_space=pltpu.VMEM)
SM = pl.BlockSpec(memory_space=pltpu.SMEM)


def dot(a, b, dims=((1,), (0,)), precision=None):
    return lax.dot_general(a, b, (dims, ((), ())), precision=precision, preferred_element_type=F32)


def same_block(size):
    r = lax.broadcasted_iota(jnp.int32, (128, 128), 0)
    c = lax.broadcasted_iota(jnp.int32, (128, 128), 1)
    return jnp.where((r // size == c // size) & (r < PERIOD) & (c < PERIOD), 1.0, 0.0).astype(F32)


def block_sum(x, size):
    return dot(x, same_block(size), precision=HIGH)


def lane_scalars(csum, length):
    i = lax.broadcasted_iota(jnp.int32, (GROUPS, 128), 0)
    k = lax.broadcasted_iota(jnp.int32, (GROUPS, 128), 1)
    mask = jnp.where((PERIOD * i + k < length) & (k < PERIOD), 1.0, 0.0).astype(F32)
    tok = block_sum(jnp.where(k % 2 == 0, mask, 0.0), 2)
    inv = [jnp.ones_like(mask)] + [1.0 / jnp.maximum(block_sum(mask, b), 1.0) for b in (2, 3, 4)]
    scores = [csum] + [block_sum(csum, b) * inv[b - 1] for b in (2, 3, 4)]
    top = functools.reduce(jnp.maximum, scores)
    ex = [jnp.exp(s - top) for s in scores]
    total = ex[0] + ex[1] + ex[2] + ex[3]
    rec = 1.0 / total
    chance = [e * rec for e in ex]
    mean = sum(c * s for c, s in zip(chance, scores))
    ent = mask * (top + jnp.log(total) - mean)
    alpha = [c * v for c, v in zip(chance, inv)]
    return mask, tok, inv, scores, chance, mean, ent, alpha


def gbst_fwd_body(tick, params, len_ref, bcol_ref, start_ref, conv_ref, csum_ref, ent_ref,
                  table, onehot, planes, coef, tiles):
    length = len_ref[0, 0]
    vocab = lax.broadcasted_iota(jnp.int32, (GROUPS, 256), 1)
    for k in range(PERIOD + 3):
        onehot[:, pl.ds(256 * k, 256)] = jnp.where(bcol_ref[:, k:k + 1] == vocab, 1.0, 0.0).astype(BF16)
    csum_ref[...] = jnp.zeros_like(csum_ref)
    tick("onehot", 0)
    emb, small = params()
    for j in range(4):
        table[pl.ds(256 * j, 256), :] = (emb * small[j:j + 1]).astype(BF16)
    s = small[4:5]
    tick("table", 0)
    rows = lax.broadcasted_iota(jnp.int32, (GROUPS, 1), 0)
    lane = lax.broadcasted_iota(jnp.int32, (GROUPS, 128), 1)

    def plane(k, _):
        tick("plane", k)
        lhs = onehot[:, pl.ds(pl.multiple_of(256 * k, 256), 1024)]
        out = dot(lhs, table[...])
        out = jnp.where(PERIOD * rows + k < length, out, 0.0)
        planes[k] = out
        conv_ref[k] = out.astype(BF16)
        c = jnp.sum(out * s, axis=1, keepdims=True)
        csum_ref[...] = jnp.where(lane == k, c, csum_ref[...])
        return 0

    lax.fori_loop(0, PERIOD, plane, 0)
    mask, tok, inv, scores, chance, mean, ent, alpha = lane_scalars(csum_ref[...], length)
    ent_ref[...] = jnp.sum(jnp.sum(ent, axis=0, keepdims=True), axis=1, keepdims=True) + jnp.zeros((8, 128), F32)
    half = 0.5 * tok
    coef[0] = (alpha[0] + block_sum(alpha[1], 2)) * half
    coef[1] = alpha[2] * half
    coef[2] = block_sum(alpha[2], 2) * half
    coef[3] = block_sum(alpha[3], 2) * half

    def rowblock(ib, _):
        tick("rows", ib)
        r0 = pl.multiple_of(ib * 16, 16)
        rs = pl.ds(r0, 16)
        ce, c3, c3p, c4p = [coef[n, rs, :] for n in range(4)]
        for lt in range(6):
            ls = pl.ds(128 * lt, 128)
            p = [planes[k, rs, ls] for k in range(PERIOD)]
            pair = [p[2 * m] + p[2 * m + 1] for m in range(6)]
            quad = [pair[2 * y] + pair[2 * y + 1] for y in range(3)]
            tri = [p[3 * x] + p[3 * x + 1] + p[3 * x + 2] for x in range(4)]
            for m in range(6):
                a, b = 2 * m, 2 * m + 1
                out = ce[:, a:a + 1] * p[a] + ce[:, b:b + 1] * p[b] + c4p[:, a:a + 1] * quad[m // 2]
                if a // 3 == b // 3:
                    out = out + c3p[:, a:a + 1] * tri[a // 3]
                else:
                    out = out + c3[:, a:a + 1] * tri[a // 3] + c3[:, b:b + 1] * tri[b // 3]
                tiles[lt, pl.ds(6 * r0 + m, 16, stride=6), :] = out
        return 0

    lax.fori_loop(0, GROUPS // 16, rowblock, 0)
    for lt in range(6):
        start_ref[:, pl.ds(128 * lt, 128)] = tiles[lt, pl.ds(0, start_ref.shape[0]), :]


def gbst_bwd_body(tick, len_ref, invc_ref, brow_ref, emb_ref, ck_ref, sc_ref, dstart_ref, conv_ref, csum_ref,
                  gemb_ref, gconv_ref, gscore_ref, dm, dots, coef, dconv, onehot, tiles):
    for lt in range(6):
        tiles[lt, pl.ds(0, 1024), :] = dstart_ref[:, pl.ds(128 * lt, 128)]
        tiles[lt, pl.ds(1024, 6 * GROUPS - 1024), :] = jnp.zeros((6 * GROUPS - 1024, 128), F32)
    length = len_ref[0, 0]
    invc = invc_ref[0, 0]
    mask, tok, inv, scores, chance, mean, ent, alpha = lane_scalars(csum_ref[...], length)
    half = 0.5 * tok
    coef[0] = half
    lane16 = lax.broadcasted_iota(jnp.int32, (16, 128), 1)

    def first(ib, _):
        tick("first", ib)
        r0 = pl.multiple_of(ib * 16, 16)
        rs = pl.ds(r0, 16)
        h = coef[0, rs, :]
        acc = [jnp.zeros((16, 128), F32) for _ in range(26)]
        for lt in range(6):
            ls = pl.ds(128 * lt, 128)
            p = [conv_ref[k, rs, ls].astype(F32) for k in range(PERIOD)]
            quad = [(p[4 * y] + p[4 * y + 1]) + (p[4 * y + 2] + p[4 * y + 3]) for y in range(3)]
            tri = [p[3 * x] + p[3 * x + 1] + p[3 * x + 2] for x in range(4)]
            n = 0
            for m in range(6):
                d = tiles[lt, pl.ds(6 * r0 + m, 16, stride=6), :] * h[:, 2 * m:2 * m + 1]
                dm[m, rs, ls] = d
                for q in terms(m, p, quad, tri):
                    acc[n] = acc[n] + d * q
                    n += 1
        g1 = jnp.zeros((16, 128), F32)
        g3 = jnp.zeros((16, 128), F32)
        g4 = jnp.zeros((16, 128), F32)
        n = 0
        for m in range(6):
            a, b = 2 * m, 2 * m + 1
            v = [jnp.sum(acc[n + q], axis=1, keepdims=True) for q in range(len(TERMS[m]))]
            n += len(TERMS[m])
            g1 = jnp.where(lane16 == a, v[0], jnp.where(lane16 == b, v[1], g1))
            g4 = jnp.where((lane16 == a) | (lane16 == b), v[2], g4)
            g3 = jnp.where(lane16 == a, v[3], jnp.where(lane16 == b, v[-1], g3))
        dots[0, rs, :] = g1
        dots[1, rs, :] = g3
        dots[2, rs, :] = g4
        return 0

    lax.fori_loop(0, GROUPS // 16, first, 0)
    g1 = dots[0]
    dch = [g1, block_sum(g1, 2) * inv[1], dots[1] * inv[2], dots[2] * inv[3]]
    dmean = sum(c * d for c, d in zip(chance, dch))
    dsc = [c * (d - dmean) - invc * mask * c * (s - mean) for c, d, s in zip(chance, dch, scores)]
    w = dsc[0] + sum(block_sum(dsc[b - 1], b) * inv[b - 1] for b in (2, 3, 4))
    coef[0] = (alpha[0] + block_sum(alpha[1], 2)) * mask
    coef[1] = alpha[2]
    coef[2] = block_sum(alpha[2], 2)
    coef[3] = block_sum(alpha[3], 2)
    coef[4] = w * mask
    coef[5] = mask
    s = sc_ref[...].astype(F32)
    gscore_ref[...] = jnp.zeros_like(gscore_ref)
    dconv[pl.ds(PERIOD * GROUPS, 2304 - PERIOD * GROUPS), :] = jnp.zeros((2304 - PERIOD * GROUPS, 768), BF16)

    def second(ib, _):
        tick("second", ib)
        r0 = pl.multiple_of(ib * 16, 16)
        rs = pl.ds(r0, 16)
        ce, c3, c3p, c4p, cw, mk = [coef[n, rs, :] for n in range(6)]
        for lt in range(6):
            ls = pl.ds(128 * lt, 128)
            d = [dm[m, rs, ls] for m in range(6)]
            tri = [c3p[:, 0:1] * d[0] + c3[:, 2:3] * d[1], c3[:, 3:4] * d[1] + c3p[:, 4:5] * d[2],
                   c3p[:, 6:7] * d[3] + c3[:, 8:9] * d[4], c3[:, 9:10] * d[4] + c3p[:, 10:11] * d[5]]
            quad = [c4p[:, 4 * y:4 * y + 1] * d[2 * y] + c4p[:, 4 * y + 2:4 * y + 3] * d[2 * y + 1] for y in range(3)]
            st = s[:, 128 * lt:128 * lt + 128]
            gs = jnp.zeros((16, 128), F32)
            for k in range(PERIOD):
                wk = cw[:, k:k + 1]
                out = ce[:, k:k + 1] * d[k // 2] + mk[:, k:k + 1] * (tri[k // 3] + quad[k // 4]) + wk * st
                gs = gs + wk * conv_ref[k, rs, ls].astype(F32)
                dconv[pl.ds(pl.multiple_of(GROUPS * k + r0, 16), 16), ls] = out.astype(BF16)
            gscore_ref[:, ls] += gs[:8] + gs[8:]
        return 0

    lax.fori_loop(0, GROUPS // 16, second, 0)
    vocab = lax.broadcasted_iota(jnp.int32, (256, 2304), 0)
    emb = emb_ref[...].astype(F32)
    for j in range(4):
        tick("taps", j)
        onehot[...] = jnp.where(brow_ref[pl.ds(j, 1), :] == vocab, 1.0, 0.0).astype(BF16)
        g = dot(onehot[...], dconv[...])
        gconv_ref[pl.ds(j, 1), :] = jnp.sum(g * emb, axis=0, keepdims=True)
        part = g * ck_ref[pl.ds(j, 1), :].astype(F32)
        gemb_ref[...] = part if j == 0 else gemb_ref[...] + part


TERMS = {m: (1, 1, 4, 3) if (2 * m) // 3 == (2 * m + 1) // 3 else (1, 1, 4, 3, 3) for m in range(6)}


def terms(m, p, quad, tri):
    a, b = 2 * m, 2 * m + 1
    out = [p[a], p[b], quad[m // 2], tri[a // 3]]
    if a // 3 != b // 3:
        out.append(tri[b // 3])
    return out


def byte_planes(byte_values, length):
    positions = byte_values.shape[0]
    real = jnp.where(jnp.arange(positions) < length, byte_values, -1)
    ext = jnp.pad(real, (1, PERIOD * (GROUPS + 2) - positions - 1), constant_values=-1)
    cols = ext.reshape(GROUPS + 2, PERIOD)
    wide = jnp.concatenate([cols[:GROUPS], cols[1:GROUPS + 1, :4]], axis=1)
    rows = wide.T
    brow = jnp.stack([jnp.pad(rows[j:j + PERIOD].reshape(-1), (0, 2304 - PERIOD * GROUPS), constant_values=-1)
                      for j in range(4)])
    return wide, brow

TOK = 1024
BLK = 256
NEG = -1e30


def rms_parts(x):
    return lax.rsqrt(jnp.mean(x * x, axis=1, keepdims=True) + EPS)


def head_lanes(h2, rows, dtype=BF16):
    lane = lax.broadcasted_iota(jnp.int32, (rows, 128), 1)
    return jnp.where(lane // 64 == h2, 1.0, 0.0).astype(dtype)


def split3(x):
    hi = x.astype(BF16).astype(F32)
    mid = (x - hi).astype(BF16).astype(F32)
    return hi, mid, x - hi - mid


def att_fwd_body(tick, len_ref, start_ref, gain, wq_ref, wk_ref, wv_ref, wo_ref,
                 qs_ref, k_ref, v_ref, ctx_ref, qx_ref, normed_ref, middle_ref,
                 kx, vext, kext, qxf):
    length = len_ref[0, 0]
    g = gain
    tick("project", 0)

    def project(r, _):
        rs = pl.ds(pl.multiple_of(r * BLK, BLK), BLK)
        x = start_ref[rs, :]
        n = (x * rms_parts(x) * g).astype(BF16)
        normed_ref[rs, :] = n
        qs_ref[rs, :] = (dot(n, wq_ref[...]).astype(BF16).astype(F32) * 0.125).astype(BF16)
        k_ref[rs, :] = dot(n, wk_ref[...]).astype(BF16)
        v_ref[rs, :] = dot(n, wv_ref[...]).astype(BF16)
        return 0

    lax.fori_loop(0, TOK // BLK, project, 0)
    lane = lax.broadcasted_iota(jnp.int32, (TOK, 128), 1)
    row = lax.broadcasted_iota(jnp.int32, (TOK, 128), 0)
    keep = 2 * row < length
    kx[...] = jnp.where((lane == 0) & ~keep, NEG, 0.0).astype(BF16)
    ones = jnp.where(keep, 1.0, 0.0).astype(BF16)
    for h2 in range(2):
        vext[h2, :, pl.ds(128, 128)] = ones
        kext[h2, :, pl.ds(128, 128)] = kx[...]
    qxf[...] = jnp.where(lane == 0, 1.0, 0.0).astype(F32)
    lane_b = lax.broadcasted_iota(jnp.int32, (BLK, 128), 1)
    first = jnp.where(lane_b == 0, 1.0, 0.0).astype(BF16)

    def pair(p, _):
        ls = pl.ds(pl.multiple_of(p * 128, 128), 128)
        for h2 in range(2):
            hm = head_lanes(h2, TOK)
            vext[h2, :, pl.ds(0, 128)] = v_ref[:, ls] * hm
            kext[h2, :, pl.ds(0, 128)] = k_ref[:, ls] * hm

        def qblock(r, _):
            tick("att", 4 * p + r)
            rs = pl.ds(pl.multiple_of(r * BLK, BLK), BLK)
            q = jnp.concatenate([qs_ref[rs, ls], first], axis=1)
            out = jnp.zeros((BLK, 128), F32)
            upd = qxf[rs, :]
            for h2 in range(2):
                s = dot(q, kext[h2], ((1,), (1,)))
                m = jnp.max(s, axis=1, keepdims=True)
                e = jnp.exp(s - m).astype(BF16)
                c = dot(e, vext[h2])
                total = c[:, 128:]
                out = out + c[:, :128] * (1.0 / total)
                hi, mid, lo = split3(-(m + jnp.log(total)))
                base = 1 + 3 * (2 * p + h2)
                upd = jnp.where(lane_b == base, hi, jnp.where(lane_b == base + 1, mid,
                                jnp.where(lane_b == base + 2, lo, upd)))
            qxf[rs, :] = upd
            ctx_ref[rs, ls] = out.astype(BF16)
            return 0

        lax.fori_loop(0, TOK // BLK, qblock, 0)
        return 0

    lax.fori_loop(0, HEADS // 2, pair, 0)
    qx_ref[...] = qxf[...].astype(BF16)

    tick("outproj", 0)

    def outproj(r, _):
        rs = pl.ds(pl.multiple_of(r * BLK, BLK), BLK)
        middle_ref[rs, :] = start_ref[rs, :] + dot(ctx_ref[rs, :], wo_ref[...])
        return 0

    lax.fori_loop(0, TOK // BLK, outproj, 0)


def att_bwd_body(tick, go_ref, len_ref, dmid_ref, start_ref, gain_ref, qs_ref, k_ref, v_ref, ctx_ref, qx_ref, normed_ref,
                 wq_ref, wk_ref, wv_ref, wo_ref,
                 gq_ref, gk_ref, gv_ref, dstart_ref, ggain_ref,
                 dctx, dx, dq, dk, dv, dqt, qcat, ocat, low):
    length = len_ref[0, 0]
    low[...] = dmid_ref[...].astype(BF16)
    lane_s = lax.broadcasted_iota(jnp.int32, (768, 128), 1)
    row_s = lax.broadcasted_iota(jnp.int32, (768, 128), 0)
    sel = jnp.where(lane_s // 3 == row_s // 64, 1.0, 0.0).astype(BF16)
    lane_b = lax.broadcasted_iota(jnp.int32, (BLK, 128), 1)

    def head(r, _):
        tick("head", r)
        rs = pl.ds(pl.multiple_of(r * BLK, BLK), BLK)
        d = dot(low[rs, :], wo_ref[...], ((1,), (1,))).astype(BF16)
        dctx[rs, :] = d
        prod = d.astype(F32) * ctx_ref[rs, :].astype(F32)
        hi = prod.astype(BF16)
        delta = dot(hi, sel) + dot((prod - hi.astype(F32)).astype(BF16), sel)
        a, b, c = split3(-delta)
        dx[rs, :] = jnp.where(lane_b % 3 == 0, a, jnp.where(lane_b % 3 == 1, b, c)).astype(BF16)
        return 0

    lax.fori_loop(0, TOK // BLK, head, 0)

    nblk, per = go_ref.shape[:2]
    whole = dot(ctx_ref[...], low[...], ((0,), (0,))).astype(BF16)
    for c in range(nblk):
        go_ref[c] = whole[per * c:per * c + per]
    tick("gout", 0)
    qcat[:, pl.ds(128, 128)] = qx_ref[...]
    ocat[:, pl.ds(128, 128)] = dx[...]
    row_b = lax.broadcasted_iota(jnp.int32, (BLK, 128), 0)

    def pair(p, _):
        ls = pl.ds(pl.multiple_of(p * 128, 128), 128)
        qcat[:, pl.ds(0, 128)] = qs_ref[:, ls]
        ocat[:, pl.ds(0, 128)] = dctx[:, ls]
        dqt[...] = jnp.zeros_like(dqt)

        def kblock(r, _):
            tick("bwd", 4 * p + r)
            rs = pl.ds(pl.multiple_of(r * BLK, BLK), BLK)
            bias = jnp.where((lane_b == 0) & (2 * (row_b + r * BLK) >= length), NEG, 0.0)
            dvb = jnp.zeros((BLK, 128), F32)
            dkb = jnp.zeros((BLK, 128), F32)
            dqb = dqt[...]
            for h2 in range(2):
                hm = head_lanes(h2, BLK)
                hd = 3 * (2 * p + h2)
                km = k_ref[rs, ls] * hm
                vm = v_ref[rs, ls] * hm
                kxl = jnp.where((lane_b > hd) & (lane_b <= hd + 3), 1.0, bias).astype(BF16)
                vxl = jnp.where((lane_b >= hd) & (lane_b < hd + 3), 1.0, 0.0).astype(BF16)
                st = dot(jnp.concatenate([km, kxl], axis=1), qcat[...], ((1,), (1,)))
                dp = dot(jnp.concatenate([vm, vxl], axis=1), ocat[...], ((1,), (1,)))
                prob = jnp.exp(st)
                dsc = (prob * dp).astype(BF16)
                dvb = dvb + dot(prob.astype(BF16), ocat[:, pl.ds(0, 128)]) * hm.astype(F32)
                dkb = dkb + dot(dsc, qcat[:, pl.ds(0, 128)]) * hm.astype(F32)
                dqb = dqb + dot(km, dsc, ((0,), (0,)))
            dv[rs, ls] = dvb.astype(BF16)
            dk[rs, ls] = dkb.astype(BF16)
            dqt[...] = dqb
            return 0

        lax.fori_loop(0, TOK // BLK, kblock, 0)
        dq[:, ls] = (dqt[...].T * 0.125).astype(BF16)
        return 0

    lax.fori_loop(0, HEADS // 2, pair, 0)

    def wgrad(c, _):
        tick("wgrad", c)
        cs = pl.ds(pl.multiple_of(c * BLK, BLK), BLK)
        n = normed_ref[:, cs]
        gq_ref[cs, :] = dot(n, dq[...], ((0,), (0,))).astype(BF16)
        gk_ref[cs, :] = dot(n, dk[...], ((0,), (0,))).astype(BF16)
        gv_ref[cs, :] = dot(n, dv[...], ((0,), (0,))).astype(BF16)
        return 0

    lax.fori_loop(0, 3, wgrad, 0)
    ggain_ref[...] = jnp.zeros_like(ggain_ref)
    g = gain_ref[...].astype(F32)

    def tail(r, _):
        tick("last", r)
        rs = pl.ds(pl.multiple_of(r * BLK, BLK), BLK)
        d = (dot(dq[rs, :], wq_ref[...], ((1,), (1,))) + dot(dk[rs, :], wk_ref[...], ((1,), (1,)))
             + dot(dv[rs, :], wv_ref[...], ((1,), (1,))))
        dxv, gg = rms_back(start_ref[rs, :], g, d)
        dstart_ref[rs, :] = dmid_ref[rs, :] + dxv
        ggain_ref[...] += gg
        return 0

    lax.fori_loop(0, TOK // BLK, tail, 0)


def rms_back(x, g, d):
    s = rms_parts(x)
    xn = x * s
    dxn = d * xn
    gg = jnp.sum(dxn.reshape(x.shape[0] // 8, 8, x.shape[1]), axis=0)
    return s * (d * g - xn * jnp.mean(dxn * g, axis=1, keepdims=True)), gg


C0 = 0.7978845608028654
C1 = 0.044715


def ffn_body(middle_ref, gain_ref, cot_ref, wg_ref, wu_ref, wd_ref,
             out_ref, gg_ref, gu_ref, gd_ref, dmid_ref, ggain_ref,
             n2, n2t, top, dn2, hid, dg, du):
    f = pl.program_id(0)
    g2 = gain_ref[...].astype(F32)

    @pl.when(f == 0)
    def _():
        def prep(r, _):
            rs = pl.ds(pl.multiple_of(r * BLK, BLK), BLK)
            x = middle_ref[rs, :]
            n = x * rms_parts(x) * g2
            n2[rs, :] = n.astype(BF16)
            n2t[:, rs] = n.T.astype(BF16)
            top[rs, :] = cot_ref[rs, :].astype(BF16)
            out_ref[rs, :] = x
            dn2[rs, :] = jnp.zeros((BLK, 768), F32)
            return 0
        lax.fori_loop(0, TOK // BLK, prep, 0)

    def rows(r, _):
        rs = pl.ds(pl.multiple_of(r * BLK, BLK), BLK)
        n = n2[rs, :]
        v = dot(n, wg_ref[...])
        u = dot(n, wu_ref[...])
        dh = dot(top[rs, :], wd_ref[...], ((1,), (1,)))
        v2 = v * v
        t = jnp.tanh(v * (C0 + (C0 * C1) * v2))
        hp = 0.5 + 0.5 * t
        gelu = v * hp
        slope = hp + (0.5 * v) * (1.0 - t * t) * (C0 + (3.0 * C0 * C1) * v2)
        h = (gelu * u).astype(BF16)
        hid[rs, :] = h
        a = (dh * u * slope).astype(BF16)
        b = (dh * gelu).astype(BF16)
        dg[rs, :] = a
        du[rs, :] = b
        out_ref[rs, :] += dot(h, wd_ref[...])
        dn2[rs, :] += dot(a, wg_ref[...], ((1,), (1,))) + dot(b, wu_ref[...], ((1,), (1,)))
        return 0

    lax.fori_loop(0, TOK // BLK, rows, 0)
    gg_ref[...] = dot(n2t[...], dg[...]).astype(BF16)
    gu_ref[...] = dot(n2t[...], du[...]).astype(BF16)
    gd_ref[...] = dot(hid[...], top[...], ((0,), (0,))).astype(BF16)

    @pl.when(f == pl.num_programs(0) - 1)
    def _():
        ggain_ref[...] = jnp.zeros_like(ggain_ref)

        def fin(r, _):
            rs = pl.ds(pl.multiple_of(r * BLK, BLK), BLK)
            dxv, gg = rms_back(middle_ref[rs, :], g2, dn2[rs, :])
            dmid_ref[rs, :] = cot_ref[rs, :] + dxv
            ggain_ref[...] += gg
            return 0
        lax.fori_loop(0, TOK // BLK, fin, 0)


def ffn(middle, gain, cot, wg, wu, wd):
    ff = wg.shape[1]
    whole = lambda *s: pl.BlockSpec(s, lambda f: (0, 0), pipeline_mode=pl.Buffered(1))
    act = jax.ShapeDtypeStruct((TOK, 768), F32)
    wide = pl.BlockSpec((768, BLK), lambda f: (0, f))
    tall = pl.BlockSpec((BLK, 768), lambda f: (f, 0))
    return pl.pallas_call(
        ffn_body,
        grid=(ff // BLK,),
        out_shape=(act, jax.ShapeDtypeStruct((768, ff), BF16), jax.ShapeDtypeStruct((768, ff), BF16),
                   jax.ShapeDtypeStruct((ff, 768), BF16), act, jax.ShapeDtypeStruct((8, 768), F32)),
        in_specs=[whole(TOK, 768), whole(1, 768), whole(TOK, 768), wide, wide, tall],
        out_specs=(whole(TOK, 768), wide, wide, tall, whole(TOK, 768), whole(8, 768)),
        scratch_shapes=[pltpu.VMEM((TOK, 768), BF16), pltpu.VMEM((768, TOK), BF16), pltpu.VMEM((TOK, 768), BF16),
                        pltpu.VMEM((TOK, 768), F32)] + [pltpu.VMEM((TOK, BLK), BF16)] * 3,
        compiler_params=pltpu.CompilerParams(vmem_limit_bytes=60 << 20),
        name="ffn",
    )(middle, gain, cot, wg, wu, wd)

MESH = pl.DeviceIdType.MESH
HB = pl.BlockSpec(memory_space=pl.ANY)


def bit_of(v, b):
    return (v // (1 << b)) % 2


def flip(v, b):
    return v + (1 - 2 * bit_of(v, b)) * (1 << b)


def with_bits(v, bits, e):
    for i, b in enumerate(bits):
        v = v + (((e >> i) & 1) - bit_of(v, b)) * (1 << b)
    return v


def here():
    return lax.axis_index("wide"), lax.axis_index("narrow")


def greet(wide, direct):
    w, n = here()
    sem = pltpu.get_barrier_semaphore()
    peers = [(lax.rem(w + d, wide), n) for d in range(1, wide)] if direct else [
        (flip(w, b), n) for b in range(wide.bit_length() - 1)]
    peers = peers + [(w, flip(n, 0)), (w, flip(n, 1))]
    for p in peers:
        pl.semaphore_signal(sem, inc=1, device_id=p, device_id_type=MESH)
    pl.semaphore_wait(sem, len(peers))


class Ticker:
    def __init__(self):
        self.todo = {}

    def add(self, name, index, fn):
        self.todo.setdefault((name, index), []).append(fn)

    def __call__(self, name, index):
        for (loop, at), fns in self.todo.items():
            if loop == name:
                if isinstance(index, int):
                    if at == index:
                        for fn in fns:
                            fn()
                else:
                    @pl.when(index == at)
                    def _(fns=fns):
                        for fn in fns:
                            fn()


def wide_order(order, wide):
    bits = wide.bit_length() - 1
    return order if bits == len(order) else tuple(range(bits - 1, -1, -1))


class Gather:
    def __init__(self, index, shard, out, region, order, split, sems):
        self.a, self.shard, self.out = index, shard, out
        self.row, self.nrow, self.col, self.ncol = region
        self.wide = out.shape[0]
        self.order = wide_order(order, self.wide)
        self.split = None
        if split:
            if self.ncol % 512 == 0:
                self.split = "col"
            elif self.nrow % 16 == 0:
                self.split = "row"
        self.send, self.recv, self.local = sems
        self.stages = len(self.order) + (2 if self.split else 1)

    def part(self, ref, quarter=True):
        _, n = here()
        half = self.ncol // 2
        col, ncol = self.col + bit_of(n, 0) * half, half
        row, nrow = self.row, self.nrow
        if self.split == "col" and quarter:
            ncol = half // 2
            col = col + bit_of(n, 1) * ncol
        rs = pl.ds(row, nrow)
        if self.split == "row" and quarter:
            nrow = nrow // 2
            rs = pl.ds(pl.multiple_of(row + bit_of(n, 1) * nrow, 8), nrow)
        lead = (slice(None),) * (len(ref.shape) - 2)
        return ref.at[lead + (rs, pl.ds(pl.multiple_of(col, 128), ncol))]

    def copy(self, src, dst, slot, device):
        return pltpu.make_async_remote_copy(src, dst, self.send.at[self.a, slot], self.recv.at[self.a, slot],
                                            device_id=device, device_id_type=MESH)

    def copies(self, i):
        w, n = here()
        if i < len(self.order):
            dev = (flip(w, self.order[i]), n)
            out = []
            for e in range(1 << i):
                blk = with_bits(w, self.order[:i], e)
                dst = self.part(self.out.at[blk])
                src = self.part(self.shard) if i == 0 else dst
                out.append(self.copy(src, dst, (1 << i) - 1 + e, dev))
            return out
        if self.split and i == len(self.order):
            ref = self.part(self.out)
            return [self.copy(ref, ref, self.wide - 1, (w, flip(n, 1)))]
        ref = self.part(self.out, quarter=False)
        return [self.copy(ref, ref, self.wide, (w, flip(n, 0)))]

    def own(self):
        w, _ = here()
        return pltpu.make_async_copy(self.part(self.shard), self.part(self.out.at[w]), self.local.at[self.a])

    def start(self, i):
        if i == 0:
            self.own().start()
        else:
            self.finish(i - 1)
            if i == 1:
                self.own().wait()
        for c in self.copies(i):
            c.start()

    def finish(self, i):
        for c in self.copies(i):
            c.wait_recv()

    def drain(self):
        for i in range(self.stages):
            for c in self.copies(i):
                c.wait_send()


class Total:
    def __init__(self, acc, slots, send, recv, wide, narrow):
        self.acc, self.slots, self.send, self.recv = acc, slots, send, recv
        self.bits = [("w", b) for b in range(wide.bit_length() - 1)] + [("n", b) for b in range(narrow.bit_length() - 1)]
        self.stages = len(self.bits)

    def copy(self, i):
        w, n = here()
        axis, b = self.bits[i]
        dev = (flip(w, b), n) if axis == "w" else (w, flip(n, b))
        return pltpu.make_async_remote_copy(self.acc.at[i], self.slots.at[i], self.send.at[i], self.recv.at[i],
                                            device_id=dev, device_id_type=MESH)

    def start(self, i):
        if i > 0:
            self.finish(i - 1)
        self.copy(i).start()

    def finish(self, i):
        self.copy(i).wait()
        self.acc[i + 1] = self.acc[i] + self.slots[i]


GATHERS = (
    (0, 0, (2, 1, 0), True),
    (1, 0, (2, 1, 0), False),
    (2, 0, (2, 0, 1), False),
    (3, 0, (2, 1, 0), True),
    (4, 0, (2, 0, 1), False),
    (4, 1, (2, 0, 1), True),
    (5, 0, (0, 2, 1), True),
    (5, 1, (1, 2, 0), False),
    (6, 0, (2, 0, 1), False),
    (6, 1, (2, 1, 0), False),
)
GATHER_PLAN = {
    ("begin", 0): [(2, 0), (0, 0), (1, 0)],
    ("table", 0): [(2, 1), (0, 1), (1, 1), (6, 0)],
    ("plane", 3): [(3, 0)],
    ("plane", 7): [(9, 0)],
    ("plane", 10): [(6, 1)],
    ("rows", 0): [(0, 2)],
    ("rows", 1): [(3, 1), (2, 2)],
    ("rows", 7): [(1, 2)],
    ("project", 0): [(5, 0), (9, 1), (3, 2), (4, 0), (6, 2)],
    ("att", 0): [(8, 0)],
    ("att", 1): [(3, 3), (7, 0)],
    ("att", 2): [(5, 1)],
    ("att", 4): [(4, 1)],
    ("att", 6): [(5, 2)],
    ("att", 8): [(3, 4), (8, 1)],
    ("att", 9): [(9, 2), (4, 2), (7, 1), (6, 3)],
    ("att", 12): [(5, 3)],
    ("att", 15): [(8, 2)],
    ("att", 17): [(7, 2)],
    ("att", 19): [(9, 3), (6, 4)],
    ("att", 22): [(5, 4), (4, 3)],
    ("outproj", 0): [(7, 3), (8, 3)],
}


def chunk_region(weight, chunk, rows, cols):
    if weight < 4:
        return (0, rows, 0, cols)
    if weight < 6:
        return (0, rows, chunk * (cols // 2), cols // 2)
    return (chunk * (rows // 2), rows // 2, 0, cols)


def front_body(wide, narrow, len_ref, bcol_ref, emb_ref, small_ref,
               sq, sk, sv, so, sg, su, sd,
               oq, ok, ov, oo, og, ou, od,
               start_ref, conv_ref, csum_ref, tot_ref, smallall_ref, emball_ref,
               qs_ref, k_ref, v_ref, ctx_ref, qx_ref, normed_ref, middle_ref,
               table, onehot, planes, coef, tiles, ent, kx, vext, kext, qxf, vq, vk, vv, vo,
               embs, smalls, tacc, tslots,
               gsend, grecv, glocal, psend, precv, tsend, trecv, wsem):
    w, n = here()
    embs[w] = emb_ref[...]
    smalls[w] = small_ref[...]
    greet(wide, True)
    shards, outs = (sq, sk, sv, so, sg, su, sd), (oq, ok, ov, oo, og, ou, od)
    gathers = [Gather(i, shards[a], outs[a], chunk_region(a, c, *shards[a].shape), order, split, (gsend, grecv, glocal))
               for i, (a, c, order, split) in enumerate(GATHERS)]
    tick = Ticker()
    started = [0] * len(gathers)

    half = emb_ref.shape[1] // 2
    hcols = pl.ds(pl.multiple_of(bit_of(n, 0) * half, 128), half)
    small_copies, emb_copies = [], []
    for d in range(1, wide):
        peer = (lax.rem(w + d, wide), n)
        emb_copies.append(pltpu.make_async_remote_copy(
            emb_ref.at[:, hcols], embs.at[w, :, hcols], psend.at[0, d], precv.at[0, d], device_id=peer, device_id_type=MESH))
        small_copies.append(pltpu.make_async_remote_copy(
            small_ref, smalls.at[w], psend.at[1, d], precv.at[1, d], device_id=peer, device_id_type=MESH))
    for c in emb_copies + small_copies:
        c.start()
    swap = pltpu.make_async_remote_copy(embs.at[:, :, hcols], embs.at[:, :, hcols], psend.at[0, 0], precv.at[0, 0],
                                        device_id=(w, flip(n, 0)), device_id_type=MESH)

    def params():
        for c in emb_copies:
            c.wait_recv()
        swap.start()
        for c in small_copies:
            c.wait_recv()
        per = 768 // wide
        l = lax.broadcasted_iota(jnp.int32, (128, 768), 0)
        c = lax.broadcasted_iota(jnp.int32, (128, 768), 1)
        small = sum(dot(smalls[i].astype(BF16), jnp.where((c == per * i + l) & (l < per), 1.0, 0.0).astype(BF16))
                    for i in range(wide))
        smallall_ref[...] = small
        swap.wait()
        emb = embs[...].astype(F32).reshape(256, 768)
        emball_ref[...] = emb.astype(BF16)
        return emb, small

    for (loop, at), stages in GATHER_PLAN.items():
        for g, s in stages:
            if s < gathers[g].stages:
                tick.add(loop, at, functools.partial(gathers[g].start, s))
                started[g] = s + 1
    weights = list(zip((0, 1, 2), outs[:3], (vq, vk, vv)))

    def load(ws, sem0):
        copies = []
        for j, (_, src, dst) in enumerate(ws):
            r = src.shape[1]
            for i in range(wide):
                copies.append(pltpu.make_async_copy(src.at[i], dst.at[pl.ds(r * i, r)], wsem.at[sem0 + j, i]))
        return copies

    def ready(ids):
        for g in ids:
            for s in range(started[g], gathers[g].stages):
                gathers[g].start(s)
            gathers[g].finish(gathers[g].stages - 1)

    def qkv_ready():
        ready((0, 1, 2))
        cs = load(weights, 0)
        for c in cs:
            c.start()
        for c in cs:
            c.wait()

    tick.add("project", 0, qkv_ready)
    total = Total(tacc, tslots, tsend, trecv, wide, narrow)

    def total_begin():
        lane = lax.broadcasted_iota(jnp.int32, (8, 128), 1)
        tacc[0] = jnp.where(lane == 0, len_ref[0, 0].astype(F32), jnp.where(lane == 1, ent[...], 0.0))
        total.start(0)

    tick.add("att", 1, total_begin)
    for i in range(1, total.stages):
        tick.add("att", 1 + 2 * i, functools.partial(total.start, i))

    def out_ready():
        total.finish(total.stages - 1)
        tot_ref[...] = tacc[total.stages]
        ready((3,))
        cs = load([(3, outs[3], vo)], 3)
        for c in cs:
            c.start()
        for c in cs:
            c.wait()

    tick.add("outproj", 0, out_ready)
    tick("begin", 0)
    gbst_fwd_body(tick, params, len_ref, bcol_ref, start_ref, conv_ref, csum_ref, ent, table, onehot, planes, coef, tiles)
    att_fwd_body(tick, len_ref, start_ref, smallall_ref[pl.ds(5, 1), :], vq, vk, vv, vo,
                 qs_ref, k_ref, v_ref, ctx_ref, qx_ref, normed_ref, middle_ref, kx, vext, kext, qxf)
    ready(range(4, len(gathers)))
    for c in emb_copies + small_copies:
        c.wait_send()
    for g in gathers:
        g.drain()


def front(wide, narrow, length, bcol, emb, small, shards):
    b = jax.ShapeDtypeStruct((TOK, 768), BF16)
    f = jax.ShapeDtypeStruct((TOK, 768), F32)
    gathered = tuple(jax.ShapeDtypeStruct((wide,) + s.shape, s.dtype) for s in shards)
    sq = pltpu.VMEM((768, 768), BF16)
    ng = len(GATHERS)
    dma = pltpu.SemaphoreType.DMA
    stages = (wide * narrow).bit_length() - 1
    return pl.pallas_call(
        functools.partial(front_body, wide, narrow),
        out_shape=gathered + (
            f, jax.ShapeDtypeStruct((PERIOD, GROUPS, 768), BF16), jax.ShapeDtypeStruct((GROUPS, 128), F32),
            jax.ShapeDtypeStruct((8, 128), F32), jax.ShapeDtypeStruct((8, 768), F32), jax.ShapeDtypeStruct((256, 768), BF16),
            b, b, b, b, jax.ShapeDtypeStruct((TOK, 128), BF16), b, f),
        in_specs=[SM, VM, VM, VM] + [HB] * 7,
        out_specs=(HB,) * 7 + (VM,) * 13,
        scratch_shapes=[
            pltpu.VMEM((1024, 768), BF16), pltpu.VMEM((GROUPS, 256 * 15), BF16), pltpu.VMEM((PERIOD, GROUPS, 768), F32),
            pltpu.VMEM((4, GROUPS, 128), F32), pltpu.VMEM((6, 6 * GROUPS, 128), F32), pltpu.VMEM((8, 128), F32),
            pltpu.VMEM((TOK, 128), BF16), pltpu.VMEM((2, TOK, 256), BF16), pltpu.VMEM((2, TOK, 256), BF16),
            pltpu.VMEM((TOK, 128), F32), sq, sq, sq, sq,
            pltpu.VMEM((wide,) + emb.shape, BF16), pltpu.VMEM((wide, 8, 128), F32),
            pltpu.VMEM((stages + 1, 8, 128), F32), pltpu.VMEM((stages, 8, 128), F32),
            dma((ng, wide + 1)), dma((ng, wide + 1)), dma((ng,)), dma((2, wide)), dma((2, wide)), dma((stages,)), dma((stages,)),
            dma((4, wide))],
        compiler_params=pltpu.CompilerParams(vmem_limit_bytes=60 << 20, collective_id=0, has_side_effects=True),
        name="front",
    )(length, bcol, emb, small, *shards)


class Scatter:
    def __init__(self, index, data, out, region, order, early, bufs, sems):
        self.a, self.data, self.out = index, data, out
        self.row, self.nrow, self.col, self.ncol = region
        self.wide = data.shape[0]
        self.order = wide_order(order, self.wide)
        self.nb = len(self.order)
        self.early = early_split(early, region)
        self.cb, self.wb, self.yb, self.fs, self.fb = bufs
        self.send, self.recv = sems
        self.kinds = ["core"] + (["early"] if self.early else []) + [("wide", i) for i in range(self.nb)]
        self.kinds += ["join" if self.early else "late", "swap"]
        self.stages = len(self.kinds)

    def share(self, other=False):
        _, n = here()
        half = self.ncol // 2
        b0 = bit_of(n, 0)
        b0 = 1 - b0 if other else b0
        return pl.ds(self.row, self.nrow), pl.ds(pl.multiple_of(self.col + b0 * half, 128), half)

    def quarter(self, other=False, base=True):
        _, n = here()
        half = self.ncol // 2
        b1 = bit_of(n, 1)
        b1 = 1 - b1 if other else b1
        row, nrow, ncol = (self.row if base else 0), self.nrow, half
        col = self.col + bit_of(n, 0) * half if base else 0
        if self.early == "col":
            ncol = half // 2
            col = pl.multiple_of(col + b1 * ncol, 128)
        elif self.early == "row":
            nrow = nrow // 2
            row = pl.multiple_of(row + b1 * nrow, 8)
        if base:
            col = pl.multiple_of(col, 128)
        return pl.ds(row, nrow), pl.ds(col, ncol)

    def mine(self):
        return self.quarter() if self.early else self.share()

    def copy(self, src, dst, slot, device):
        return pltpu.make_async_remote_copy(src, dst, self.send.at[self.a, slot], self.recv.at[self.a, slot],
                                            device_id=device, device_id_type=MESH)

    def base(self, i):
        return sum(1 << (self.nb - 1 - j) for j in range(i))

    def copies(self, s):
        w, n = here()
        kind = self.kinds[s]
        W = self.wide
        if kind == "core":
            r, c = self.share(other=True)
            return [self.copy(self.data.at[:, r, c], self.cb, W - 1, (w, flip(n, 0)))]
        if kind == "early":
            r, c = self.quarter(other=True)
            return [self.copy(self.data.at[:, r, c], self.yb, W, (w, flip(n, 1)))]
        r, c = self.mine()
        if kind == "late":
            return [self.copy(self.data.at[w, r, c], self.yb, W, (w, flip(n, 1)))]
        if kind == "join":
            ref = self.fs.at[self.quarter(base=False)]
            return [self.copy(ref, ref, W + 1, (w, flip(n, 1)))]
        if kind == "swap":
            return [self.copy(self.fs, self.fb, W + 2, (w, flip(n, 0)))]
        i = kind[1]
        peer = flip(w, self.order[i])
        out = []
        for e in range(1 << (self.nb - 1 - i)):
            blk = with_bits(peer, self.order[i + 1:], e)
            out.append(self.copy(self.data.at[blk, r, c], self.wb.at[self.base(i) + e], self.base(i) + e, (peer, n)))
        return out

    def add(self, blk, where, term):
        idx = (blk,) + where
        self.data[idx] = (self.data[idx].astype(F32) + term.astype(F32)).astype(BF16)

    def combine(self, s):
        w, n = here()
        for c in self.copies(s):
            c.wait_recv()
        kind = self.kinds[s]
        if kind in ("core", "early"):
            where = self.share() if kind == "core" else self.quarter()
            if kind == "core" and self.early:
                pass
            buf = self.cb if kind == "core" else self.yb

            def block(b, _):
                self.add(b, where, buf[b])
                return 0

            lax.fori_loop(0, self.wide, block, 0)
        elif kind == "late":
            self.fs[...] = (self.data[(w,) + self.mine()].astype(F32) + self.yb[...].astype(F32)).astype(BF16)
        elif kind == "swap":
            r, c = self.share()
            self.out[r, c] = self.fs[...].astype(F32)
            r, c = self.share(other=True)
            self.out[r, c] = self.fb[...].astype(F32)
        elif kind != "join":
            i = kind[1]
            for e in range(1 << (self.nb - 1 - i)):
                self.add(with_bits(w, self.order[i + 1:], e), self.mine(), self.wb[self.base(i) + e])
            if i == self.nb - 1 and self.early:
                self.fs[self.quarter(base=False)] = self.data[(w,) + self.mine()]

    def start(self, s):
        if s > 0:
            self.combine(s - 1)
        for c in self.copies(s):
            c.start()

    def finish(self):
        self.combine(self.stages - 1)

    def drain(self):
        for s in range(self.stages):
            for c in self.copies(s):
                c.wait_send()


def early_split(early, region):
    if not early:
        return None
    if region[3] % 512 == 0:
        return "col"
    return "row" if region[1] % 32 == 0 else None


def scatter_buffers(wide, region, early):
    _, nrow, _, ncol = region
    half = ncol // 2
    kind = early_split(early, region)
    qr, qc = (nrow // 2, half) if kind == "row" else (nrow, half // 2) if kind == "col" else (nrow, half)
    y = (wide, qr, qc) if kind else (nrow, half)
    return [pltpu.VMEM((wide, nrow, half), BF16), pltpu.VMEM((wide - 1, qr, qc), BF16), pltpu.VMEM(y, BF16),
            pltpu.VMEM((nrow, half), BF16), pltpu.VMEM((nrow, half), BF16)]


SCATTERS = (
    (0, 0, (0, 1, 2), False),
    (0, 1, (1, 0, 2), False),
    (1, 0, (0, 1, 2), False),
    (1, 1, (0, 1, 2), True),
    (2, 0, (0, 1, 2), True),
    (2, 1, (0, 2, 1), True),
    (3, 0, (2, 1, 0), False),
)
SCATTER_PLAN = {
    ("begin", 0): [(3, 0), (2, 0)],
    ("head", 2): [(4, 0), (1, 0)],
    ("gout", 0): [(3, 1), (2, 1)],
    ("bwd", 0): [(5, 0)],
    ("bwd", 1): [(4, 1), (6, 0), (1, 1)],
    ("bwd", 2): [(0, 0)],
    ("bwd", 3): [(5, 1)],
    ("bwd", 4): [(6, 1)],
    ("bwd", 5): [(0, 1)],
    ("bwd", 7): [(2, 2)],
    ("bwd", 10): [(1, 2)],
    ("bwd", 12): [(3, 2), (0, 2)],
    ("bwd", 14): [(6, 2), (2, 3)],
    ("bwd", 15): [(4, 2), (1, 3)],
    ("bwd", 16): [(5, 2)],
    ("bwd", 17): [(3, 3)],
    ("bwd", 18): [(0, 3)],
    ("bwd", 21): [(4, 3), (2, 4)],
    ("bwd", 22): [(5, 3)],
    ("bwd", 23): [(6, 3), (1, 4)],
    ("wgrad", 0): [(3, 4), (2, 5), (0, 4)],
    ("wgrad", 2): [(4, 4), (2, 6)],
    ("last", 0): [(5, 4), (6, 4), (1, 5)],
    ("last", 2): [(3, 5), (1, 6), (0, 5)],
    ("last", 3): [(4, 5), (5, 5)],
}


def scatter_region(weight, chunk, rows, cols):
    if weight == 3:
        return (0, rows, 0, cols)
    if weight < 2:
        return (0, rows, chunk * (cols // 2), cols // 2)
    return (chunk * (rows // 2), rows // 2, 0, cols)


def back_body(wide, nin, *refs):
    ins, refs = refs[:17], refs[17:]
    outs, refs = refs[:9], refs[9:]
    att, refs = refs[:9], refs[9:]
    gfull, refs = refs[0], refs[1:]
    bufs, (ssend, srecv) = refs[:-2], refs[-2:]
    greet(wide, False)
    tick = Ticker()
    datas = (ins[14], ins[15], ins[16], gfull)
    results = outs[5:9]
    scatters = []
    for i, (a, c, order, early) in enumerate(SCATTERS):
        region = scatter_region(a, c, *datas[a].shape[1:])
        scatters.append(Scatter(i, datas[a], results[a], region, order, early, bufs[5 * i:5 * i + 5], (ssend, srecv)))
    started = [0] * len(scatters)
    for (loop, at), stages in SCATTER_PLAN.items():
        for g, s in stages:
            if s == scatters[g].stages:
                tick.add(loop, at, scatters[g].finish)
                started[g] = s + 1
            elif s < scatters[g].stages:
                tick.add(loop, at, functools.partial(scatters[g].start, s))
                started[g] = s + 1
    tick("begin", 0)
    att_bwd_body(tick, gfull, *ins[:14], *outs[:5], *att)
    for s in range(16):
        for g, sc in enumerate(scatters):
            if started[g] <= s < sc.stages:
                sc.start(s)
            elif s == sc.stages and started[g] <= s:
                sc.finish()
    for sc in scatters:
        sc.drain()


def back(wide, args, ffn_grads):
    w = jax.ShapeDtypeStruct((768, 768), BF16)
    act = pltpu.VMEM((TOK, 768), BF16)
    rows = 768 // wide
    shapes = [x.shape[1:] for x in ffn_grads] + [(rows, 768)]
    bufs = []
    for a, c, _, early in SCATTERS:
        bufs += scatter_buffers(wide, scatter_region(a, c, *shapes[a]), early)
    dma = pltpu.SemaphoreType.DMA((len(SCATTERS), wide + 3))
    return pl.pallas_call(
        functools.partial(back_body, wide, 14),
        out_shape=(w, w, w, jax.ShapeDtypeStruct((TOK, 768), F32), jax.ShapeDtypeStruct((8, 768), F32))
        + tuple(jax.ShapeDtypeStruct(s, F32) for s in shapes),
        in_specs=[SM] + [VM] * 16,
        out_specs=(VM,) * 9,
        scratch_shapes=[act, pltpu.VMEM((TOK, 128), BF16), act, act, act, pltpu.VMEM((128, TOK), F32),
                        pltpu.VMEM((TOK, 256), BF16), pltpu.VMEM((TOK, 256), BF16), act,
                        pltpu.VMEM((wide, rows, 768), BF16)] + bufs + [dma, dma],
        compiler_params=pltpu.CompilerParams(vmem_limit_bytes=63 << 20, collective_id=1, has_side_effects=True),
        name="back",
    )(*args, *ffn_grads)


TAIL = ((0, 0, (0, 1, 2), False), (1, 0, (1, 0, 2), False), (2, 0, (2, 0, 1), False))
TAIL_PLAN = {
    ("begin", 0): [(1, 0), (2, 0), (0, 0)],
    ("first", 3): [(1, 1)],
    ("first", 6): [(2, 1)],
    ("first", 8): [(0, 1)],
    ("second", 10): [(1, 2)],
    ("taps", 3): [(0, 2)],
}


def tail_body(wide, *refs):
    ins, refs = refs[:11], refs[11:]
    qkv, refs = refs[:3], refs[3:]
    (gembs, smalls, *results), refs = refs[:5], refs[5:]
    work, refs = refs[:9], refs[9:]
    (cb, esend, eb, ysend, yb, fs, fb, sall, sb, ssum, yss), refs = refs[:11], refs[11:]
    bufs, (ssend, srecv, dsend, drecv) = refs[:-4], refs[-4:]
    w, n = here()
    greet(wide, True)
    tick = Ticker()
    scatters = [Scatter(i, qkv[a], results[a], scatter_region(3, 0, *qkv[a].shape[1:]), order, early,
                        bufs[5 * i:5 * i + 5], (ssend, srecv)) for i, (a, c, order, early) in enumerate(TAIL)]
    started = [0] * len(scatters)
    for (loop, at), stages in TAIL_PLAN.items():
        for g, s in stages:
            if s == scatters[g].stages:
                tick.add(loop, at, scatters[g].finish)
                started[g] = s + 1
            elif s < scatters[g].stages:
                tick.add(loop, at, functools.partial(scatters[g].start, s))
                started[g] = s + 1
    tick("begin", 0)
    len_ref, invc_ref, brow_ref, emb_ref, small_ref, dstart_ref, conv_ref, csum_ref, gg1_ref, gg2_ref, _ = ins
    gemb, gconv, gscore = work[:3]
    gbst_bwd_body(tick, len_ref, invc_ref, brow_ref, emb_ref, small_ref.at[pl.ds(0, 4)], small_ref.at[pl.ds(4, 1)],
                  dstart_ref, conv_ref, csum_ref, gemb, gconv, gscore, *work[3:])

    def copy(src, dst, k, slot, device):
        return pltpu.make_async_remote_copy(src, dst, dsend.at[k, slot], drecv.at[k, slot],
                                            device_id=device, device_id_type=MESH)

    per = 768 // wide
    r8 = lax.broadcasted_iota(jnp.int32, (8, 768), 0)
    total = gconv[...] * jnp.where(r8 < 4, 1.0, 0.0)
    for row, ref in ((4, gscore), (5, gg1_ref), (6, gg2_ref)):
        total = jnp.where(r8 == row, jnp.sum(ref[...], axis=0, keepdims=True), total)
    rl = lax.broadcasted_iota(jnp.int32, (768, 128), 0)
    cl = lax.broadcasted_iota(jnp.int32, (768, 128), 1)
    for i in range(wide):
        sall[i] = dot(total, jnp.where((rl == per * i + cl) & (cl < per), 1.0, 0.0).astype(F32), precision=HIGH)
    rows = 256 // wide
    half = 384
    gc = lambda b: pl.ds(pl.multiple_of(b * half, 128), half)
    b0 = bit_of(n, 0)
    esend[...] = gemb[:, gc(1 - b0)].astype(BF16).reshape(esend.shape)
    core = copy(esend, cb, 0, 0, (w, flip(n, 0)))
    core.start()
    peers = [(lax.rem(w + d, wide), n) for d in range(1, wide)]
    small_copies = [copy(sall.at[p[0]], sb.at[w], 1, d + 1, p) for d, p in enumerate(peers)]
    for c in small_copies:
        c.start()
    core.wait()
    mine = gemb[:, gc(b0)].reshape(esend.shape) + cb[...].astype(F32)
    esend[...] = mine.astype(BF16)
    emb_copies = [copy(esend.at[p[0]], eb.at[w], 2, d + 1, p) for d, p in enumerate(peers)]
    for c in emb_copies:
        c.start()
    sb[w] = sall[w]
    eb[w] = esend[w]
    for s in range(16):
        for g, sc in enumerate(scatters):
            if started[g] <= s < sc.stages:
                sc.start(s)
            elif s == sc.stages and started[g] <= s:
                sc.finish()
    for c in small_copies + emb_copies:
        c.wait_recv()
    ysend[...] = sum(eb[i].astype(F32) for i in range(wide))
    ssum[0] = sum(sb[i] for i in range(wide))
    late = [copy(ysend, yb, 3, 0, (w, flip(n, 1))), copy(ssum.at[0], yss.at[0], 3, 1, (w, flip(n, 1)))]
    for c in late:
        c.start()
    for c in late:
        c.wait_recv()
    fs[...] = (ysend[...] + yb[...]).astype(BF16)
    ssum[1] = ssum[0] + yss[0]
    last = [copy(fs, fb, 4, 0, (w, flip(n, 0))), copy(ssum.at[1], yss.at[1], 4, 1, (w, flip(n, 0)))]
    for c in last:
        c.start()
    for c in last:
        c.wait_recv()
    gembs[:, gc(b0)] = fs[...].astype(F32)
    gembs[:, gc(1 - b0)] = fb[...].astype(F32)
    smalls[...] = ssum[1] + yss[1]
    for c in small_copies + emb_copies + late + last:
        c.wait_send()
    for sc in scatters:
        sc.drain()


def tail(wide, args, qkv):
    rows, per = 256 // wide, 768 // wide
    bufs = []
    for a, c, _, early in TAIL:
        bufs += scatter_buffers(wide, scatter_region(3, 0, per, 768), early)
    v = pltpu.VMEM
    dma = pltpu.SemaphoreType.DMA((len(TAIL), wide + 3))
    ddma = pltpu.SemaphoreType.DMA((5, wide))
    shard = jax.ShapeDtypeStruct((per, 768), F32)
    return pl.pallas_call(
        functools.partial(tail_body, wide),
        out_shape=(jax.ShapeDtypeStruct((rows, 768), F32), jax.ShapeDtypeStruct((8, 128), F32), shard, shard, shard),
        in_specs=[SM, SM] + [VM] * 12,
        out_specs=(VM,) * 5,
        scratch_shapes=[
            v((256, 768), F32), v((8, 768), F32), v((8, 768), F32),
            v((6, GROUPS, 768), F32), v((3, GROUPS, 128), F32), v((6, GROUPS, 128), F32), v((2304, 768), BF16),
            v((256, 2304), BF16), v((6, 6 * GROUPS, 128), F32),
            v((wide, rows, 384), BF16), v((wide, rows, 384), BF16), v((wide, rows, 384), BF16), v((rows, 384), F32),
            v((rows, 384), F32), v((rows, 384), BF16), v((rows, 384), BF16), v((wide, 8, 128), F32), v((wide, 8, 128), F32),
            v((2, 8, 128), F32), v((2, 8, 128), F32)] + bufs + [dma, dma, ddma, ddma],
        compiler_params=pltpu.CompilerParams(vmem_limit_bytes=60 << 20, collective_id=2, has_side_effects=True),
        name="tail",
    )(*args, *qkv)


def body(
    wide, narrow,
    byte_values, row_lengths, embedding, conv_kernel, score_vector, attn_gain, query_weight, key_weight,
    value_weight, output_weight, ffn_gain, gate_weight, up_weight, down_weight, cotangent,
):
    length = row_lengths.reshape(1, 1)
    bcol, brow = byte_planes(byte_values[0], row_lengths[0])
    small = jnp.concatenate([conv_kernel, score_vector[None], attn_gain[None], ffn_gain[None]], axis=0).astype(F32)
    small = jnp.pad(small, ((0, 8 - small.shape[0]), (0, 128 - small.shape[1])))
    shards = (query_weight, key_weight, value_weight, output_weight, gate_weight, up_weight, down_weight)
    got = front(wide, narrow, length, bcol, embedding, small, shards)
    wq, wk, wv, wo, wg, wu, wd = [x.reshape(-1, x.shape[-1]) for x in got[:7]]
    start, conv, csum, tot, smallall, emb, qs, k, v, ctx, qx, normed, middle = got[7:]
    count, entropy_total = tot[0, 0], tot[0, 1]
    entropy = entropy_total / count
    g1, g2 = smallall[5:6], smallall[6:7]
    blocks = lambda x: x.reshape(wide, x.shape[0] // wide, x.shape[1])
    out, gg, gu, gd, dmid, gg2 = ffn(middle, g2, cotangent[0], wg, wu, wd)
    gq, gk, gv, dstart, gg1, sg, su, sd, so = back(
        wide, (length, dmid, start, g1, qs, k, v, ctx, qx, normed, wq, wk, wv, wo), [blocks(x) for x in (gg, gu, gd)])
    ge, gs, sq, sk, sv = tail(
        wide, (length, (ENT_WEIGHT / count).reshape(1, 1), brow, emb, smallall, dstart, conv, csum, gg1, gg2, qx),
        [blocks(x) for x in (gq, gk, gv)])
    per = 768 // wide
    return (out[None], entropy, ge, gs[:4, :per], gs[4, :per], gs[5, :per], sq, sk, sv, so, gs[6, :per], sg, su, sd)


def solution(mesh):
    both = ("wide", "narrow")
    row, flat = P("wide", None), P("wide")
    return jax.shard_map(
        functools.partial(body, mesh.shape["wide"], mesh.shape["narrow"]),
        mesh=mesh,
        in_specs=(P(both, None), P(both), row, P(None, "wide"), flat, flat, row, row, row, row, flat,
                  row, row, row, P(both, None, None)),
        out_specs=(P(both, None, None), P(), row, P(None, "wide"), flat, flat, row, row, row, row, flat,
                   row, row, row),
        check_vma=False,
    )
```

```python
import functools
import jax
import jax.numpy as jnp
from jax import lax
from jax.experimental import pallas as pl
from jax.experimental.pallas import tpu as pltpu
from jax.sharding import PartitionSpec as P

F32 = jnp.float32
BF16 = jnp.bfloat16
EPS = 1e-06
HEADS = 12
ENT_WEIGHT = 1.0
PERIOD = 12
GROUPS = 176
HIGH = lax.Precision.HIGHEST
VM = pl.BlockSpec(memory_space=pltpu.VMEM)
SM = pl.BlockSpec(memory_space=pltpu.SMEM)


def dot(a, b, dims=((1,), (0,)), precision=None):
    return lax.dot_general(a, b, (dims, ((), ())), precision=precision, preferred_element_type=F32)


def same_block(size):
    r = lax.broadcasted_iota(jnp.int32, (128, 128), 0)
    c = lax.broadcasted_iota(jnp.int32, (128, 128), 1)
    return jnp.where((r // size == c // size) & (r < PERIOD) & (c < PERIOD), 1.0, 0.0).astype(F32)


def block_sum(x, size):
    return dot(x, same_block(size), precision=HIGH)


def lane_scalars(csum, length):
    i = lax.broadcasted_iota(jnp.int32, (GROUPS, 128), 0)
    k = lax.broadcasted_iota(jnp.int32, (GROUPS, 128), 1)
    mask = jnp.where((PERIOD * i + k < length) & (k < PERIOD), 1.0, 0.0).astype(F32)
    tok = block_sum(jnp.where(k % 2 == 0, mask, 0.0), 2)
    inv = [jnp.ones_like(mask)] + [1.0 / jnp.maximum(block_sum(mask, b), 1.0) for b in (2, 3, 4)]
    scores = [csum] + [block_sum(csum, b) * inv[b - 1] for b in (2, 3, 4)]
    top = functools.reduce(jnp.maximum, scores)
    ex = [jnp.exp(s - top) for s in scores]
    total = ex[0] + ex[1] + ex[2] + ex[3]
    rec = 1.0 / total
    chance = [e * rec for e in ex]
    mean = sum(c * s for c, s in zip(chance, scores))
    ent = mask * (top + jnp.log(total) - mean)
    alpha = [c * v for c, v in zip(chance, inv)]
    return mask, tok, inv, scores, chance, mean, ent, alpha


def gbst_fwd_body(tick, params, len_ref, bcol_ref, start_ref, conv_ref, csum_ref, ent_ref,
                  table, onehot, planes, coef, tiles):
    length = len_ref[0, 0]
    vocab = lax.broadcasted_iota(jnp.int32, (GROUPS, 256), 1)
    for k in range(PERIOD + 3):
        onehot[:, pl.ds(256 * k, 256)] = jnp.where(bcol_ref[:, k:k + 1] == vocab, 1.0, 0.0).astype(BF16)
    csum_ref[...] = jnp.zeros_like(csum_ref)
    tick("onehot", 0)
    emb, small = params()
    for j in range(4):
        table[pl.ds(256 * j, 256), :] = (emb * small[j:j + 1]).astype(BF16)
    s = small[4:5]
    tick("table", 0)
    rows = lax.broadcasted_iota(jnp.int32, (GROUPS, 1), 0)
    lane = lax.broadcasted_iota(jnp.int32, (GROUPS, 128), 1)

    def plane(k, _):
        tick("plane", k)
        lhs = onehot[:, pl.ds(pl.multiple_of(256 * k, 256), 1024)]
        out = dot(lhs, table[...])
        out = jnp.where(PERIOD * rows + k < length, out, 0.0)
        planes[k] = out
        conv_ref[k] = out.astype(BF16)
        c = jnp.sum(out * s, axis=1, keepdims=True)
        csum_ref[...] = jnp.where(lane == k, c, csum_ref[...])
        return 0

    lax.fori_loop(0, PERIOD, plane, 0)
    mask, tok, inv, scores, chance, mean, ent, alpha = lane_scalars(csum_ref[...], length)
    ent_ref[...] = jnp.sum(jnp.sum(ent, axis=0, keepdims=True), axis=1, keepdims=True) + jnp.zeros((8, 128), F32)
    half = 0.5 * tok
    coef[0] = (alpha[0] + block_sum(alpha[1], 2)) * half
    coef[1] = alpha[2] * half
    coef[2] = block_sum(alpha[2], 2) * half
    coef[3] = block_sum(alpha[3], 2) * half

    def rowblock(ib, _):
        tick("rows", ib)
        r0 = pl.multiple_of(ib * 16, 16)
        rs = pl.ds(r0, 16)
        ce, c3, c3p, c4p = [coef[n, rs, :] for n in range(4)]
        for lt in range(6):
            ls = pl.ds(128 * lt, 128)
            p = [planes[k, rs, ls] for k in range(PERIOD)]
            pair = [p[2 * m] + p[2 * m + 1] for m in range(6)]
            quad = [pair[2 * y] + pair[2 * y + 1] for y in range(3)]
            tri = [p[3 * x] + p[3 * x + 1] + p[3 * x + 2] for x in range(4)]
            for m in range(6):
                a, b = 2 * m, 2 * m + 1
                out = ce[:, a:a + 1] * p[a] + ce[:, b:b + 1] * p[b] + c4p[:, a:a + 1] * quad[m // 2]
                if a // 3 == b // 3:
                    out = out + c3p[:, a:a + 1] * tri[a // 3]
                else:
                    out = out + c3[:, a:a + 1] * tri[a // 3] + c3[:, b:b + 1] * tri[b // 3]
                tiles[lt, pl.ds(6 * r0 + m, 16, stride=6), :] = out
        return 0

    lax.fori_loop(0, GROUPS // 16, rowblock, 0)
    for lt in range(6):
        start_ref[:, pl.ds(128 * lt, 128)] = tiles[lt, pl.ds(0, start_ref.shape[0]), :]


def gbst_bwd_body(tick, len_ref, invc_ref, brow_ref, emb_ref, ck_ref, sc_ref, conv_ref, csum_ref,
                  gemb_ref, gconv_ref, gscore_ref, dm, dots, coef, dconv, onehot, tiles):
    length = len_ref[0, 0]
    at = lambda k, r0: pl.ds(pl.multiple_of(GROUPS * k + r0, 16), 16)
    invc = invc_ref[0, 0]
    mask, tok, inv, scores, chance, mean, ent, alpha = lane_scalars(csum_ref[...], length)
    half = 0.5 * tok
    coef[0] = half
    lane16 = lax.broadcasted_iota(jnp.int32, (16, 128), 1)

    def first(ib, _):
        tick("first", ib)
        r0 = pl.multiple_of(ib * 16, 16)
        rs = pl.ds(r0, 16)
        h = coef[0, rs, :]
        acc = [jnp.zeros((16, 128), F32) for _ in range(26)]
        for lt in range(6):
            ls = pl.ds(128 * lt, 128)
            p = [conv_ref[at(k, r0), ls].astype(F32) for k in range(PERIOD)]
            quad = [(p[4 * y] + p[4 * y + 1]) + (p[4 * y + 2] + p[4 * y + 3]) for y in range(3)]
            tri = [p[3 * x] + p[3 * x + 1] + p[3 * x + 2] for x in range(4)]
            n = 0
            for m in range(6):
                d = tiles[lt, pl.ds(6 * r0 + m, 16, stride=6), :] * h[:, 2 * m:2 * m + 1]
                dm[at(m, r0), ls] = d
                for q in terms(m, p, quad, tri):
                    acc[n] = acc[n] + d * q
                    n += 1
        g1 = jnp.zeros((16, 128), F32)
        g3 = jnp.zeros((16, 128), F32)
        g4 = jnp.zeros((16, 128), F32)
        n = 0
        for m in range(6):
            a, b = 2 * m, 2 * m + 1
            v = [jnp.sum(acc[n + q], axis=1, keepdims=True) for q in range(len(TERMS[m]))]
            n += len(TERMS[m])
            g1 = jnp.where(lane16 == a, v[0], jnp.where(lane16 == b, v[1], g1))
            g4 = jnp.where((lane16 == a) | (lane16 == b), v[2], g4)
            g3 = jnp.where(lane16 == a, v[3], jnp.where(lane16 == b, v[-1], g3))
        dots[0, rs, :] = g1
        dots[1, rs, :] = g3
        dots[2, rs, :] = g4
        return 0

    lax.fori_loop(0, GROUPS // 16, first, 0)
    g1 = dots[0]
    dch = [g1, block_sum(g1, 2) * inv[1], dots[1] * inv[2], dots[2] * inv[3]]
    dmean = sum(c * d for c, d in zip(chance, dch))
    dsc = [c * (d - dmean) - invc * mask * c * (s - mean) for c, d, s in zip(chance, dch, scores)]
    w = dsc[0] + sum(block_sum(dsc[b - 1], b) * inv[b - 1] for b in (2, 3, 4))
    coef[0] = (alpha[0] + block_sum(alpha[1], 2)) * mask
    coef[1] = alpha[2]
    coef[2] = block_sum(alpha[2], 2)
    coef[3] = block_sum(alpha[3], 2)
    coef[4] = w * mask
    coef[5] = mask
    s = sc_ref[...].astype(F32)
    gscore_ref[...] = jnp.zeros_like(gscore_ref)
    dconv[pl.ds(PERIOD * GROUPS, 2304 - PERIOD * GROUPS), :] = jnp.zeros((2304 - PERIOD * GROUPS, 768), BF16)

    def second(ib, _):
        tick("second", ib)
        r0 = pl.multiple_of(ib * 16, 16)
        rs = pl.ds(r0, 16)
        ce, c3, c3p, c4p, cw, mk = [coef[n, rs, :] for n in range(6)]
        for lt in range(6):
            ls = pl.ds(128 * lt, 128)
            d = [dm[at(m, r0), ls] for m in range(6)]
            tri = [c3p[:, 0:1] * d[0] + c3[:, 2:3] * d[1], c3[:, 3:4] * d[1] + c3p[:, 4:5] * d[2],
                   c3p[:, 6:7] * d[3] + c3[:, 8:9] * d[4], c3[:, 9:10] * d[4] + c3p[:, 10:11] * d[5]]
            quad = [c4p[:, 4 * y:4 * y + 1] * d[2 * y] + c4p[:, 4 * y + 2:4 * y + 3] * d[2 * y + 1] for y in range(3)]
            st = s[:, 128 * lt:128 * lt + 128]
            gs = jnp.zeros((16, 128), F32)
            for k in range(PERIOD):
                wk = cw[:, k:k + 1]
                out = ce[:, k:k + 1] * d[k // 2] + mk[:, k:k + 1] * (tri[k // 3] + quad[k // 4]) + wk * st
                gs = gs + wk * conv_ref[at(k, r0), ls].astype(F32)
                dconv[pl.ds(pl.multiple_of(GROUPS * k + r0, 16), 16), ls] = out.astype(BF16)
            gscore_ref[:, ls] += gs[:8] + gs[8:]
        return 0

    lax.fori_loop(0, GROUPS // 16, second, 0)
    vocab = lax.broadcasted_iota(jnp.int32, (256, 2304), 0)
    emb = emb_ref[...].astype(F32)
    for j in range(4):
        tick("taps", j)
        onehot[...] = jnp.where(brow_ref[pl.ds(j, 1), :] == vocab, 1.0, 0.0).astype(BF16)
        g = dot(onehot[...], dconv[...])
        gconv_ref[pl.ds(j, 1), :] = jnp.sum(g * emb, axis=0, keepdims=True)
        part = g * ck_ref[pl.ds(j, 1), :].astype(F32)
        gemb_ref[...] = part if j == 0 else gemb_ref[...] + part


TERMS = {m: (1, 1, 4, 3) if (2 * m) // 3 == (2 * m + 1) // 3 else (1, 1, 4, 3, 3) for m in range(6)}


def terms(m, p, quad, tri):
    a, b = 2 * m, 2 * m + 1
    out = [p[a], p[b], quad[m // 2], tri[a // 3]]
    if a // 3 != b // 3:
        out.append(tri[b // 3])
    return out


def byte_planes(byte_values, length):
    positions = byte_values.shape[0]
    real = jnp.where(jnp.arange(positions) < length, byte_values, -1)
    ext = jnp.pad(real, (1, PERIOD * (GROUPS + 2) - positions - 1), constant_values=-1)
    cols = ext.reshape(GROUPS + 2, PERIOD)
    wide = jnp.concatenate([cols[:GROUPS], cols[1:GROUPS + 1, :4]], axis=1)
    rows = wide.T
    brow = jnp.stack([jnp.pad(rows[j:j + PERIOD].reshape(-1), (0, 2304 - PERIOD * GROUPS), constant_values=-1)
                      for j in range(4)])
    return wide, brow

TOK = 1024
BLK = 256
NEG = -1e30


def rms_parts(x):
    return lax.rsqrt(jnp.mean(x * x, axis=1, keepdims=True) + EPS)


def head_lanes(h2, rows, dtype=BF16):
    lane = lax.broadcasted_iota(jnp.int32, (rows, 128), 1)
    return jnp.where(lane // 64 == h2, 1.0, 0.0).astype(dtype)


def split3(x):
    hi = x.astype(BF16).astype(F32)
    mid = (x - hi).astype(BF16).astype(F32)
    return hi, mid, x - hi - mid


def att_fwd_body(tick, len_ref, start_ref, gain, wq_ref, wk_ref, wv_ref, wo_ref,
                 qs_ref, k_ref, v_ref, ctx_ref, qx_ref, normed_ref, middle_ref,
                 kx, vext, kext, qxf):
    length = len_ref[0, 0]
    g = gain
    tick("project", 0)

    def project(r, _):
        rs = pl.ds(pl.multiple_of(r * BLK, BLK), BLK)
        x = start_ref[rs, :]
        n = (x * rms_parts(x) * g).astype(BF16)
        normed_ref[rs, :] = n
        qs_ref[rs, :] = (dot(n, wq_ref[...]).astype(BF16).astype(F32) * 0.125).astype(BF16)
        k_ref[rs, :] = dot(n, wk_ref[...]).astype(BF16)
        v_ref[rs, :] = dot(n, wv_ref[...]).astype(BF16)
        return 0

    lax.fori_loop(0, TOK // BLK, project, 0)
    lane = lax.broadcasted_iota(jnp.int32, (TOK, 128), 1)
    row = lax.broadcasted_iota(jnp.int32, (TOK, 128), 0)
    keep = 2 * row < length
    kx[...] = jnp.where((lane == 0) & ~keep, NEG, 0.0).astype(BF16)
    ones = jnp.where(keep, 1.0, 0.0).astype(BF16)
    for h2 in range(2):
        vext[h2, :, pl.ds(128, 128)] = ones
        kext[h2, :, pl.ds(128, 128)] = kx[...]
    qxf[...] = jnp.where(lane == 0, 1.0, 0.0).astype(F32)
    lane_b = lax.broadcasted_iota(jnp.int32, (BLK, 128), 1)
    first = jnp.where(lane_b == 0, 1.0, 0.0).astype(BF16)

    def pair(p, _):
        ls = pl.ds(pl.multiple_of(p * 128, 128), 128)
        for h2 in range(2):
            hm = head_lanes(h2, TOK)
            vext[h2, :, pl.ds(0, 128)] = v_ref[:, ls] * hm
            kext[h2, :, pl.ds(0, 128)] = k_ref[:, ls] * hm

        def qblock(r, _):
            tick("att", 4 * p + r)
            rs = pl.ds(pl.multiple_of(r * BLK, BLK), BLK)
            q = jnp.concatenate([qs_ref[rs, ls], first], axis=1)
            out = jnp.zeros((BLK, 128), F32)
            upd = qxf[rs, :]
            for h2 in range(2):
                s = dot(q, kext[h2], ((1,), (1,)))
                m = jnp.max(s, axis=1, keepdims=True)
                e = jnp.exp(s - m).astype(BF16)
                c = dot(e, vext[h2])
                total = c[:, 128:]
                out = out + c[:, :128] * (1.0 / total)
                hi, mid, lo = split3(-(m + jnp.log(total)))
                base = 1 + 3 * (2 * p + h2)
                upd = jnp.where(lane_b == base, hi, jnp.where(lane_b == base + 1, mid,
                                jnp.where(lane_b == base + 2, lo, upd)))
            qxf[rs, :] = upd
            ctx_ref[rs, ls] = out.astype(BF16)
            return 0

        lax.fori_loop(0, TOK // BLK, qblock, 0)
        return 0

    lax.fori_loop(0, HEADS // 2, pair, 0)
    qx_ref[...] = qxf[...].astype(BF16)

    tick("outproj", 0)

    def outproj(r, _):
        rs = pl.ds(pl.multiple_of(r * BLK, BLK), BLK)
        middle_ref[rs, :] = start_ref[rs, :] + dot(ctx_ref[rs, :], wo_ref[...])
        return 0

    lax.fori_loop(0, TOK // BLK, outproj, 0)


def rms_back(x, g, d):
    s = rms_parts(x)
    xn = x * s
    dxn = d * xn
    gg = jnp.sum(dxn.reshape(x.shape[0] // 8, 8, x.shape[1]), axis=0)
    return s * (d * g - xn * jnp.mean(dxn * g, axis=1, keepdims=True)), gg


C0 = 0.7978845608028654
C1 = 0.044715


MESH = pl.DeviceIdType.MESH
HB = pl.BlockSpec(memory_space=pl.ANY)


def bit_of(v, b):
    return (v // (1 << b)) % 2


def flip(v, b):
    return v + (1 - 2 * bit_of(v, b)) * (1 << b)


def with_bits(v, bits, e):
    for i, b in enumerate(bits):
        v = v + (((e >> i) & 1) - bit_of(v, b)) * (1 << b)
    return v


def here():
    return lax.axis_index("wide"), lax.axis_index("narrow")


def greet(wide, direct):
    w, n = here()
    sem = pltpu.get_barrier_semaphore()
    peers = [(lax.rem(w + d, wide), n) for d in range(1, wide)] if direct else [
        (flip(w, b), n) for b in range(wide.bit_length() - 1)]
    peers = peers + [(w, flip(n, 0)), (w, flip(n, 1))]
    for p in peers:
        pl.semaphore_signal(sem, inc=1, device_id=p, device_id_type=MESH)
    pl.semaphore_wait(sem, len(peers))


class Ticker:
    def __init__(self):
        self.todo = {}

    def add(self, name, index, fn):
        self.todo.setdefault((name, index), []).append(fn)

    def __call__(self, name, index):
        for (loop, at), fns in self.todo.items():
            if loop == name:
                if isinstance(index, int):
                    if at == index:
                        for fn in fns:
                            fn()
                else:
                    @pl.when(index == at)
                    def _(fns=fns):
                        for fn in fns:
                            fn()


def wide_order(order, wide):
    bits = wide.bit_length() - 1
    return order if bits == len(order) else tuple(range(bits - 1, -1, -1))


class Gather:
    def __init__(self, index, shard, out, region, order, split, sems):
        self.a, self.shard, self.out = index, shard, out
        self.row, self.nrow, self.col, self.ncol = region
        self.wide = out.shape[0]
        self.order = wide_order(order, self.wide)
        self.split = None
        if split:
            if self.ncol % 512 == 0:
                self.split = "col"
            elif self.nrow % 16 == 0:
                self.split = "row"
        self.send, self.recv, self.local = sems
        self.stages = len(self.order) + (2 if self.split else 1)

    def part(self, ref, quarter=True):
        _, n = here()
        half = self.ncol // 2
        col, ncol = self.col + bit_of(n, 0) * half, half
        row, nrow = self.row, self.nrow
        if self.split == "col" and quarter:
            ncol = half // 2
            col = col + bit_of(n, 1) * ncol
        rs = pl.ds(row, nrow)
        if self.split == "row" and quarter:
            nrow = nrow // 2
            rs = pl.ds(pl.multiple_of(row + bit_of(n, 1) * nrow, 8), nrow)
        lead = (slice(None),) * (len(ref.shape) - 2)
        return ref.at[lead + (rs, pl.ds(pl.multiple_of(col, 128), ncol))]

    def copy(self, src, dst, slot, device):
        return pltpu.make_async_remote_copy(src, dst, self.send.at[self.a, slot], self.recv.at[self.a, slot],
                                            device_id=device, device_id_type=MESH)

    def copies(self, i):
        w, n = here()
        if i < len(self.order):
            dev = (flip(w, self.order[i]), n)
            out = []
            for e in range(1 << i):
                blk = with_bits(w, self.order[:i], e)
                dst = self.part(self.out.at[blk])
                src = self.part(self.shard) if i == 0 else dst
                out.append(self.copy(src, dst, (1 << i) - 1 + e, dev))
            return out
        if self.split and i == len(self.order):
            ref = self.part(self.out)
            return [self.copy(ref, ref, self.wide - 1, (w, flip(n, 1)))]
        ref = self.part(self.out, quarter=False)
        return [self.copy(ref, ref, self.wide, (w, flip(n, 0)))]

    def own(self):
        w, _ = here()
        return pltpu.make_async_copy(self.part(self.shard), self.part(self.out.at[w]), self.local.at[self.a])

    def start(self, i):
        if i == 0:
            self.own().start()
        else:
            self.finish(i - 1)
            if i == 1:
                self.own().wait()
        for c in self.copies(i):
            c.start()

    def finish(self, i):
        for c in self.copies(i):
            c.wait_recv()

    def drain(self):
        for i in range(self.stages):
            for c in self.copies(i):
                c.wait_send()


class Total:
    def __init__(self, acc, slots, send, recv, wide, narrow):
        self.acc, self.slots, self.send, self.recv = acc, slots, send, recv
        self.bits = [("w", b) for b in range(wide.bit_length() - 1)] + [("n", b) for b in range(narrow.bit_length() - 1)]
        self.stages = len(self.bits)

    def copy(self, i):
        w, n = here()
        axis, b = self.bits[i]
        dev = (flip(w, b), n) if axis == "w" else (w, flip(n, b))
        return pltpu.make_async_remote_copy(self.acc.at[i], self.slots.at[i], self.send.at[i], self.recv.at[i],
                                            device_id=dev, device_id_type=MESH)

    def start(self, i):
        if i > 0:
            self.finish(i - 1)
        self.copy(i).start()

    def finish(self, i):
        self.copy(i).wait()
        self.acc[i + 1] = self.acc[i] + self.slots[i]


GATHERS = (
    (0, 0, (2, 0, 1), False),
    (1, 0, (2, 1, 0), True),
    (2, 0, (1, 2, 0), False),
    (3, 0, (0, 2, 1), False),
    (4, 0, (2, 1, 0), False),
    (4, 1, (2, 0, 1), True),
    (5, 0, (2, 0, 1), True),
    (5, 1, (2, 1, 0), True),
    (6, 0, (0, 1, 2), True),
    (6, 1, (2, 0, 1), False),
)
GATHER_PLAN = {
    ("begin", 0): [(2, 0), (1, 0)],
    ("pre", 0): [(0, 0), (8, 0)],
    ("emb", 0): [(2, 1), (1, 1)],
    ("table", 0): [(6, 0), (8, 1)],
    ("plane", 0): [(0, 1)],
    ("plane", 7): [(1, 2)],
    ("rows", 2): [(0, 2)],
    ("rows", 3): [(6, 1)],
    ("rows", 6): [(2, 2)],
    ("rows", 7): [(5, 0), (8, 2)],
    ("rows", 9): [(1, 3)],
    ("project", 0): [(5, 1), (7, 0), (6, 2), (8, 3)],
    ("att", 0): [(5, 2), (7, 1), (4, 0)],
    ("att", 2): [(9, 0), (6, 3)],
    ("att", 4): [(3, 0), (8, 4)],
    ("att", 7): [(3, 1), (7, 2), (4, 1)],
    ("att", 8): [(9, 1)],
    ("att", 9): [(5, 3)],
    ("att", 10): [(6, 4)],
    ("att", 13): [(3, 2)],
    ("att", 14): [(7, 3), (4, 2)],
    ("att", 15): [(9, 2)],
    ("att", 17): [(5, 4)],
    ("att", 21): [(3, 3)],
    ("att", 22): [(7, 4), (4, 3)],
    ("outproj", 0): [(9, 3)],
}


def chunk_region(weight, chunk, rows, cols):
    if weight < 4:
        return (0, rows, 0, cols)
    if weight < 6:
        return (0, rows, chunk * (cols // 2), cols // 2)
    return (chunk * (rows // 2), rows // 2, 0, cols)


def front_body(wide, narrow, len_ref, bcol_ref, emb_ref, small_ref,
               sq, sk, sv, so, sg, su, sd,
               oq, ok, ov, oo, og, ou, od,
               start_ref, conv_ref, csum_ref, tot_ref, smallall_ref, emball_ref,
               qs_ref, k_ref, v_ref, ctx_ref, qx_ref, normed_ref, middle_ref,
               table, onehot, planes, coef, tiles, ent, kx, vext, kext, qxf, vq, vk, vv, vo,
               embs, smalls, tacc, tslots,
               gsend, grecv, glocal, psend, precv, tsend, trecv, wsem):
    w, n = here()
    embs[w] = emb_ref[...]
    smalls[w] = small_ref[...]
    greet(wide, True)
    shards, outs = (sq, sk, sv, so, sg, su, sd), (oq, ok, ov, oo, og, ou, od)
    gathers = [Gather(i, shards[a], outs[a], chunk_region(a, c, *shards[a].shape), order, split, (gsend, grecv, glocal))
               for i, (a, c, order, split) in enumerate(GATHERS)]
    tick = Ticker()
    started = [0] * len(gathers)

    half = emb_ref.shape[1] // 2
    hcols = pl.ds(pl.multiple_of(bit_of(n, 0) * half, 128), half)
    small_copies, emb_copies = [], []
    for d in range(1, wide):
        peer = (lax.rem(w + d, wide), n)
        emb_copies.append(pltpu.make_async_remote_copy(
            emb_ref.at[:, hcols], embs.at[w, :, hcols], psend.at[0, d], precv.at[0, d], device_id=peer, device_id_type=MESH))
        small_copies.append(pltpu.make_async_remote_copy(
            small_ref, smalls.at[w], psend.at[1, d], precv.at[1, d], device_id=peer, device_id_type=MESH))
    for c in emb_copies + small_copies:
        c.start()
    swap = pltpu.make_async_remote_copy(embs.at[:, :, hcols], embs.at[:, :, hcols], psend.at[0, 0], precv.at[0, 0],
                                        device_id=(w, flip(n, 0)), device_id_type=MESH)

    def params():
        tick("pre", 0)
        for c in emb_copies:
            c.wait_recv()
        swap.start()
        tick("emb", 0)
        for c in small_copies:
            c.wait_recv()
        per = 768 // wide
        l = lax.broadcasted_iota(jnp.int32, (128, 768), 0)
        c = lax.broadcasted_iota(jnp.int32, (128, 768), 1)
        small = sum(dot(smalls[i].astype(BF16), jnp.where((c == per * i + l) & (l < per), 1.0, 0.0).astype(BF16))
                    for i in range(wide))
        smallall_ref[...] = small
        swap.wait()
        emb = embs[...].astype(F32).reshape(256, 768)
        emball_ref[...] = emb.astype(BF16)
        return emb, small

    for (loop, at), stages in GATHER_PLAN.items():
        for g, s in stages:
            if s < gathers[g].stages:
                tick.add(loop, at, functools.partial(gathers[g].start, s))
                started[g] = s + 1
    weights = list(zip((0, 1, 2), outs[:3], (vq, vk, vv)))

    def load(ws, sem0):
        copies = []
        for j, (_, src, dst) in enumerate(ws):
            r = src.shape[1]
            for i in range(wide):
                copies.append(pltpu.make_async_copy(src.at[i], dst.at[pl.ds(r * i, r)], wsem.at[sem0 + j, i]))
        return copies

    def ready(ids):
        for g in ids:
            for s in range(started[g], gathers[g].stages):
                gathers[g].start(s)
            gathers[g].finish(gathers[g].stages - 1)

    def qkv_ready():
        ready((0, 1, 2))
        cs = load(weights, 0)
        for c in cs:
            c.start()
        for c in cs:
            c.wait()

    tick.add("project", 0, qkv_ready)
    total = Total(tacc, tslots, tsend, trecv, wide, narrow)

    def total_begin():
        lane = lax.broadcasted_iota(jnp.int32, (8, 128), 1)
        tacc[0] = jnp.where(lane == 0, len_ref[0, 0].astype(F32), jnp.where(lane == 1, ent[...], 0.0))
        total.start(0)

    tick.add("att", 1, total_begin)
    for i in range(1, total.stages):
        tick.add("att", 1 + 2 * i, functools.partial(total.start, i))

    def out_ready():
        total.finish(total.stages - 1)
        tot_ref[...] = tacc[total.stages]
        ready((3,))
        cs = load([(3, outs[3], vo)], 3)
        for c in cs:
            c.start()
        for c in cs:
            c.wait()

    tick.add("outproj", 0, out_ready)
    tick("begin", 0)
    gbst_fwd_body(tick, params, len_ref, bcol_ref, start_ref, conv_ref, csum_ref, ent, table, onehot, planes, coef, tiles)
    att_fwd_body(tick, len_ref, start_ref, smallall_ref[pl.ds(5, 1), :], vq, vk, vv, vo,
                 qs_ref, k_ref, v_ref, ctx_ref, qx_ref, normed_ref, middle_ref, kx, vext, kext, qxf)
    ready(range(4, len(gathers)))
    for c in emb_copies + small_copies:
        c.wait_send()
    for g in gathers:
        g.drain()


def front(wide, narrow, length, bcol, emb, small, shards):
    b = jax.ShapeDtypeStruct((TOK, 768), BF16)
    f = jax.ShapeDtypeStruct((TOK, 768), F32)
    gathered = tuple(jax.ShapeDtypeStruct((wide,) + s.shape, s.dtype) for s in shards)
    sq = pltpu.VMEM((768, 768), BF16)
    ng = len(GATHERS)
    dma = pltpu.SemaphoreType.DMA
    stages = (wide * narrow).bit_length() - 1
    return pl.pallas_call(
        functools.partial(front_body, wide, narrow),
        out_shape=gathered + (
            f, jax.ShapeDtypeStruct((PERIOD, GROUPS, 768), BF16), jax.ShapeDtypeStruct((GROUPS, 128), F32),
            jax.ShapeDtypeStruct((8, 128), F32), jax.ShapeDtypeStruct((8, 768), F32), jax.ShapeDtypeStruct((256, 768), BF16),
            b, b, b, b, jax.ShapeDtypeStruct((TOK, 128), BF16), b, f),
        in_specs=[SM] + [VM] * 10,
        out_specs=(HB,) * 7 + (VM,) * 13,
        scratch_shapes=[
            pltpu.VMEM((1024, 768), BF16), pltpu.VMEM((GROUPS, 256 * 15), BF16), pltpu.VMEM((PERIOD, GROUPS, 768), F32),
            pltpu.VMEM((4, GROUPS, 128), F32), pltpu.VMEM((6, 6 * GROUPS, 128), F32), pltpu.VMEM((8, 128), F32),
            pltpu.VMEM((TOK, 128), BF16), pltpu.VMEM((2, TOK, 256), BF16), pltpu.VMEM((2, TOK, 256), BF16),
            pltpu.VMEM((TOK, 128), F32), sq, sq, sq, sq,
            pltpu.VMEM((wide,) + emb.shape, BF16), pltpu.VMEM((wide, 8, 128), F32),
            pltpu.VMEM((stages + 1, 8, 128), F32), pltpu.VMEM((stages, 8, 128), F32),
            dma((ng, wide + 1)), dma((ng, wide + 1)), dma((ng,)), dma((2, wide)), dma((2, wide)), dma((stages,)), dma((stages,)),
            dma((4, wide))],
        compiler_params=pltpu.CompilerParams(vmem_limit_bytes=60 << 20, collective_id=0, has_side_effects=True),
        name="front",
    )(length, bcol, emb, small, *shards)


class Scatter:
    def __init__(self, index, data, out, region, order, early, bufs, sems, base=(0, 0)):
        self.a, self.data, self.out = index, data, out
        self.row, self.nrow, self.col, self.ncol = region
        self.wide = data.shape[0]
        self.order = wide_order(order, self.wide)
        self.nb = len(self.order)
        self.early = early_split(early, region)
        self.cb, self.wb, self.yb, self.fs, self.fb = bufs
        self.send, self.recv = sems
        self.base_row, self.base_col = base
        self.kinds = ["core"] + (["early"] if self.early else []) + [("wide", i) for i in range(self.nb)]
        self.kinds += ["join" if self.early else "late", "swap"]
        self.stages = len(self.kinds)

    def share(self, other=False):
        _, n = here()
        half = self.ncol // 2
        b0 = bit_of(n, 0)
        b0 = 1 - b0 if other else b0
        return pl.ds(self.row, self.nrow), pl.ds(pl.multiple_of(self.col + b0 * half, 128), half)

    def quarter(self, other=False, base=True):
        _, n = here()
        half = self.ncol // 2
        b1 = bit_of(n, 1)
        b1 = 1 - b1 if other else b1
        row, nrow, ncol = (self.row if base else 0), self.nrow, half
        col = self.col + bit_of(n, 0) * half if base else 0
        if self.early == "col":
            ncol = half // 2
            col = pl.multiple_of(col + b1 * ncol, 128)
        elif self.early == "row":
            nrow = nrow // 2
            row = pl.multiple_of(row + b1 * nrow, 8)
        if base:
            col = pl.multiple_of(col, 128)
        return pl.ds(row, nrow), pl.ds(col, ncol)

    def mine(self):
        return self.quarter() if self.early else self.share()

    def copy(self, src, dst, slot, device):
        return pltpu.make_async_remote_copy(src, dst, self.send.at[self.a, slot], self.recv.at[self.a, slot],
                                            device_id=device, device_id_type=MESH)

    def base(self, i):
        return sum(1 << (self.nb - 1 - j) for j in range(i))

    def copies(self, s):
        w, n = here()
        kind = self.kinds[s]
        W = self.wide
        if kind == "core":
            r, c = self.share(other=True)
            return [self.copy(self.data.at[:, r, c], self.cb, W - 1, (w, flip(n, 0)))]
        if kind == "early":
            r, c = self.quarter(other=True)
            return [self.copy(self.data.at[:, r, c], self.yb, W, (w, flip(n, 1)))]
        r, c = self.mine()
        if kind == "late":
            return [self.copy(self.data.at[w, r, c], self.yb, W, (w, flip(n, 1)))]
        if kind == "join":
            ref = self.fs.at[self.quarter(base=False)]
            return [self.copy(ref, ref, W + 1, (w, flip(n, 1)))]
        if kind == "swap":
            return [self.copy(self.fs, self.fb, W + 2, (w, flip(n, 0)))]
        i = kind[1]
        peer = flip(w, self.order[i])
        out = []
        for e in range(1 << (self.nb - 1 - i)):
            blk = with_bits(peer, self.order[i + 1:], e)
            out.append(self.copy(self.data.at[blk, r, c], self.wb.at[self.base(i) + e], self.base(i) + e, (peer, n)))
        return out

    def add(self, blk, where, term):
        idx = (blk,) + where
        self.data[idx] = (self.data[idx].astype(F32) + term.astype(F32)).astype(BF16)

    def combine(self, s):
        w, n = here()
        for c in self.copies(s):
            c.wait_recv()
        kind = self.kinds[s]
        if kind in ("core", "early"):
            where = self.share() if kind == "core" else self.quarter()
            if kind == "core" and self.early:
                pass
            buf = self.cb if kind == "core" else self.yb

            def block(b, _):
                self.add(b, where, buf[b])
                return 0

            lax.fori_loop(0, self.wide, block, 0)
        elif kind == "late":
            self.fs[...] = (self.data[(w,) + self.mine()].astype(F32) + self.yb[...].astype(F32)).astype(BF16)
        elif kind == "swap":
            b0, half = bit_of(n, 0), self.ncol // 2
            rows = pl.ds(self.row - self.base_row, self.nrow)
            for b, ref in ((b0, self.fs), (1 - b0, self.fb)):
                self.out[rows, pl.ds(pl.multiple_of(self.col - self.base_col + b * half, 128), half)] = ref[...]
        elif kind != "join":
            i = kind[1]
            for e in range(1 << (self.nb - 1 - i)):
                self.add(with_bits(w, self.order[i + 1:], e), self.mine(), self.wb[self.base(i) + e])
            if i == self.nb - 1 and self.early:
                self.fs[self.quarter(base=False)] = self.data[(w,) + self.mine()]

    def start(self, s):
        if s > 0:
            self.combine(s - 1)
        for c in self.copies(s):
            c.start()

    def finish(self):
        self.combine(self.stages - 1)

    def drain(self):
        for s in range(self.stages):
            for c in self.copies(s):
                c.wait_send()


def early_split(early, region):
    if not early:
        return None
    if region[3] % 512 == 0:
        return "col"
    return "row" if region[1] % 32 == 0 else None


def scatter_buffers(wide, region, early):
    _, nrow, _, ncol = region
    half = ncol // 2
    kind = early_split(early, region)
    qr, qc = (nrow // 2, half) if kind == "row" else (nrow, half // 2) if kind == "col" else (nrow, half)
    y = (wide, qr, qc) if kind else (nrow, half)
    return [pltpu.VMEM((wide, nrow, half), BF16), pltpu.VMEM((wide - 1, qr, qc), BF16), pltpu.VMEM(y, BF16),
            pltpu.VMEM((nrow, half), BF16), pltpu.VMEM((nrow, half), BF16)]


SCATTERS = (
    (0, 0, (2, 1, 0), True),
    (0, 1, (1, 0, 2), True),
    (1, 0, (1, 0, 2), False),
    (1, 1, (1, 2, 0), False),
    (2, 0, (0, 1, 2), False),
    (2, 1, (0, 1, 2), False),
    (3, 0, (0, 1, 2), False),
    (4, 0, (0, 1, 2), False),
    (5, 0, (2, 1, 0), False),
    (6, 0, (1, 0, 2), False),
)
SCATTER_PLAN = {
    ("ffn", 16): [(2, 0), (0, 0)],
    ("ffn", 21): [(2, 1), (0, 1)],
    ("ffn", 31): [(2, 2), (0, 2)],
    ("fin", 0): [(3, 0), (1, 0), (5, 0), (4, 0)],
    ("gout", 0): [(2, 3), (6, 0)],
    ("head", 2): [(0, 3), (3, 1), (1, 1), (5, 1), (4, 1)],
    ("head", 3): [(6, 1)],
    ("bwd", 1): [(2, 4)],
    ("bwd", 3): [(0, 4)],
    ("bwd", 6): [(2, 5), (1, 2)],
    ("bwd", 7): [(3, 2)],
    ("bwd", 8): [(2, 6), (0, 5)],
    ("bwd", 11): [(0, 6)],
    ("bwd", 12): [(1, 3)],
    ("bwd", 13): [(0, 7), (6, 2)],
    ("bwd", 14): [(3, 3), (5, 2), (4, 2)],
    ("bwd", 16): [(1, 4)],
    ("bwd", 18): [(3, 4)],
    ("bwd", 19): [(6, 3)],
    ("bwd", 20): [(1, 5)],
    ("bwd", 22): [(3, 5)],
    ("bwd", 23): [(1, 6), (5, 3), (4, 3)],
    ("free", 0): [(3, 6), (6, 4)],
    ("wgrad", 1): [(1, 7)],
    ("last", 0): [(9, 0), (7, 0), (8, 0)],
    ("last", 1): [(6, 5)],
    ("last", 3): [(6, 6)],
    ("first", 0): [(9, 1), (7, 1), (5, 4), (4, 4), (8, 1)],
    ("second", 3): [(5, 5), (4, 5)],
    ("second", 8): [(7, 2)],
    ("second", 9): [(5, 6), (4, 6)],
}
PADROWS = 6 * GROUPS


def scatter_place(weight, chunk, wide):
    per = 768 // wide
    if weight < 2:
        return (0, per, chunk * 1024, 1024), (0, 0)
    if weight == 2:
        rows = 2048 // wide
        return (chunk * (rows // 2), rows // 2, 0, 768), (0, 0)
    if weight == 5:
        return (0, per, 768, 768), (0, 768)
    return (0, per, 0, 768), (0, 0)


def rest_body(wide, *refs):
    (len_ref, invc_ref, small_ref, brow_ref, emb_ref, csum_ref, qx_ref, middle_h, cot_h, start_h, qs_h, k_h, v_h, ctx_h,
     normed_h, conv_h, wg_h, wu_h, wd_h, wq_h, wk_h, wv_h, wo_h), refs = refs[:23], refs[23:]
    (out_h, *shard, gembs, smalls), refs = refs[:10], refs[10:]
    (f0, f1, f2, tiles, x1, x2, x3, n2t, onehot, dx, qcat, ocat, dqt, gg, gu, gd, go,
     gemb, gconv, gscore, gg1, gg2, dots, coef, lsem, wsem,
     cb, esend, eb, ysend, yb, fs, fb, sall, sb, ssum, yss), refs = refs[:37], refs[37:]
    bufs, (ssend, srecv, dsend, drecv) = refs[:-4], refs[-4:]
    w, n = here()
    greet(wide, True)
    tick = Ticker()
    datas = (gg, gu, gd, go, gg, gg, gu)
    scatters = []
    for i, (a, c, order, early) in enumerate(SCATTERS):
        region, base = scatter_place(a, c, wide)
        scatters.append(Scatter(i, datas[a], shard[a], region, order, early, bufs[5 * i:5 * i + 5], (ssend, srecv), base))
    started = [0] * len(scatters)
    for (loop, at), stages in SCATTER_PLAN.items():
        for g, s in stages:
            if s == scatters[g].stages:
                tick.add(loop, at, scatters[g].finish)
                started[g] = s + 1
            elif s < scatters[g].stages:
                tick.add(loop, at, functools.partial(scatters[g].start, s))
                started[g] = s + 1

    def complete(ids):
        for s in range(16):
            for g in ids:
                sc = scatters[g]
                if started[g] <= s < sc.stages:
                    sc.start(s)
                elif s == sc.stages and started[g] <= s:
                    sc.finish()
                    started[g] = 99

    def local(src, dst, i):
        return pltpu.make_async_copy(src, dst, lsem.at[i])

    top_rows, low_rows = pl.ds(0, TOK), pl.ds(TOK, TOK)

    g2 = small_ref[pl.ds(6, 1), :]
    n2, top = x1.at[top_rows], x1.at[low_rows]
    hdd = x2.at[top_rows]
    per = 768 // wide
    ntile = wd_h.shape[0] // BLK

    def weight_tiles(f, slot):
        fs_ = pl.ds(pl.multiple_of(f * BLK, BLK), BLK)
        return [pltpu.make_async_copy(wg_h.at[:, fs_], x3.at[pl.ds(768 * slot, 768), pl.ds(0, BLK)], wsem.at[slot, 0]),
                pltpu.make_async_copy(wu_h.at[:, fs_], x3.at[pl.ds(768 * slot, 768), pl.ds(BLK, BLK)], wsem.at[slot, 1]),
                pltpu.make_async_copy(wd_h.at[fs_, :], x2.at[pl.ds(TOK + BLK * slot, BLK), :], wsem.at[slot, 2])]

    loads = [local(middle_h, f0.at[top_rows], 0), local(cot_h, f1.at[top_rows], 1)]
    for c in loads:
        c.start()
    for c in weight_tiles(0, 0):
        c.start()
    for c in loads:
        c.wait()

    def prep(r, _):
        rs = pl.ds(pl.multiple_of(r * BLK, BLK), BLK)
        x = f0[rs, :]
        nn = x * rms_parts(x) * g2
        n2[rs, :] = nn.astype(BF16)
        n2t[:, rs] = nn.T.astype(BF16)
        top[rs, :] = f1[rs, :].astype(BF16)
        for lt in range(6):
            tiles[lt, rs, :] = x[:, 128 * lt:128 * lt + 128]
        f2[rs, :] = jnp.zeros((BLK, 768), F32)
        return 0

    lax.fori_loop(0, TOK // BLK, prep, 0)
    tick("prep", 0)

    def ffn_tile(f, slot):
        for c in weight_tiles(f, slot):
            c.wait()

        @pl.when(f + 1 < ntile)
        def _():
            for c in weight_tiles(f + 1, 1 - slot):
                c.start()

        wg = x3.at[pl.ds(768 * slot, 768), pl.ds(0, BLK)]
        wu = x3.at[pl.ds(768 * slot, 768), pl.ds(BLK, BLK)]
        wd = x2.at[pl.ds(TOK + BLK * slot, BLK), :]

        def rows(r, _):
            tick("ffn", 4 * f + r)
            rs = pl.ds(pl.multiple_of(r * BLK, BLK), BLK)
            nn = n2[rs, :]
            v = dot(nn, wg[...])
            u = dot(nn, wu[...])
            dh = dot(top[rs, :], wd[...], ((1,), (1,)))
            v2 = v * v
            t = jnp.tanh(v * (C0 + (C0 * C1) * v2))
            hp = 0.5 + 0.5 * t
            gelu = v * hp
            slope = hp + (0.5 * v) * (1.0 - t * t) * (C0 + (3.0 * C0 * C1) * v2)
            h = (gelu * u).astype(BF16)
            a = (dh * u * slope).astype(BF16)
            b = (dh * gelu).astype(BF16)
            hdd[rs, pl.ds(0, BLK)] = h
            hdd[rs, pl.ds(BLK, BLK)] = a
            hdd[rs, pl.ds(2 * BLK, BLK)] = b
            o = dot(h, wd[...])
            for lt in range(6):
                tiles[lt, rs, :] += o[:, 128 * lt:128 * lt + 128]
            f2[rs, :] += dot(a, wg[...], ((1,), (1,))) + dot(b, wu[...], ((1,), (1,)))
            return 0

        lax.fori_loop(0, TOK // BLK, rows, 0)
        cols = pl.ds(pl.multiple_of(f * BLK, BLK), BLK)
        for j, ref in ((1, gg), (2, gu)):
            res = dot(n2t[...], hdd[:, pl.ds(j * BLK, BLK)])
            for i in range(wide):
                ref[i, :, cols] = res[per * i:per * i + per].astype(BF16)
        res = dot(hdd[:, pl.ds(0, BLK)], top[...], ((0,), (0,)))
        high = 2048 // wide
        for i in range(BLK // high):
            gd[f * (BLK // high) + i] = res[high * i:high * i + high].astype(BF16)

    def tile_pair(i, _):
        ffn_tile(2 * i, 0)
        ffn_tile(2 * i + 1, 1)
        return 0

    lax.fori_loop(0, ntile // 2, tile_pair, 0)
    q, k, v, ctx, normed, low = [x.at[r] for x in (x1, x2, x3) for r in (top_rows, low_rows)]
    loads = [local(h, d, i) for i, (h, d) in enumerate(
        ((qs_h, q), (k_h, k), (v_h, v), (ctx_h, ctx), (normed_h, normed), (wo_h, n2t.at[:, pl.ds(0, 768)])))]
    for c in loads:
        c.start()
    stores = [local(tiles.at[lt, top_rows, :], out_h.at[:, pl.ds(128 * lt, 128)], 8 + lt) for lt in range(6)]
    for c in stores:
        c.start()
    tick("fin", 0)
    gg2[...] = jnp.zeros_like(gg2)

    def fin(r, _):
        rs = pl.ds(pl.multiple_of(r * BLK, BLK), BLK)
        dxv, part = rms_back(f0[rs, :], g2, f2[rs, :])
        f1[rs, :] += dxv
        gg2[...] += part
        return 0

    lax.fori_loop(0, TOK // BLK, fin, 0)
    start_load = local(start_h, f0.at[top_rows], 6)
    start_load.start()
    for c in loads:
        c.wait()

    wo = n2t.at[:, pl.ds(0, 768)]
    length = len_ref[0, 0]

    def lower(r, _):
        rs = pl.ds(pl.multiple_of(r * BLK, BLK), BLK)
        low[rs, :] = f1[rs, :].astype(BF16)
        return 0

    lax.fori_loop(0, TOK // BLK, lower, 0)
    whole = dot(ctx[...], low[...], ((0,), (0,))).astype(BF16)
    for c in range(wide):
        go[c] = whole[per * c:per * c + per]
    tick("gout", 0)
    lane_s = lax.broadcasted_iota(jnp.int32, (768, 128), 1)
    row_s = lax.broadcasted_iota(jnp.int32, (768, 128), 0)
    sel = jnp.where(lane_s // 3 == row_s // 64, 1.0, 0.0).astype(BF16)
    lane_b = lax.broadcasted_iota(jnp.int32, (BLK, 128), 1)
    row_b = lax.broadcasted_iota(jnp.int32, (BLK, 128), 0)

    def head(r, _):
        tick("head", r)
        rs = pl.ds(pl.multiple_of(r * BLK, BLK), BLK)
        d = dot(low[rs, :], wo[...], ((1,), (1,))).astype(BF16)
        prod = d.astype(F32) * ctx[rs, :].astype(F32)
        ctx[rs, :] = d
        hi = prod.astype(BF16)
        delta = dot(hi, sel) + dot((prod - hi.astype(F32)).astype(BF16), sel)
        a, b, c = split3(-delta)
        dx[rs, :] = jnp.where(lane_b % 3 == 0, a, jnp.where(lane_b % 3 == 1, b, c)).astype(BF16)
        return 0

    lax.fori_loop(0, TOK // BLK, head, 0)
    late_loads = [local(wk_h, x3.at[pl.ds(TOK, 768)], 0), local(wv_h, n2t.at[:, pl.ds(0, 768)], 1)]
    for c in late_loads:
        c.start()
    qcat[:, pl.ds(128, 128)] = qx_ref[...]
    ocat[:, pl.ds(128, 128)] = dx[...]

    def pair(p, _):
        ls = pl.ds(pl.multiple_of(p * 128, 128), 128)
        qcat[:, pl.ds(0, 128)] = q[:, ls]
        ocat[:, pl.ds(0, 128)] = ctx[:, ls]
        dqt[...] = jnp.zeros_like(dqt)

        def kblock(r, _):
            tick("bwd", 4 * p + r)
            rs = pl.ds(pl.multiple_of(r * BLK, BLK), BLK)
            bias = jnp.where((lane_b == 0) & (2 * (row_b + r * BLK) >= length), NEG, 0.0)
            dvb = jnp.zeros((BLK, 128), F32)
            dkb = jnp.zeros((BLK, 128), F32)
            dqb = dqt[...]
            for h2 in range(2):
                hm = head_lanes(h2, BLK)
                hd = 3 * (2 * p + h2)
                km = k[rs, ls] * hm
                vm = v[rs, ls] * hm
                kxl = jnp.where((lane_b > hd) & (lane_b <= hd + 3), 1.0, bias).astype(BF16)
                vxl = jnp.where((lane_b >= hd) & (lane_b < hd + 3), 1.0, 0.0).astype(BF16)
                st = dot(jnp.concatenate([km, kxl], axis=1), qcat[...], ((1,), (1,)))
                dp = dot(jnp.concatenate([vm, vxl], axis=1), ocat[...], ((1,), (1,)))
                prob = jnp.exp(st)
                dsc = (prob * dp).astype(BF16)
                dvb = dvb + dot(prob.astype(BF16), ocat[:, pl.ds(0, 128)]) * hm.astype(F32)
                dkb = dkb + dot(dsc, qcat[:, pl.ds(0, 128)]) * hm.astype(F32)
                dqb = dqb + dot(km, dsc, ((0,), (0,)))
            v[rs, ls] = dvb.astype(BF16)
            k[rs, ls] = dkb.astype(BF16)
            dqt[...] = dqb
            return 0

        lax.fori_loop(0, TOK // BLK, kblock, 0)
        q[:, ls] = (dqt[...].T * 0.125).astype(BF16)
        return 0

    lax.fori_loop(0, HEADS // 2, pair, 0)
    wq_load = local(wq_h, x2.at[pl.ds(TOK, 768)], 2)
    wq_load.start()
    tick("free", 0)
    complete(range(4))
    for g in range(4):
        scatters[g].drain()

    def wgrad(c, _):
        tick("wgrad", c)
        cs = pl.ds(pl.multiple_of(c * BLK, BLK), BLK)
        for src, ref, base in ((q, gg, 0), (k, gg, 768), (v, gu, 0)):
            res = dot(normed[...], src[:, cs], ((0,), (0,))).astype(BF16)
            for i in range(wide):
                ref[i, :, pl.ds(pl.multiple_of(base + c * BLK, BLK), BLK)] = res[per * i:per * i + per]
        return 0

    lax.fori_loop(0, 3, wgrad, 0)
    start_load.wait()
    for c in late_loads + [wq_load]:
        c.wait()
    for c in stores:
        c.wait()
    gg1[...] = jnp.zeros_like(gg1)
    g1 = small_ref[pl.ds(5, 1), :]
    wq, wk, wv = x2.at[pl.ds(TOK, 768)], x3.at[pl.ds(TOK, 768)], n2t.at[:, pl.ds(0, 768)]

    def last(r, _):
        tick("last", r)
        rs = pl.ds(pl.multiple_of(r * BLK, BLK), BLK)
        d = (dot(q[rs, :], wq[...], ((1,), (1,))) + dot(k[rs, :], wk[...], ((1,), (1,)))
             + dot(v[rs, :], wv[...], ((1,), (1,))))
        dxv, part = rms_back(f0[rs, :], g1, d)
        res = f1[rs, :] + dxv
        for lt in range(6):
            tiles[lt, rs, :] = res[:, 128 * lt:128 * lt + 128]
        gg1[...] += part
        return 0

    lax.fori_loop(0, TOK // BLK, last, 0)
    conv = x3.at[pl.ds(0, PERIOD * GROUPS)]
    conv_load = local(conv_h, conv, 7)
    conv_load.start()
    for lt in range(6):
        tiles[lt, pl.ds(TOK, PADROWS - TOK), :] = jnp.zeros((PADROWS - TOK, 128), F32)
    conv_load.wait()

    gbst_bwd_body(tick, len_ref, invc_ref, brow_ref, emb_ref, small_ref.at[pl.ds(0, 4)], small_ref.at[pl.ds(4, 1)],
                  conv, csum_ref, gemb, gconv, gscore, f2, dots, coef, x1, onehot, tiles)

    def copy(src, dst, kk, slot, device):
        return pltpu.make_async_remote_copy(src, dst, dsend.at[kk, slot], drecv.at[kk, slot],
                                            device_id=device, device_id_type=MESH)

    half = 384
    gc = lambda b: pl.ds(pl.multiple_of(b * half, 128), half)
    b0 = bit_of(n, 0)
    esend[...] = gemb[:, gc(1 - b0)].astype(BF16).reshape(esend.shape)
    core = copy(esend, cb, 0, 0, (w, flip(n, 0)))
    core.start()
    r8 = lax.broadcasted_iota(jnp.int32, (8, 768), 0)
    total = gconv[...] * jnp.where(r8 < 4, 1.0, 0.0)
    for row, ref in ((4, gscore), (5, gg1), (6, gg2)):
        total = jnp.where(r8 == row, jnp.sum(ref[...], axis=0, keepdims=True), total)
    rl = lax.broadcasted_iota(jnp.int32, (768, 128), 0)
    cl = lax.broadcasted_iota(jnp.int32, (768, 128), 1)
    for i in range(wide):
        sall[i] = dot(total, jnp.where((rl == per * i + cl) & (cl < per), 1.0, 0.0).astype(F32), precision=HIGH)
    peers = [(lax.rem(w + d, wide), n) for d in range(1, wide)]
    small_copies = [copy(sall.at[p[0]], sb.at[w], 1, d + 1, p) for d, p in enumerate(peers)]
    for c in small_copies:
        c.start()
    core.wait()
    esend[...] = (gemb[:, gc(b0)].reshape(esend.shape) + cb[...].astype(F32)).astype(BF16)
    emb_copies = [copy(esend.at[p[0]], eb.at[w], 2, d + 1, p) for d, p in enumerate(peers)]
    for c in emb_copies:
        c.start()
    sb[w] = sall[w]
    eb[w] = esend[w]
    complete(range(4, len(scatters)))
    for c in small_copies + emb_copies:
        c.wait_recv()
    ysend[...] = sum(eb[i].astype(F32) for i in range(wide))
    ssum[0] = sum(sb[i] for i in range(wide))
    late = [copy(ysend, yb, 3, 0, (w, flip(n, 1))), copy(ssum.at[0], yss.at[0], 3, 1, (w, flip(n, 1)))]
    for c in late:
        c.start()
    for c in late:
        c.wait_recv()
    fs[...] = (ysend[...] + yb[...]).astype(BF16)
    ssum[1] = ssum[0] + yss[0]
    swap = [copy(fs, fb, 4, 0, (w, flip(n, 0))), copy(ssum.at[1], yss.at[1], 4, 1, (w, flip(n, 0)))]
    for c in swap:
        c.start()
    for c in swap:
        c.wait_recv()
    gembs[:, gc(b0)] = fs[...]
    gembs[:, gc(1 - b0)] = fb[...]
    smalls[...] = ssum[1] + yss[1]
    for c in small_copies + emb_copies + late + swap:
        c.wait_send()
    for g in range(4, len(scatters)):
        scatters[g].drain()


def rest(wide, args):
    rows, per, high = 256 // wide, 768 // wide, 2048 // wide
    bufs = []
    for a, c, _, early in SCATTERS:
        bufs += scatter_buffers(wide, scatter_place(a, c, wide)[0], early)
    v = pltpu.VMEM
    dma = pltpu.SemaphoreType.DMA
    ns = len(SCATTERS)
    shape = lambda *s: jax.ShapeDtypeStruct(s, BF16)
    return pl.pallas_call(
        functools.partial(rest_body, wide),
        out_shape=(jax.ShapeDtypeStruct((TOK, 768), F32), shape(per, 2048), shape(per, 2048), shape(high, 768),
                   shape(per, 768), shape(per, 768), shape(per, 768), shape(per, 768), shape(rows, 768),
                   jax.ShapeDtypeStruct((8, 128), F32)),
        in_specs=[SM, SM] + [VM] * 5 + [HB] * 16,
        out_specs=(HB,) + (VM,) * 9,
        scratch_shapes=[
            v((PADROWS, 768), F32), v((TOK, 768), F32), v((PADROWS, 768), F32), v((6, PADROWS, 128), F32),
            v((2304, 768), BF16), v((2 * TOK, 768), BF16), v((2112, 768), BF16), v((768, TOK), BF16), v((256, 2304), BF16),
            v((TOK, 128), BF16), v((TOK, 256), BF16), v((TOK, 256), BF16), v((128, TOK), F32),
            v((wide, per, 2048), BF16), v((wide, per, 2048), BF16), v((wide, high, 768), BF16), v((wide, per, 768), BF16),
            v((256, 768), F32), v((8, 768), F32), v((8, 768), F32), v((8, 768), F32), v((8, 768), F32),
            v((3, GROUPS, 128), F32), v((6, GROUPS, 128), F32), dma((16,)), dma((2, 3)),
            v((wide, rows, 384), BF16), v((wide, rows, 384), BF16), v((wide, rows, 384), BF16), v((rows, 384), F32),
            v((rows, 384), F32), v((rows, 384), BF16), v((rows, 384), BF16), v((wide, 8, 128), F32), v((wide, 8, 128), F32),
            v((2, 8, 128), F32), v((2, 8, 128), F32)]
        + bufs + [dma((ns, wide + 3)), dma((ns, wide + 3)), dma((5, wide)), dma((5, wide))],
        compiler_params=pltpu.CompilerParams(vmem_limit_bytes=64 << 20, collective_id=1, has_side_effects=True),
        name="rest",
    )(*args)


def finish_body(wide, out_ref, *refs):
    shard, (gembs, smalls, tot), refs = refs[:7], refs[7:10], refs[10:]
    (res, ent, emb, conv, score, g1, g2), outs = refs[:7], refs[7:14]
    per = 768 // wide
    res[...] = out_ref[...]
    for src, dst in zip(shard, outs):
        dst[...] = src[...].astype(F32)
    emb[...] = gembs[...].astype(F32)
    ent[0, 0] = tot[0, 1] / tot[0, 0]
    conv[...] = smalls[pl.ds(0, 4), pl.ds(0, per)]
    score[...] = smalls[pl.ds(4, 1), pl.ds(0, per)]
    g1[...] = smalls[pl.ds(5, 1), pl.ds(0, per)]
    g2[...] = smalls[pl.ds(6, 1), pl.ds(0, per)]


def finish(wide, out, shards, gembs, smalls, tot):
    rows, per = 256 // wide, 768 // wide
    f = lambda *s: jax.ShapeDtypeStruct(s, F32)
    return pl.pallas_call(
        functools.partial(finish_body, wide),
        out_shape=(f(TOK, 768), f(1, 1), f(rows, 768), f(4, per), f(1, per), f(1, per), f(1, per))
        + tuple(f(*s.shape) for s in shards),
        in_specs=[VM] * 10 + [SM],
        out_specs=(VM, SM) + (VM,) * 12,
        compiler_params=pltpu.CompilerParams(vmem_limit_bytes=60 << 20),
        name="finish",
    )(out, *shards, gembs, smalls, tot)


def body(
    wide, narrow,
    byte_values, row_lengths, embedding, conv_kernel, score_vector, attn_gain, query_weight, key_weight,
    value_weight, output_weight, ffn_gain, gate_weight, up_weight, down_weight, cotangent,
):
    length = row_lengths.reshape(1, 1)
    bcol, brow = byte_planes(byte_values[0], row_lengths[0])
    small = jnp.concatenate([conv_kernel, score_vector[None], attn_gain[None], ffn_gain[None]], axis=0).astype(F32)
    small = jnp.pad(small, ((0, 8 - small.shape[0]), (0, 128 - small.shape[1])))
    shards = (query_weight, key_weight, value_weight, output_weight, gate_weight, up_weight, down_weight)
    got = front(wide, narrow, length, bcol, embedding, small, shards)
    wq, wk, wv, wo, wg, wu, wd = [x.reshape(-1, x.shape[-1]) for x in got[:7]]
    start, conv, csum, tot, smallall, emb, qs, k, v, ctx, qx, normed, middle = got[7:]
    invc = (ENT_WEIGHT / tot[0, 0]).reshape(1, 1)
    out, *rest_out = rest(wide, (length, invc, smallall, brow, emb, csum, qx, middle, cotangent[0], start, qs, k, v, ctx,
                                 normed, conv.reshape(PERIOD * GROUPS, 768), wg, wu, wd, wq, wk, wv, wo))
    shard, (gembs, smalls) = rest_out[:7], rest_out[7:]
    res, ent, ge, gc, gs, gg1, gg2, sg, su, sd, so, sq, sk, sv = finish(wide, out, shard, gembs, smalls, tot)
    flat = lambda x: x.reshape(-1)
    return (res[None], ent.reshape(()), ge, gc, flat(gs), flat(gg1), sq, sk, sv, so, flat(gg2), sg, su, sd)


def solution(mesh):
    both = ("wide", "narrow")
    row, flat = P("wide", None), P("wide")
    return jax.shard_map(
        functools.partial(body, mesh.shape["wide"], mesh.shape["narrow"]),
        mesh=mesh,
        in_specs=(P(both, None), P(both), row, P(None, "wide"), flat, flat, row, row, row, row, flat,
                  row, row, row, P(both, None, None)),
        out_specs=(P(both, None, None), P(), row, P(None, "wide"), flat, flat, row, row, row, row, flat,
                   row, row, row),
        check_vma=False,
    )
```

```python
import functools
import jax
import jax.numpy as jnp
from jax import lax
from jax.experimental import pallas as pl
from jax.experimental.pallas import tpu as pltpu
from jax.sharding import PartitionSpec as P

F32 = jnp.float32
BF16 = jnp.bfloat16
EPS = 1e-06
HEADS = 12
ENT_WEIGHT = 1.0
PERIOD = 12
GROUPS = 176
HIGH = lax.Precision.HIGHEST
VM = pl.BlockSpec(memory_space=pltpu.VMEM)
SM = pl.BlockSpec(memory_space=pltpu.SMEM)


def dot(a, b, dims=((1,), (0,)), precision=None):
    return lax.dot_general(a, b, (dims, ((), ())), precision=precision, preferred_element_type=F32)


def same_block(size):
    r = lax.broadcasted_iota(jnp.int32, (128, 128), 0)
    c = lax.broadcasted_iota(jnp.int32, (128, 128), 1)
    return jnp.where((r // size == c // size) & (r < PERIOD) & (c < PERIOD), 1.0, 0.0).astype(F32)


def block_sum(x, size):
    return dot(x, same_block(size), precision=HIGH)


def lane_scalars(csum, length):
    i = lax.broadcasted_iota(jnp.int32, (GROUPS, 128), 0)
    k = lax.broadcasted_iota(jnp.int32, (GROUPS, 128), 1)
    mask = jnp.where((PERIOD * i + k < length) & (k < PERIOD), 1.0, 0.0).astype(F32)
    tok = block_sum(jnp.where(k % 2 == 0, mask, 0.0), 2)
    inv = [jnp.ones_like(mask)] + [1.0 / jnp.maximum(block_sum(mask, b), 1.0) for b in (2, 3, 4)]
    scores = [csum] + [block_sum(csum, b) * inv[b - 1] for b in (2, 3, 4)]
    top = functools.reduce(jnp.maximum, scores)
    ex = [jnp.exp(s - top) for s in scores]
    total = ex[0] + ex[1] + ex[2] + ex[3]
    rec = 1.0 / total
    chance = [e * rec for e in ex]
    mean = sum(c * s for c, s in zip(chance, scores))
    ent = mask * (top + jnp.log(total) - mean)
    alpha = [c * v for c, v in zip(chance, inv)]
    return mask, tok, inv, scores, chance, mean, ent, alpha


def gbst_fwd_body(tick, params, len_ref, bcol_ref, start_ref, conv_ref, csum_ref, ent_ref,
                  table, onehot, planes, coef, tiles):
    length = len_ref[0, 0]
    vocab = lax.broadcasted_iota(jnp.int32, (GROUPS, 256), 1)
    for k in range(PERIOD + 3):
        onehot[:, pl.ds(256 * k, 256)] = jnp.where(bcol_ref[:, k:k + 1] == vocab, 1.0, 0.0).astype(BF16)
    csum_ref[...] = jnp.zeros_like(csum_ref)
    tick("onehot", 0)
    emb, small = params()
    for j in range(4):
        table[pl.ds(256 * j, 256), :] = (emb * small[j:j + 1]).astype(BF16)
    s = small[4:5]
    tick("table", 0)
    rows = lax.broadcasted_iota(jnp.int32, (GROUPS, 1), 0)
    lane = lax.broadcasted_iota(jnp.int32, (GROUPS, 128), 1)

    def plane(k, _):
        tick("plane", k)
        lhs = onehot[:, pl.ds(pl.multiple_of(256 * k, 256), 1024)]
        out = dot(lhs, table[...])
        out = jnp.where(PERIOD * rows + k < length, out, 0.0)
        planes[k] = out
        conv_ref[k] = out.astype(BF16)
        c = jnp.sum(out * s, axis=1, keepdims=True)
        csum_ref[...] = jnp.where(lane == k, c, csum_ref[...])
        return 0

    lax.fori_loop(0, PERIOD, plane, 0)
    mask, tok, inv, scores, chance, mean, ent, alpha = lane_scalars(csum_ref[...], length)
    ent_ref[...] = jnp.sum(jnp.sum(ent, axis=0, keepdims=True), axis=1, keepdims=True) + jnp.zeros((8, 128), F32)
    half = 0.5 * tok
    coef[0] = (alpha[0] + block_sum(alpha[1], 2)) * half
    coef[1] = alpha[2] * half
    coef[2] = block_sum(alpha[2], 2) * half
    coef[3] = block_sum(alpha[3], 2) * half

    def rowblock(ib, _):
        tick("rows", ib)
        r0 = pl.multiple_of(ib * 16, 16)
        rs = pl.ds(r0, 16)
        ce, c3, c3p, c4p = [coef[n, rs, :] for n in range(4)]
        for lt in range(6):
            ls = pl.ds(128 * lt, 128)
            p = [planes[k, rs, ls] for k in range(PERIOD)]
            pair = [p[2 * m] + p[2 * m + 1] for m in range(6)]
            quad = [pair[2 * y] + pair[2 * y + 1] for y in range(3)]
            tri = [p[3 * x] + p[3 * x + 1] + p[3 * x + 2] for x in range(4)]
            for m in range(6):
                a, b = 2 * m, 2 * m + 1
                out = ce[:, a:a + 1] * p[a] + ce[:, b:b + 1] * p[b] + c4p[:, a:a + 1] * quad[m // 2]
                if a // 3 == b // 3:
                    out = out + c3p[:, a:a + 1] * tri[a // 3]
                else:
                    out = out + c3[:, a:a + 1] * tri[a // 3] + c3[:, b:b + 1] * tri[b // 3]
                tiles[lt, pl.ds(6 * r0 + m, 16, stride=6), :] = out
        return 0

    lax.fori_loop(0, GROUPS // 16, rowblock, 0)
    for lt in range(6):
        start_ref[:, pl.ds(128 * lt, 128)] = tiles[lt, pl.ds(0, start_ref.shape[0]), :]


def gbst_bwd_body(tick, len_ref, invc_ref, brow_ref, emb_ref, ck_ref, sc_ref, conv_ref, csum_ref,
                  gemb_ref, gconv_ref, gscore_ref, dm, dots, coef, dconv, onehot, tiles):
    length = len_ref[0, 0]
    at = lambda k, r0: pl.ds(pl.multiple_of(GROUPS * k + r0, 16), 16)
    invc = invc_ref[0, 0]
    mask, tok, inv, scores, chance, mean, ent, alpha = lane_scalars(csum_ref[...], length)
    half = 0.5 * tok
    coef[0] = half
    lane16 = lax.broadcasted_iota(jnp.int32, (16, 128), 1)

    def first(ib, _):
        tick("first", ib)
        r0 = pl.multiple_of(ib * 16, 16)
        rs = pl.ds(r0, 16)
        h = coef[0, rs, :]
        acc = [jnp.zeros((16, 128), F32) for _ in range(26)]
        for lt in range(6):
            ls = pl.ds(128 * lt, 128)
            p = [conv_ref[at(k, r0), ls].astype(F32) for k in range(PERIOD)]
            quad = [(p[4 * y] + p[4 * y + 1]) + (p[4 * y + 2] + p[4 * y + 3]) for y in range(3)]
            tri = [p[3 * x] + p[3 * x + 1] + p[3 * x + 2] for x in range(4)]
            n = 0
            for m in range(6):
                d = tiles[lt, pl.ds(6 * r0 + m, 16, stride=6), :] * h[:, 2 * m:2 * m + 1]
                dm[at(m, r0), ls] = d
                for q in terms(m, p, quad, tri):
                    acc[n] = acc[n] + d * q
                    n += 1
        g1 = jnp.zeros((16, 128), F32)
        g3 = jnp.zeros((16, 128), F32)
        g4 = jnp.zeros((16, 128), F32)
        n = 0
        for m in range(6):
            a, b = 2 * m, 2 * m + 1
            v = [jnp.sum(acc[n + q], axis=1, keepdims=True) for q in range(len(TERMS[m]))]
            n += len(TERMS[m])
            g1 = jnp.where(lane16 == a, v[0], jnp.where(lane16 == b, v[1], g1))
            g4 = jnp.where((lane16 == a) | (lane16 == b), v[2], g4)
            g3 = jnp.where(lane16 == a, v[3], jnp.where(lane16 == b, v[-1], g3))
        dots[0, rs, :] = g1
        dots[1, rs, :] = g3
        dots[2, rs, :] = g4
        return 0

    lax.fori_loop(0, GROUPS // 16, first, 0)
    g1 = dots[0]
    dch = [g1, block_sum(g1, 2) * inv[1], dots[1] * inv[2], dots[2] * inv[3]]
    dmean = sum(c * d for c, d in zip(chance, dch))
    dsc = [c * (d - dmean) - invc * mask * c * (s - mean) for c, d, s in zip(chance, dch, scores)]
    w = dsc[0] + sum(block_sum(dsc[b - 1], b) * inv[b - 1] for b in (2, 3, 4))
    coef[0] = (alpha[0] + block_sum(alpha[1], 2)) * mask
    coef[1] = alpha[2]
    coef[2] = block_sum(alpha[2], 2)
    coef[3] = block_sum(alpha[3], 2)
    coef[4] = w * mask
    coef[5] = mask
    s = sc_ref[...].astype(F32)
    gscore_ref[...] = jnp.zeros_like(gscore_ref)
    dconv[pl.ds(PERIOD * GROUPS, 2304 - PERIOD * GROUPS), :] = jnp.zeros((2304 - PERIOD * GROUPS, 768), BF16)

    def second(ib, _):
        tick("second", ib)
        r0 = pl.multiple_of(ib * 16, 16)
        rs = pl.ds(r0, 16)
        ce, c3, c3p, c4p, cw, mk = [coef[n, rs, :] for n in range(6)]
        for lt in range(6):
            ls = pl.ds(128 * lt, 128)
            d = [dm[at(m, r0), ls] for m in range(6)]
            tri = [c3p[:, 0:1] * d[0] + c3[:, 2:3] * d[1], c3[:, 3:4] * d[1] + c3p[:, 4:5] * d[2],
                   c3p[:, 6:7] * d[3] + c3[:, 8:9] * d[4], c3[:, 9:10] * d[4] + c3p[:, 10:11] * d[5]]
            quad = [c4p[:, 4 * y:4 * y + 1] * d[2 * y] + c4p[:, 4 * y + 2:4 * y + 3] * d[2 * y + 1] for y in range(3)]
            st = s[:, 128 * lt:128 * lt + 128]
            gs = jnp.zeros((16, 128), F32)
            for k in range(PERIOD):
                wk = cw[:, k:k + 1]
                out = ce[:, k:k + 1] * d[k // 2] + mk[:, k:k + 1] * (tri[k // 3] + quad[k // 4]) + wk * st
                gs = gs + wk * conv_ref[at(k, r0), ls].astype(F32)
                dconv[pl.ds(pl.multiple_of(GROUPS * k + r0, 16), 16), ls] = out.astype(BF16)
            gscore_ref[:, ls] += gs[:8] + gs[8:]
        return 0

    lax.fori_loop(0, GROUPS // 16, second, 0)
    vocab = lax.broadcasted_iota(jnp.int32, (256, 768), 0)
    emb = emb_ref[...].astype(F32)
    for j in range(4):
        tick("taps", j)
        g = jnp.zeros((256, 768), F32)
        for p in range(3):
            onehot[pl.ds(256 * p, 256), :] = jnp.where(brow_ref[pl.ds(j, 1), pl.ds(768 * p, 768)] == vocab, 1.0, 0.0).astype(BF16)
            g = g + dot(onehot[pl.ds(256 * p, 256), :], dconv[pl.ds(768 * p, 768), :])
        gconv_ref[pl.ds(j, 1), :] = jnp.sum(g * emb, axis=0, keepdims=True)
        part = g * ck_ref[pl.ds(j, 1), :].astype(F32)
        gemb_ref[...] = part if j == 0 else gemb_ref[...] + part


class Planes:
    def __init__(self, ref, col):
        self.ref, self.cols = ref, pl.ds(col, 128)

    def where(self, key):
        if isinstance(key, tuple):
            return pl.ds(pl.multiple_of(GROUPS * key[0] + key[1].start, 16), key[1].size), self.cols
        return pl.ds(GROUPS * key, GROUPS), self.cols

    def __getitem__(self, key):
        return self.ref[self.where(key)]

    def __setitem__(self, key, value):
        self.ref[self.where(key)] = value


TERMS = {m: (1, 1, 4, 3) if (2 * m) // 3 == (2 * m + 1) // 3 else (1, 1, 4, 3, 3) for m in range(6)}


def terms(m, p, quad, tri):
    a, b = 2 * m, 2 * m + 1
    out = [p[a], p[b], quad[m // 2], tri[a // 3]]
    if a // 3 != b // 3:
        out.append(tri[b // 3])
    return out


def byte_planes(byte_values, length):
    positions = byte_values.shape[0]
    real = jnp.where(jnp.arange(positions) < length, byte_values, -1)
    ext = jnp.pad(real, (1, PERIOD * (GROUPS + 2) - positions - 1), constant_values=-1)
    cols = ext.reshape(GROUPS + 2, PERIOD)
    wide = jnp.concatenate([cols[:GROUPS], cols[1:GROUPS + 1, :4]], axis=1)
    rows = wide.T
    brow = jnp.stack([jnp.pad(rows[j:j + PERIOD].reshape(-1), (0, 2304 - PERIOD * GROUPS), constant_values=-1)
                      for j in range(4)])
    return wide, brow

TOK = 1024
BLK = 256
NEG = -1e30


def rms_parts(x):
    return lax.rsqrt(jnp.mean(x * x, axis=1, keepdims=True) + EPS)


def head_lanes(h2, rows, dtype=BF16):
    lane = lax.broadcasted_iota(jnp.int32, (rows, 128), 1)
    return jnp.where(lane // 64 == h2, 1.0, 0.0).astype(dtype)


def split3(x):
    hi = x.astype(BF16).astype(F32)
    mid = (x - hi).astype(BF16).astype(F32)
    return hi, mid, x - hi - mid


def att_fwd_body(tick, len_ref, start_ref, gain, wq_ref, wk_ref, wv_ref, wo_ref,
                 qs_ref, k_ref, v_ref, ctx_ref, qx_ref, normed_ref, middle_ref,
                 kx, vext, kext, qxf):
    length = len_ref[0, 0]
    g = gain
    tick("project", 0)

    def project(r, _):
        rs = pl.ds(pl.multiple_of(r * BLK, BLK), BLK)
        x = start_ref[rs, :]
        n = (x * rms_parts(x) * g).astype(BF16)
        normed_ref[rs, :] = n
        qs_ref[rs, :] = (dot(n, wq_ref[...]).astype(BF16).astype(F32) * 0.125).astype(BF16)
        k_ref[rs, :] = dot(n, wk_ref[...]).astype(BF16)
        v_ref[rs, :] = dot(n, wv_ref[...]).astype(BF16)
        return 0

    lax.fori_loop(0, TOK // BLK, project, 0)
    lane = lax.broadcasted_iota(jnp.int32, (TOK, 128), 1)
    row = lax.broadcasted_iota(jnp.int32, (TOK, 128), 0)
    keep = 2 * row < length
    kx[...] = jnp.where((lane == 0) & ~keep, NEG, 0.0).astype(BF16)
    ones = jnp.where(keep, 1.0, 0.0).astype(BF16)
    for h2 in range(2):
        vext[h2, :, pl.ds(128, 128)] = ones
        kext[h2, :, pl.ds(128, 128)] = kx[...]
    qxf[...] = jnp.where(lane == 0, 1.0, 0.0).astype(F32)
    lane_b = lax.broadcasted_iota(jnp.int32, (BLK, 128), 1)
    first = jnp.where(lane_b == 0, 1.0, 0.0).astype(BF16)

    def pair(p, _):
        ls = pl.ds(pl.multiple_of(p * 128, 128), 128)
        for h2 in range(2):
            hm = head_lanes(h2, TOK)
            vext[h2, :, pl.ds(0, 128)] = v_ref[:, ls] * hm
            kext[h2, :, pl.ds(0, 128)] = k_ref[:, ls] * hm

        def qblock(r, _):
            tick("att", 4 * p + r)
            rs = pl.ds(pl.multiple_of(r * BLK, BLK), BLK)
            q = jnp.concatenate([qs_ref[rs, ls], first], axis=1)
            out = jnp.zeros((BLK, 128), F32)
            upd = qxf[rs, :]
            for h2 in range(2):
                s = dot(q, kext[h2], ((1,), (1,)))
                m = jnp.max(s, axis=1, keepdims=True)
                e = jnp.exp(s - m).astype(BF16)
                c = dot(e, vext[h2])
                total = c[:, 128:]
                out = out + c[:, :128] * (1.0 / total)
                hi, mid, lo = split3(-(m + jnp.log(total)))
                base = 1 + 3 * (2 * p + h2)
                upd = jnp.where(lane_b == base, hi, jnp.where(lane_b == base + 1, mid,
                                jnp.where(lane_b == base + 2, lo, upd)))
            qxf[rs, :] = upd
            ctx_ref[rs, ls] = out.astype(BF16)
            return 0

        lax.fori_loop(0, TOK // BLK, qblock, 0)
        return 0

    lax.fori_loop(0, HEADS // 2, pair, 0)
    qx_ref[...] = qxf[...].astype(BF16)

    tick("outproj", 0)

    def outproj(r, _):
        rs = pl.ds(pl.multiple_of(r * BLK, BLK), BLK)
        middle_ref[rs, :] = start_ref[rs, :] + dot(ctx_ref[rs, :], wo_ref[...])
        return 0

    lax.fori_loop(0, TOK // BLK, outproj, 0)


def rms_back(x, g, d):
    s = rms_parts(x)
    xn = x * s
    dxn = d * xn
    gg = jnp.sum(dxn.reshape(x.shape[0] // 8, 8, x.shape[1]), axis=0)
    return s * (d * g - xn * jnp.mean(dxn * g, axis=1, keepdims=True)), gg


C0 = 0.7978845608028654
C1 = 0.044715


MESH = pl.DeviceIdType.MESH
HB = pl.BlockSpec(memory_space=pl.ANY)


def bit_of(v, b):
    return (v // (1 << b)) % 2


def flip(v, b):
    return v + (1 - 2 * bit_of(v, b)) * (1 << b)


def with_bits(v, bits, e):
    for i, b in enumerate(bits):
        v = v + (((e >> i) & 1) - bit_of(v, b)) * (1 << b)
    return v


def here():
    return lax.axis_index("wide"), lax.axis_index("narrow")


def greet(wide, direct):
    w, n = here()
    sem = pltpu.get_barrier_semaphore()
    peers = [(lax.rem(w + d, wide), n) for d in range(1, wide)] if direct else [
        (flip(w, b), n) for b in range(wide.bit_length() - 1)]
    peers = peers + [(w, flip(n, 0)), (w, flip(n, 1))]
    for p in peers:
        pl.semaphore_signal(sem, inc=1, device_id=p, device_id_type=MESH)
    pl.semaphore_wait(sem, len(peers))


class Ticker:
    def __init__(self):
        self.todo = {}

    def add(self, name, index, fn):
        self.todo.setdefault((name, index), []).append(fn)

    def __call__(self, name, index):
        for (loop, at), fns in self.todo.items():
            if loop == name:
                if isinstance(index, int):
                    if at == index:
                        for fn in fns:
                            fn()
                else:
                    @pl.when(index == at)
                    def _(fns=fns):
                        for fn in fns:
                            fn()


def wide_order(order, wide):
    bits = wide.bit_length() - 1
    return order if bits == len(order) else tuple(range(bits - 1, -1, -1))


class Gather:
    def __init__(self, index, shard, out, region, order, split, sems):
        self.a, self.shard, self.out = index, shard, out
        self.row, self.nrow, self.col, self.ncol = region
        self.wide = out.shape[0]
        self.order = wide_order(order, self.wide)
        self.split = None
        if split:
            if self.ncol % 512 == 0:
                self.split = "col"
            elif self.nrow % 16 == 0:
                self.split = "row"
        self.send, self.recv, self.local = sems
        self.stages = len(self.order) + (2 if self.split else 1)

    def part(self, ref, quarter=True):
        _, n = here()
        half = self.ncol // 2
        col, ncol = self.col + bit_of(n, 0) * half, half
        row, nrow = self.row, self.nrow
        if self.split == "col" and quarter:
            ncol = half // 2
            col = col + bit_of(n, 1) * ncol
        rs = pl.ds(row, nrow)
        if self.split == "row" and quarter:
            nrow = nrow // 2
            rs = pl.ds(pl.multiple_of(row + bit_of(n, 1) * nrow, 8), nrow)
        lead = (slice(None),) * (len(ref.shape) - 2)
        return ref.at[lead + (rs, pl.ds(pl.multiple_of(col, 128), ncol))]

    def copy(self, src, dst, slot, device):
        return pltpu.make_async_remote_copy(src, dst, self.send.at[self.a, slot], self.recv.at[self.a, slot],
                                            device_id=device, device_id_type=MESH)

    def copies(self, i):
        w, n = here()
        if i < len(self.order):
            dev = (flip(w, self.order[i]), n)
            out = []
            for e in range(1 << i):
                blk = with_bits(w, self.order[:i], e)
                dst = self.part(self.out.at[blk])
                src = self.part(self.shard) if i == 0 else dst
                out.append(self.copy(src, dst, (1 << i) - 1 + e, dev))
            return out
        if self.split and i == len(self.order):
            ref = self.part(self.out)
            return [self.copy(ref, ref, self.wide - 1, (w, flip(n, 1)))]
        ref = self.part(self.out, quarter=False)
        return [self.copy(ref, ref, self.wide, (w, flip(n, 0)))]

    def own(self):
        w, _ = here()
        return pltpu.make_async_copy(self.part(self.shard), self.part(self.out.at[w]), self.local.at[self.a])

    def start(self, i):
        if i == 0:
            self.own().start()
        else:
            self.finish(i - 1)
            if i == 1:
                self.own().wait()
        for c in self.copies(i):
            c.start()

    def finish(self, i):
        for c in self.copies(i):
            c.wait_recv()

    def drain(self):
        for i in range(self.stages):
            for c in self.copies(i):
                c.wait_send()


class Total:
    def __init__(self, acc, slots, send, recv, wide, narrow):
        self.acc, self.slots, self.send, self.recv = acc, slots, send, recv
        self.bits = [("w", b) for b in range(wide.bit_length() - 1)] + [("n", b) for b in range(narrow.bit_length() - 1)]
        self.stages = len(self.bits)

    def copy(self, i):
        w, n = here()
        axis, b = self.bits[i]
        dev = (flip(w, b), n) if axis == "w" else (w, flip(n, b))
        return pltpu.make_async_remote_copy(self.acc.at[i], self.slots.at[i], self.send.at[i], self.recv.at[i],
                                            device_id=dev, device_id_type=MESH)

    def start(self, i):
        if i > 0:
            self.finish(i - 1)
        self.copy(i).start()

    def finish(self, i):
        self.copy(i).wait()
        self.acc[i + 1] = self.acc[i] + self.slots[i]


GATHERS = (
    (0, 0, (2, 0, 1), False),
    (1, 0, (2, 1, 0), True),
    (2, 0, (1, 2, 0), False),
    (3, 0, (0, 2, 1), False),
    (4, 0, (2, 1, 0), False),
    (4, 1, (2, 0, 1), True),
    (5, 0, (2, 0, 1), True),
    (5, 1, (2, 1, 0), True),
    (6, 0, (0, 1, 2), True),
    (6, 1, (2, 0, 1), False),
)
GATHER_PLAN = {
    ("begin", 0): [(2, 0), (1, 0)],
    ("pre", 0): [(0, 0), (8, 0)],
    ("emb", 0): [(2, 1), (1, 1)],
    ("table", 0): [(6, 0), (8, 1)],
    ("plane", 0): [(0, 1)],
    ("plane", 7): [(1, 2)],
    ("rows", 2): [(0, 2)],
    ("rows", 3): [(6, 1)],
    ("rows", 6): [(2, 2)],
    ("rows", 7): [(5, 0), (8, 2)],
    ("rows", 9): [(1, 3)],
    ("project", 0): [(5, 1), (7, 0), (6, 2), (8, 3)],
    ("att", 0): [(5, 2), (7, 1), (4, 0)],
    ("att", 2): [(9, 0), (6, 3)],
    ("att", 4): [(3, 0), (8, 4)],
    ("att", 7): [(3, 1), (7, 2), (4, 1)],
    ("att", 8): [(9, 1)],
    ("att", 9): [(5, 3)],
    ("att", 10): [(6, 4)],
    ("att", 13): [(3, 2)],
    ("att", 14): [(7, 3), (4, 2)],
    ("att", 15): [(9, 2)],
    ("att", 17): [(5, 4)],
    ("att", 21): [(3, 3)],
    ("att", 22): [(7, 4), (4, 3)],
    ("outproj", 0): [(9, 3)],
}


def chunk_region(weight, chunk, rows, cols):
    if weight < 4:
        return (0, rows, 0, cols)
    if weight < 6:
        return (0, rows, chunk * (cols // 2), cols // 2)
    return (chunk * (rows // 2), rows // 2, 0, cols)


def front_body(wide, narrow, len_ref, bcol_ref, emb_ref, small_ref,
               sq, sk, sv, so, sg, su, sd,
               oq, ok, ov, oo, og, ou, od,
               start_ref, conv_ref, csum_ref, tot_ref, smallall_ref, emball_ref,
               qs_ref, k_ref, v_ref, ctx_ref, qx_ref, normed_ref, middle_ref,
               table, onehot, planes, coef, tiles, ent, kx, vext, kext, qxf, vq, vk, vv, vo,
               embs, smalls, tacc, tslots,
               gsend, grecv, glocal, psend, precv, tsend, trecv, wsem):
    w, n = here()
    embs[w] = emb_ref[...]
    smalls[w] = small_ref[...]
    greet(wide, True)
    shards, outs = (sq, sk, sv, so, sg, su, sd), (oq, ok, ov, oo, og, ou, od)
    gathers = [Gather(i, shards[a], outs[a], chunk_region(a, c, *shards[a].shape), order, split, (gsend, grecv, glocal))
               for i, (a, c, order, split) in enumerate(GATHERS)]
    tick = Ticker()
    started = [0] * len(gathers)

    half = emb_ref.shape[1] // 2
    hcols = pl.ds(pl.multiple_of(bit_of(n, 0) * half, 128), half)
    small_copies, emb_copies = [], []
    for d in range(1, wide):
        peer = (lax.rem(w + d, wide), n)
        emb_copies.append(pltpu.make_async_remote_copy(
            emb_ref.at[:, hcols], embs.at[w, :, hcols], psend.at[0, d], precv.at[0, d], device_id=peer, device_id_type=MESH))
        small_copies.append(pltpu.make_async_remote_copy(
            small_ref, smalls.at[w], psend.at[1, d], precv.at[1, d], device_id=peer, device_id_type=MESH))
    for c in emb_copies + small_copies:
        c.start()
    swap = pltpu.make_async_remote_copy(embs.at[:, :, hcols], embs.at[:, :, hcols], psend.at[0, 0], precv.at[0, 0],
                                        device_id=(w, flip(n, 0)), device_id_type=MESH)

    def params():
        tick("pre", 0)
        for c in emb_copies:
            c.wait_recv()
        swap.start()
        tick("emb", 0)
        for c in small_copies:
            c.wait_recv()
        per = 768 // wide
        l = lax.broadcasted_iota(jnp.int32, (128, 768), 0)
        c = lax.broadcasted_iota(jnp.int32, (128, 768), 1)
        small = sum(dot(smalls[i].astype(BF16), jnp.where((c == per * i + l) & (l < per), 1.0, 0.0).astype(BF16))
                    for i in range(wide))
        smallall_ref[...] = small
        swap.wait()
        emb = embs[...].astype(F32).reshape(256, 768)
        emball_ref[...] = emb.astype(BF16)
        return emb, small

    for (loop, at), stages in GATHER_PLAN.items():
        for g, s in stages:
            if s < gathers[g].stages:
                tick.add(loop, at, functools.partial(gathers[g].start, s))
                started[g] = s + 1
    weights = list(zip((0, 1, 2), outs[:3], (vq, vk, vv)))

    def load(ws, sem0):
        copies = []
        for j, (_, src, dst) in enumerate(ws):
            r = src.shape[1]
            for i in range(wide):
                copies.append(pltpu.make_async_copy(src.at[i], dst.at[pl.ds(r * i, r)], wsem.at[sem0 + j, i]))
        return copies

    def ready(ids):
        for g in ids:
            for s in range(started[g], gathers[g].stages):
                gathers[g].start(s)
            gathers[g].finish(gathers[g].stages - 1)

    def qkv_ready():
        ready((0, 1, 2))
        cs = load(weights, 0)
        for c in cs:
            c.start()
        for c in cs:
            c.wait()

    tick.add("project", 0, qkv_ready)
    total = Total(tacc, tslots, tsend, trecv, wide, narrow)

    def total_begin():
        lane = lax.broadcasted_iota(jnp.int32, (8, 128), 1)
        tacc[0] = jnp.where(lane == 0, len_ref[0, 0].astype(F32), jnp.where(lane == 1, ent[...], 0.0))
        total.start(0)

    tick.add("att", 1, total_begin)
    for i in range(1, total.stages):
        tick.add("att", 1 + 2 * i, functools.partial(total.start, i))

    def out_ready():
        total.finish(total.stages - 1)
        tot_ref[...] = tacc[total.stages]
        ready((3,))
        cs = load([(3, outs[3], vo)], 3)
        for c in cs:
            c.start()
        for c in cs:
            c.wait()

    tick.add("outproj", 0, out_ready)
    tick("begin", 0)
    gbst_fwd_body(tick, params, len_ref, bcol_ref, start_ref, conv_ref, csum_ref, ent, table, onehot, planes, coef, tiles)
    att_fwd_body(tick, len_ref, start_ref, smallall_ref[pl.ds(5, 1), :], vq, vk, vv, vo,
                 qs_ref, k_ref, v_ref, ctx_ref, qx_ref, normed_ref, middle_ref, kx, vext, kext, qxf)
    ready(range(4, len(gathers)))
    for c in emb_copies + small_copies:
        c.wait_send()
    for g in gathers:
        g.drain()


def front(wide, narrow, length, bcol, emb, small, shards):
    b = jax.ShapeDtypeStruct((TOK, 768), BF16)
    f = jax.ShapeDtypeStruct((TOK, 768), F32)
    gathered = tuple(jax.ShapeDtypeStruct((wide,) + s.shape, s.dtype) for s in shards)
    sq = pltpu.VMEM((768, 768), BF16)
    ng = len(GATHERS)
    dma = pltpu.SemaphoreType.DMA
    stages = (wide * narrow).bit_length() - 1
    return pl.pallas_call(
        functools.partial(front_body, wide, narrow),
        out_shape=gathered + (
            f, jax.ShapeDtypeStruct((PERIOD, GROUPS, 768), BF16), jax.ShapeDtypeStruct((GROUPS, 128), F32),
            jax.ShapeDtypeStruct((8, 128), F32), jax.ShapeDtypeStruct((8, 768), F32), jax.ShapeDtypeStruct((256, 768), BF16),
            b, b, b, b, jax.ShapeDtypeStruct((TOK, 128), BF16), b, f),
        in_specs=[SM] + [VM] * 10,
        out_specs=(HB,) * 7 + (VM,) * 13,
        scratch_shapes=[
            pltpu.VMEM((1024, 768), BF16), pltpu.VMEM((GROUPS, 256 * 15), BF16), pltpu.VMEM((PERIOD, GROUPS, 768), F32),
            pltpu.VMEM((4, GROUPS, 128), F32), pltpu.VMEM((6, 6 * GROUPS, 128), F32), pltpu.VMEM((8, 128), F32),
            pltpu.VMEM((TOK, 128), BF16), pltpu.VMEM((2, TOK, 256), BF16), pltpu.VMEM((2, TOK, 256), BF16),
            pltpu.VMEM((TOK, 128), F32), sq, sq, sq, sq,
            pltpu.VMEM((wide,) + emb.shape, BF16), pltpu.VMEM((wide, 8, 128), F32),
            pltpu.VMEM((stages + 1, 8, 128), F32), pltpu.VMEM((stages, 8, 128), F32),
            dma((ng, wide + 1)), dma((ng, wide + 1)), dma((ng,)), dma((2, wide)), dma((2, wide)), dma((stages,)), dma((stages,)),
            dma((4, wide))],
        compiler_params=pltpu.CompilerParams(vmem_limit_bytes=60 << 20, collective_id=0, has_side_effects=True),
        name="front",
    )(length, bcol, emb, small, *shards)


class Scatter:
    def __init__(self, index, data, out, region, order, early, bufs, sems, base=(0, 0)):
        self.a, self.data, self.out = index, data, out
        self.row, self.nrow, self.col, self.ncol = region
        self.wide = data.shape[0]
        self.order = wide_order(order, self.wide)
        self.nb = len(self.order)
        self.early = early_split(early, region)
        self.cb, self.wb, self.yb, self.fs, self.fb = bufs
        self.send, self.recv = sems
        self.base_row, self.base_col = base
        self.kinds = ["core"] + (["early"] if self.early else []) + [("wide", i) for i in range(self.nb)]
        self.kinds += ["join" if self.early else "late", "swap"]
        self.stages = len(self.kinds)

    def share(self, other=False):
        _, n = here()
        half = self.ncol // 2
        b0 = bit_of(n, 0)
        b0 = 1 - b0 if other else b0
        return pl.ds(self.row, self.nrow), pl.ds(pl.multiple_of(self.col + b0 * half, 128), half)

    def quarter(self, other=False, base=True):
        _, n = here()
        half = self.ncol // 2
        b1 = bit_of(n, 1)
        b1 = 1 - b1 if other else b1
        row, nrow, ncol = (self.row if base else 0), self.nrow, half
        col = self.col + bit_of(n, 0) * half if base else 0
        if self.early == "col":
            ncol = half // 2
            col = pl.multiple_of(col + b1 * ncol, 128)
        elif self.early == "row":
            nrow = nrow // 2
            row = pl.multiple_of(row + b1 * nrow, 8)
        if base:
            col = pl.multiple_of(col, 128)
        return pl.ds(row, nrow), pl.ds(col, ncol)

    def mine(self):
        return self.quarter() if self.early else self.share()

    def copy(self, src, dst, slot, device):
        return pltpu.make_async_remote_copy(src, dst, self.send.at[self.a, slot], self.recv.at[self.a, slot],
                                            device_id=device, device_id_type=MESH)

    def base(self, i):
        return sum(1 << (self.nb - 1 - j) for j in range(i))

    def copies(self, s):
        w, n = here()
        kind = self.kinds[s]
        W = self.wide
        if kind == "core":
            r, c = self.share(other=True)
            return [self.copy(self.data.at[:, r, c], self.cb, W - 1, (w, flip(n, 0)))]
        if kind == "early":
            r, c = self.quarter(other=True)
            return [self.copy(self.data.at[:, r, c], self.yb, W, (w, flip(n, 1)))]
        r, c = self.mine()
        if kind == "late":
            return [self.copy(self.data.at[w, r, c], self.yb, W, (w, flip(n, 1)))]
        if kind == "join":
            ref = self.fs.at[self.quarter(base=False)]
            return [self.copy(ref, ref, W + 1, (w, flip(n, 1)))]
        if kind == "swap":
            return [self.copy(self.fs, self.fb, W + 2, (w, flip(n, 0)))]
        i = kind[1]
        peer = flip(w, self.order[i])
        out = []
        for e in range(1 << (self.nb - 1 - i)):
            blk = with_bits(peer, self.order[i + 1:], e)
            out.append(self.copy(self.data.at[blk, r, c], self.wb.at[self.base(i) + e], self.base(i) + e, (peer, n)))
        return out

    def add(self, blk, where, term):
        idx = (blk,) + where
        self.data[idx] = (self.data[idx].astype(F32) + term.astype(F32)).astype(BF16)

    def combine(self, s):
        w, n = here()
        for c in self.copies(s):
            c.wait_recv()
        kind = self.kinds[s]
        if kind in ("core", "early"):
            where = self.share() if kind == "core" else self.quarter()
            if kind == "core" and self.early:
                pass
            buf = self.cb if kind == "core" else self.yb

            def block(b, _):
                self.add(b, where, buf[b])
                return 0

            lax.fori_loop(0, self.wide, block, 0)
        elif kind == "late":
            self.fs[...] = (self.data[(w,) + self.mine()].astype(F32) + self.yb[...].astype(F32)).astype(BF16)
        elif kind == "swap":
            b0, half = bit_of(n, 0), self.ncol // 2
            rows = pl.ds(self.row - self.base_row, self.nrow)
            for b, ref in ((b0, self.fs), (1 - b0, self.fb)):
                self.out[rows, pl.ds(pl.multiple_of(self.col - self.base_col + b * half, 128), half)] = ref[...]
        elif kind != "join":
            i = kind[1]
            for e in range(1 << (self.nb - 1 - i)):
                self.add(with_bits(w, self.order[i + 1:], e), self.mine(), self.wb[self.base(i) + e])
            if i == self.nb - 1 and self.early:
                self.fs[self.quarter(base=False)] = self.data[(w,) + self.mine()]

    def start(self, s):
        if s > 0:
            self.combine(s - 1)
        for c in self.copies(s):
            c.start()

    def finish(self):
        self.combine(self.stages - 1)

    def drain(self):
        for s in range(self.stages):
            for c in self.copies(s):
                c.wait_send()


def early_split(early, region):
    if not early:
        return None
    if region[3] % 512 == 0:
        return "col"
    return "row" if region[1] % 32 == 0 else None


def scatter_buffers(wide, region, early):
    _, nrow, _, ncol = region
    half = ncol // 2
    kind = early_split(early, region)
    qr, qc = (nrow // 2, half) if kind == "row" else (nrow, half // 2) if kind == "col" else (nrow, half)
    y = (wide, qr, qc) if kind else (nrow, half)
    return [pltpu.VMEM((wide, nrow, half), BF16), pltpu.VMEM((wide - 1, qr, qc), BF16), pltpu.VMEM(y, BF16),
            pltpu.VMEM((nrow, half), BF16), pltpu.VMEM((nrow, half), BF16)]


SCATTERS = (
    (0, 0, (0, 2, 1), True),
    (0, 1, (1, 2, 0), True),
    (1, 0, (2, 0, 1), False),
    (1, 1, (0, 1, 2), False),
    (2, 0, (0, 1, 2), True),
    (2, 1, (1, 2, 0), False),
    (3, 0, (1, 0, 2), False),
    (4, 0, (0, 1, 2), True),
    (5, 0, (1, 0, 2), False),
    (6, 0, (0, 1, 2), False),
    (4, 1, (0, 1, 2), False),
    (5, 1, (2, 1, 0), False),
    (6, 1, (1, 0, 2), False),
)
SCATTER_PLAN = {
    ("ffn", 8): [(2, 0), (0, 0)],
    ("ffn", 11): [(2, 1), (0, 1)],
    ("fin", 0): [(4, 0), (5, 0), (3, 0), (1, 0)],
    ("gout", 0): [(6, 0), (0, 2)],
    ("head", 2): [(2, 2)],
    ("head", 3): [(4, 1), (5, 1), (3, 1), (1, 1)],
    ("bwd", 0): [(6, 1)],
    ("bwd", 1): [(0, 3)],
    ("bwd", 3): [(2, 3)],
    ("bwd", 4): [(0, 4)],
    ("bwd", 5): [(3, 2)],
    ("bwd", 6): [(4, 2), (1, 2)],
    ("bwd", 7): [(6, 2), (2, 4), (5, 2), (0, 5)],
    ("mid", 0): [(4, 3), (8, 0), (7, 0), (9, 0), (3, 3), (0, 6)],
    ("bwd", 8): [(2, 5)],
    ("bwd", 9): [(6, 3), (2, 6), (0, 7), (1, 3)],
    ("bwd", 10): [(8, 1), (7, 1), (9, 1)],
    ("bwd", 11): [(5, 3)],
    ("wgrad", 0): [(4, 4), (11, 0), (7, 2), (3, 4), (12, 0), (10, 0)],
    ("last", 0): [(9, 2)],
    ("last", 1): [(6, 4), (5, 4), (1, 4)],
    ("last", 2): [(11, 1), (12, 1), (10, 1)],
    ("last", 3): [(8, 2)],
    ("first", 0): [(4, 5), (7, 3), (9, 3), (3, 5), (1, 5)],
    ("first", 2): [(6, 5)],
    ("first", 3): [(5, 5)],
    ("first", 4): [(10, 2)],
    ("first", 5): [(3, 6)],
    ("first", 7): [(6, 6)],
    ("first", 8): [(5, 6), (11, 2), (8, 3), (12, 2)],
    ("second", 0): [(4, 6), (7, 4), (9, 4), (1, 6)],
    ("second", 2): [(10, 3)],
    ("second", 5): [(12, 3)],
    ("second", 6): [(4, 7), (1, 7)],
    ("second", 8): [(11, 3), (8, 4)],
    ("taps", 0): [(7, 5), (9, 5)],
    ("taps", 1): [(10, 4)],
    ("taps", 2): [(12, 4)],
    ("taps", 3): [(11, 4)],
}
PADROWS = 6 * GROUPS
FROWS = 1024
KROWS = 512


def scatter_place(weight, chunk, wide):
    per = 768 // wide
    if weight < 2:
        return (0, per, chunk * 1024, 1024), (0, 0)
    if weight == 2:
        rows = 2048 // wide
        return (chunk * (rows // 2), rows // 2, 0, 768), (0, 0)
    if weight == 3:
        return (0, per, 0, 768), (0, 0)
    return ((0, per, 0, 512) if chunk == 0 else (0, per, 512, 256)), (0, 0)


def rest_body(wide, *refs):
    (len_ref, invc_ref, small_ref, brow_ref, csum_ref, emb_h, qx_h, middle_h, cot_h, start_h, qs_h, k_h, v_h, ctx_h,
     normed_h, conv_h, wg_h, wu_h, wd_h, wq_h, wk_h, wv_h, wo_h), refs = refs[:23], refs[23:]
    (out_h, *shard, gembs, smalls), refs = refs[:10], refs[10:]
    (f0, f1, f2, tiles, x1, x2, x3, n2t, qcat, ocat, dqt, gg, gu, gd, go, gq, gk, gv,
     gconv, gscore, gg1, gg2, lsem, wsem,
     cb, esend, eb, ysend, yb, fs, fb, sall, sb, ssum, yss), refs = refs[:35], refs[35:]
    bufs, (ssend, srecv, dsend, drecv) = refs[:-4], refs[-4:]
    w, n = here()
    greet(wide, True)
    tick = Ticker()
    datas = (gg, gu, gd, go, gq, gk, gv)
    scatters = []
    for i, (a, c, order, early) in enumerate(SCATTERS):
        region, base = scatter_place(a, c, wide)
        scatters.append(Scatter(i, datas[a], shard[a], region, order, early, bufs[5 * i:5 * i + 5], (ssend, srecv), base))
    started = [0] * len(scatters)
    for (loop, at), stages in SCATTER_PLAN.items():
        for g, s in stages:
            if s == scatters[g].stages:
                tick.add(loop, at, scatters[g].finish)
                started[g] = s + 1
            elif s < scatters[g].stages:
                tick.add(loop, at, functools.partial(scatters[g].start, s))
                started[g] = s + 1

    def complete(ids):
        for s in range(16):
            for g in ids:
                sc = scatters[g]
                if started[g] <= s < sc.stages:
                    sc.start(s)
                elif s == sc.stages and started[g] <= s:
                    sc.finish()
                    started[g] = 99

    def local(src, dst, i):
        return pltpu.make_async_copy(src, dst, lsem.at[i])

    top_rows, low_rows = pl.ds(0, TOK), pl.ds(TOK, TOK)

    g2 = small_ref[pl.ds(6, 1), :]
    n2, top = x1.at[top_rows], x1.at[low_rows]
    hdd = x2.at[top_rows]
    per = 768 // wide
    ntile = wd_h.shape[0] // BLK

    def weight_tiles(f, slot):
        fs_ = pl.ds(pl.multiple_of(f * BLK, BLK), BLK)
        return [pltpu.make_async_copy(wg_h.at[:, fs_], x3.at[pl.ds(768 * slot, 768), pl.ds(0, BLK)], wsem.at[slot, 0]),
                pltpu.make_async_copy(wu_h.at[:, fs_], x3.at[pl.ds(768 * slot, 768), pl.ds(BLK, BLK)], wsem.at[slot, 1]),
                pltpu.make_async_copy(wd_h.at[fs_, :], x2.at[pl.ds(TOK + BLK * slot, BLK), :], wsem.at[slot, 2])]

    loads = [local(middle_h, f0.at[top_rows], 0), local(cot_h, f1.at[top_rows], 1)]
    for c in loads:
        c.start()
    for c in weight_tiles(0, 0):
        c.start()
    for c in loads:
        c.wait()

    def prep(r, _):
        rs = pl.ds(pl.multiple_of(r * BLK, BLK), BLK)
        x = f0[rs, :]
        nn = x * rms_parts(x) * g2
        n2[rs, :] = nn.astype(BF16)
        n2t[:, rs] = nn.T.astype(BF16)
        top[rs, :] = f1[rs, :].astype(BF16)
        for lt in range(6):
            tiles[lt, rs, :] = x[:, 128 * lt:128 * lt + 128]
        f2[rs, :] = jnp.zeros((BLK, 768), F32)
        return 0

    lax.fori_loop(0, TOK // BLK, prep, 0)
    tick("prep", 0)

    def ffn_tile(f, slot):
        for c in weight_tiles(f, slot):
            c.wait()

        @pl.when(f + 1 < ntile)
        def _():
            for c in weight_tiles(f + 1, 1 - slot):
                c.start()

        wg = x3.at[pl.ds(768 * slot, 768), pl.ds(0, BLK)]
        wu = x3.at[pl.ds(768 * slot, 768), pl.ds(BLK, BLK)]
        wd = x2.at[pl.ds(TOK + BLK * slot, BLK), :]

        tick("ffn", 2 * f)

        def rows(r, _):
            rs = pl.ds(pl.multiple_of(r * FROWS, FROWS), FROWS)
            nn = n2[rs, :]
            v = dot(nn, wg[...])
            u = dot(nn, wu[...])
            dh = dot(top[rs, :], wd[...], ((1,), (1,)))
            v2 = v * v
            t = jnp.tanh(v * (C0 + (C0 * C1) * v2))
            hp = 0.5 + 0.5 * t
            gelu = v * hp
            slope = hp + (0.5 * v) * (1.0 - t * t) * (C0 + (3.0 * C0 * C1) * v2)
            h = (gelu * u).astype(BF16)
            a = (dh * u * slope).astype(BF16)
            b = (dh * gelu).astype(BF16)
            hdd[rs, pl.ds(0, BLK)] = h
            hdd[rs, pl.ds(BLK, BLK)] = a
            hdd[rs, pl.ds(2 * BLK, BLK)] = b
            o = dot(h, wd[...])
            for lt in range(6):
                tiles[lt, rs, :] += o[:, 128 * lt:128 * lt + 128]
            f2[rs, :] += dot(a, wg[...], ((1,), (1,))) + dot(b, wu[...], ((1,), (1,)))
            return 0

        lax.fori_loop(0, TOK // FROWS, rows, 0)
        tick("ffn", 2 * f + 1)
        cols = pl.ds(pl.multiple_of(f * BLK, BLK), BLK)
        for j, ref in ((1, gg), (2, gu)):
            res = dot(n2t[...], hdd[:, pl.ds(j * BLK, BLK)])
            for i in range(wide):
                ref[i, :, cols] = res[per * i:per * i + per].astype(BF16)
        res = dot(hdd[:, pl.ds(0, BLK)], top[...], ((0,), (0,)))
        high = 2048 // wide
        for i in range(BLK // high):
            gd[f * (BLK // high) + i] = res[high * i:high * i + high].astype(BF16)

    def tile_pair(i, _):
        ffn_tile(2 * i, 0)
        ffn_tile(2 * i + 1, 1)
        return 0

    lax.fori_loop(0, ntile // 2, tile_pair, 0)
    q, k, v, ctx, normed, low = [x.at[r] for x in (x1, x2, x3) for r in (top_rows, low_rows)]
    loads = [local(h, d, i) for i, (h, d) in enumerate(
        ((qs_h, q), (k_h, k), (v_h, v), (ctx_h, ctx), (normed_h, normed), (wo_h, n2t.at[:, pl.ds(0, 768)]),
         (qx_h, qcat.at[:, pl.ds(128, 128)])))]
    for c in loads:
        c.start()
    stores = [local(tiles.at[lt, top_rows, :], out_h.at[:, pl.ds(128 * lt, 128)], 8 + lt) for lt in range(6)]
    for c in stores:
        c.start()
    tick("fin", 0)
    gg2[...] = jnp.zeros_like(gg2)

    def fin(r, _):
        rs = pl.ds(pl.multiple_of(r * BLK, BLK), BLK)
        dxv, part = rms_back(f0[rs, :], g2, f2[rs, :])
        f1[rs, :] += dxv
        gg2[...] += part
        return 0

    lax.fori_loop(0, TOK // BLK, fin, 0)
    start_load = local(start_h, f0.at[top_rows], 7)
    start_load.start()
    for c in loads:
        c.wait()

    wo = n2t.at[:, pl.ds(0, 768)]
    length = len_ref[0, 0]

    def lower(r, _):
        rs = pl.ds(pl.multiple_of(r * BLK, BLK), BLK)
        low[rs, :] = f1[rs, :].astype(BF16)
        return 0

    lax.fori_loop(0, TOK // BLK, lower, 0)
    whole = dot(ctx[...], low[...], ((0,), (0,))).astype(BF16)
    for c in range(wide):
        go[c] = whole[per * c:per * c + per]
    tick("gout", 0)
    lane_s = lax.broadcasted_iota(jnp.int32, (768, 128), 1)
    row_s = lax.broadcasted_iota(jnp.int32, (768, 128), 0)
    sel = jnp.where(lane_s // 3 == row_s // 64, 1.0, 0.0).astype(BF16)
    lane_b = lax.broadcasted_iota(jnp.int32, (BLK, 128), 1)
    row_b = lax.broadcasted_iota(jnp.int32, (BLK, 128), 0)

    def head(r, _):
        tick("head", r)
        rs = pl.ds(pl.multiple_of(r * BLK, BLK), BLK)
        d = dot(low[rs, :], wo[...], ((1,), (1,))).astype(BF16)
        prod = d.astype(F32) * ctx[rs, :].astype(F32)
        ctx[rs, :] = d
        hi = prod.astype(BF16)
        delta = dot(hi, sel) + dot((prod - hi.astype(F32)).astype(BF16), sel)
        a, b, c = split3(-delta)
        ocat[rs, pl.ds(128, 128)] = jnp.where(lane_b % 3 == 0, a, jnp.where(lane_b % 3 == 1, b, c)).astype(BF16)
        return 0

    lax.fori_loop(0, TOK // BLK, head, 0)
    late_loads = [local(wk_h, x3.at[pl.ds(TOK, 768)], 0), local(wv_h, n2t.at[:, pl.ds(0, 768)], 1)]
    for c in late_loads:
        c.start()

    lane_k = lax.broadcasted_iota(jnp.int32, (KROWS, 128), 1)
    row_k = lax.broadcasted_iota(jnp.int32, (KROWS, 128), 0)

    def pair(p, _):
        ls = pl.ds(pl.multiple_of(p * 128, 128), 128)
        qcat[:, pl.ds(0, 128)] = q[:, ls]
        ocat[:, pl.ds(0, 128)] = ctx[:, ls]
        dqt[...] = jnp.zeros_like(dqt)

        def kblock(r, _):
            tick("bwd", 2 * p + r)
            rs = pl.ds(pl.multiple_of(r * KROWS, KROWS), KROWS)
            bias = jnp.where((lane_k == 0) & (2 * (row_k + r * KROWS) >= length), NEG, 0.0)
            dvb = jnp.zeros((KROWS, 128), F32)
            dkb = jnp.zeros((KROWS, 128), F32)
            dqb = dqt[...]
            for h2 in range(2):
                hm = head_lanes(h2, KROWS)
                hd = 3 * (2 * p + h2)
                km = k[rs, ls] * hm
                vm = v[rs, ls] * hm
                kxl = jnp.where((lane_k > hd) & (lane_k <= hd + 3), 1.0, bias).astype(BF16)
                vxl = jnp.where((lane_k >= hd) & (lane_k < hd + 3), 1.0, 0.0).astype(BF16)
                st = dot(jnp.concatenate([km, kxl], axis=1), qcat[...], ((1,), (1,)))
                dp = dot(jnp.concatenate([vm, vxl], axis=1), ocat[...], ((1,), (1,)))
                prob = jnp.exp(st)
                dsc = (prob * dp).astype(BF16)
                dvb = dvb + dot(prob.astype(BF16), ocat[:, pl.ds(0, 128)]) * hm.astype(F32)
                dkb = dkb + dot(dsc, qcat[:, pl.ds(0, 128)]) * hm.astype(F32)
                dqb = dqb + dot(km, dsc, ((0,), (0,)))
            v[rs, ls] = dvb.astype(BF16)
            k[rs, ls] = dkb.astype(BF16)
            dqt[...] = dqb
            return 0

        lax.fori_loop(0, TOK // KROWS, kblock, 0)
        q[:, ls] = (dqt[...].T * 0.125).astype(BF16)
        return 0

    def wgrad(c, _):
        cs = pl.ds(pl.multiple_of(c * BLK, BLK), BLK)
        for src, ref in ((q, gq), (k, gk), (v, gv)):
            res = dot(normed[...], src[:, cs], ((0,), (0,))).astype(BF16)
            for i in range(wide):
                ref[i, :, cs] = res[per * i:per * i + per]
        return 0

    lax.fori_loop(0, 4, pair, 0)
    lax.fori_loop(0, 2, wgrad, 0)
    tick("mid", 0)
    lax.fori_loop(4, HEADS // 2, pair, 0)
    wq_load = local(wq_h, x2.at[pl.ds(TOK, 768)], 2)
    wq_load.start()
    lax.fori_loop(2, 3, wgrad, 0)
    tick("wgrad", 0)
    start_load.wait()
    for c in late_loads + [wq_load]:
        c.wait()
    for c in stores:
        c.wait()
    gg1[...] = jnp.zeros_like(gg1)
    g1 = small_ref[pl.ds(5, 1), :]
    wq, wk, wv = x2.at[pl.ds(TOK, 768)], x3.at[pl.ds(TOK, 768)], n2t.at[:, pl.ds(0, 768)]

    def last(r, _):
        tick("last", r)
        rs = pl.ds(pl.multiple_of(r * BLK, BLK), BLK)
        d = (dot(q[rs, :], wq[...], ((1,), (1,))) + dot(k[rs, :], wk[...], ((1,), (1,)))
             + dot(v[rs, :], wv[...], ((1,), (1,))))
        dxv, part = rms_back(f0[rs, :], g1, d)
        res = f1[rs, :] + dxv
        for lt in range(6):
            tiles[lt, rs, :] = res[:, 128 * lt:128 * lt + 128]
        gg1[...] += part
        return 0

    lax.fori_loop(0, TOK // BLK, last, 0)
    conv = x3.at[pl.ds(0, PERIOD * GROUPS)]
    emb = x2.at[pl.ds(TOK, 256)]
    final_loads = [local(conv_h, conv, 14), local(emb_h, emb, 15)]
    for c in final_loads:
        c.start()
    for lt in range(6):
        tiles[lt, pl.ds(TOK, PADROWS - TOK), :] = jnp.zeros((PADROWS - TOK, 128), F32)
    for c in final_loads:
        c.wait()

    gemb = f0.at[pl.ds(0, 256)]
    gbst_bwd_body(tick, len_ref, invc_ref, brow_ref, emb, small_ref.at[pl.ds(0, 4)], small_ref.at[pl.ds(4, 1)],
                  conv, csum_ref, gemb, gconv, gscore, f2, Planes(f1, 128), Planes(f1, 0), x1, x2, tiles)

    def copy(src, dst, kk, slot, device):
        return pltpu.make_async_remote_copy(src, dst, dsend.at[kk, slot], drecv.at[kk, slot],
                                            device_id=device, device_id_type=MESH)

    half = 384
    gc = lambda b: pl.ds(pl.multiple_of(b * half, 128), half)
    b0 = bit_of(n, 0)
    esend[...] = gemb[:, gc(1 - b0)].astype(BF16).reshape(esend.shape)
    core = copy(esend, cb, 0, 0, (w, flip(n, 0)))
    core.start()
    r8 = lax.broadcasted_iota(jnp.int32, (8, 768), 0)
    total = gconv[...] * jnp.where(r8 < 4, 1.0, 0.0)
    for row, ref in ((4, gscore), (5, gg1), (6, gg2)):
        total = jnp.where(r8 == row, jnp.sum(ref[...], axis=0, keepdims=True), total)
    rl = lax.broadcasted_iota(jnp.int32, (768, 128), 0)
    cl = lax.broadcasted_iota(jnp.int32, (768, 128), 1)
    for i in range(wide):
        sall[i] = dot(total, jnp.where((rl == per * i + cl) & (cl < per), 1.0, 0.0).astype(F32), precision=HIGH)
    peers = [(lax.rem(w + d, wide), n) for d in range(1, wide)]
    small_copies = [copy(sall.at[p[0]], sb.at[w], 1, d + 1, p) for d, p in enumerate(peers)]
    for c in small_copies:
        c.start()
    core.wait()
    esend[...] = (gemb[:, gc(b0)].reshape(esend.shape) + cb[...].astype(F32)).astype(BF16)
    emb_copies = [copy(esend.at[p[0]], eb.at[w], 2, d + 1, p) for d, p in enumerate(peers)]
    for c in emb_copies:
        c.start()
    sb[w] = sall[w]
    eb[w] = esend[w]
    complete(range(len(scatters)))
    for c in small_copies + emb_copies:
        c.wait_recv()
    ysend[...] = sum(eb[i].astype(F32) for i in range(wide))
    ssum[0] = sum(sb[i] for i in range(wide))
    late = [copy(ysend, yb, 3, 0, (w, flip(n, 1))), copy(ssum.at[0], yss.at[0], 3, 1, (w, flip(n, 1)))]
    for c in late:
        c.start()
    for c in late:
        c.wait_recv()
    fs[...] = (ysend[...] + yb[...]).astype(BF16)
    ssum[1] = ssum[0] + yss[0]
    swap = [copy(fs, fb, 4, 0, (w, flip(n, 0))), copy(ssum.at[1], yss.at[1], 4, 1, (w, flip(n, 0)))]
    for c in swap:
        c.start()
    for c in swap:
        c.wait_recv()
    gembs[:, gc(b0)] = fs[...]
    gembs[:, gc(1 - b0)] = fb[...]
    smalls[...] = ssum[1] + yss[1]
    for c in small_copies + emb_copies + late + swap:
        c.wait_send()
    for g in range(len(scatters)):
        scatters[g].drain()


def rest(wide, args):
    rows, per, high = 256 // wide, 768 // wide, 2048 // wide
    bufs = []
    for a, c, _, early in SCATTERS:
        bufs += scatter_buffers(wide, scatter_place(a, c, wide)[0], early)
    v = pltpu.VMEM
    dma = pltpu.SemaphoreType.DMA
    ns = len(SCATTERS)
    shape = lambda *s: jax.ShapeDtypeStruct(s, BF16)
    return pl.pallas_call(
        functools.partial(rest_body, wide),
        out_shape=(jax.ShapeDtypeStruct((TOK, 768), F32), shape(per, 2048), shape(per, 2048), shape(high, 768),
                   shape(per, 768), shape(per, 768), shape(per, 768), shape(per, 768), shape(rows, 768),
                   jax.ShapeDtypeStruct((8, 128), F32)),
        in_specs=[SM, SM] + [VM] * 3 + [HB] * 18,
        out_specs=(HB,) + (VM,) * 9,
        scratch_shapes=[
            v((PADROWS, 768), F32), v((PADROWS, 768), F32), v((PADROWS, 768), F32), v((6, PADROWS, 128), F32),
            v((2304, 768), BF16), v((2 * TOK, 768), BF16), v((2112, 768), BF16), v((768, TOK), BF16),
            v((TOK, 256), BF16), v((TOK, 256), BF16), v((128, TOK), F32),
            v((wide, per, 2048), BF16), v((wide, per, 2048), BF16), v((wide, high, 768), BF16), v((wide, per, 768), BF16),
            v((wide, per, 768), BF16), v((wide, per, 768), BF16), v((wide, per, 768), BF16),
            v((8, 768), F32), v((8, 768), F32), v((8, 768), F32), v((8, 768), F32), dma((16,)), dma((2, 3)),
            v((wide, rows, 384), BF16), v((wide, rows, 384), BF16), v((wide, rows, 384), BF16), v((rows, 384), F32),
            v((rows, 384), F32), v((rows, 384), BF16), v((rows, 384), BF16), v((wide, 8, 128), F32), v((wide, 8, 128), F32),
            v((2, 8, 128), F32), v((2, 8, 128), F32)]
        + bufs + [dma((ns, wide + 3)), dma((ns, wide + 3)), dma((5, wide)), dma((5, wide))],
        compiler_params=pltpu.CompilerParams(vmem_limit_bytes=64 << 20, collective_id=1, has_side_effects=True),
        name="rest",
    )(*args)


def finish_body(wide, out_ref, *refs):
    shard, (gembs, smalls, tot), refs = refs[:7], refs[7:10], refs[10:]
    (res, ent, emb, conv, score, g1, g2), outs = refs[:7], refs[7:14]
    per = 768 // wide
    res[...] = out_ref[...]
    for src, dst in zip(shard, outs):
        dst[...] = src[...].astype(F32)
    emb[...] = gembs[...].astype(F32)
    ent[0, 0] = tot[0, 1] / tot[0, 0]
    conv[...] = smalls[pl.ds(0, 4), pl.ds(0, per)]
    score[...] = smalls[pl.ds(4, 1), pl.ds(0, per)]
    g1[...] = smalls[pl.ds(5, 1), pl.ds(0, per)]
    g2[...] = smalls[pl.ds(6, 1), pl.ds(0, per)]


def finish(wide, out, shards, gembs, smalls, tot):
    rows, per = 256 // wide, 768 // wide
    f = lambda *s: jax.ShapeDtypeStruct(s, F32)
    return pl.pallas_call(
        functools.partial(finish_body, wide),
        out_shape=(f(TOK, 768), f(1, 1), f(rows, 768), f(4, per), f(1, per), f(1, per), f(1, per))
        + tuple(f(*s.shape) for s in shards),
        in_specs=[VM] * 10 + [SM],
        out_specs=(VM, SM) + (VM,) * 12,
        compiler_params=pltpu.CompilerParams(vmem_limit_bytes=60 << 20),
        name="finish",
    )(out, *shards, gembs, smalls, tot)


def body(
    wide, narrow,
    byte_values, row_lengths, embedding, conv_kernel, score_vector, attn_gain, query_weight, key_weight,
    value_weight, output_weight, ffn_gain, gate_weight, up_weight, down_weight, cotangent,
):
    length = row_lengths.reshape(1, 1)
    bcol, brow = byte_planes(byte_values[0], row_lengths[0])
    small = jnp.concatenate([conv_kernel, score_vector[None], attn_gain[None], ffn_gain[None]], axis=0).astype(F32)
    small = jnp.pad(small, ((0, 8 - small.shape[0]), (0, 128 - small.shape[1])))
    shards = (query_weight, key_weight, value_weight, output_weight, gate_weight, up_weight, down_weight)
    got = front(wide, narrow, length, bcol, embedding, small, shards)
    wq, wk, wv, wo, wg, wu, wd = [x.reshape(-1, x.shape[-1]) for x in got[:7]]
    start, conv, csum, tot, smallall, emb, qs, k, v, ctx, qx, normed, middle = got[7:]
    invc = (ENT_WEIGHT / tot[0, 0]).reshape(1, 1)
    out, *rest_out = rest(wide, (length, invc, smallall, brow, csum, emb, qx, middle, cotangent[0], start, qs, k, v, ctx,
                                 normed, conv.reshape(PERIOD * GROUPS, 768), wg, wu, wd, wq, wk, wv, wo))
    shard, (gembs, smalls) = rest_out[:7], rest_out[7:]
    res, ent, ge, gc, gs, gg1, gg2, sg, su, sd, so, sq, sk, sv = finish(wide, out, shard, gembs, smalls, tot)
    flat = lambda x: x.reshape(-1)
    return (res[None], ent.reshape(()), ge, gc, flat(gs), flat(gg1), sq, sk, sv, so, flat(gg2), sg, su, sd)


def solution(mesh):
    both = ("wide", "narrow")
    row, flat = P("wide", None), P("wide")
    return jax.shard_map(
        functools.partial(body, mesh.shape["wide"], mesh.shape["narrow"]),
        mesh=mesh,
        in_specs=(P(both, None), P(both), row, P(None, "wide"), flat, flat, row, row, row, row, flat,
                  row, row, row, P(both, None, None)),
        out_specs=(P(both, None, None), P(), row, P(None, "wide"), flat, flat, row, row, row, row, flat,
                   row, row, row),
        check_vma=False,
    )
```

```python
import functools
import jax
import jax.numpy as jnp
from jax import lax
from jax.experimental import pallas as pl
from jax.experimental.pallas import tpu as pltpu
from jax.sharding import PartitionSpec as P

F32 = jnp.float32
BF16 = jnp.bfloat16
EPS = 1e-06
HEADS = 12
ENT_WEIGHT = 1.0
PERIOD = 12
GROUPS = 176
HIGH = lax.Precision.HIGHEST
VM = pl.BlockSpec(memory_space=pltpu.VMEM)
SM = pl.BlockSpec(memory_space=pltpu.SMEM)


def dot(a, b, dims=((1,), (0,)), precision=None):
    return lax.dot_general(a, b, (dims, ((), ())), precision=precision, preferred_element_type=F32)


def same_block(size):
    r = lax.broadcasted_iota(jnp.int32, (128, 128), 0)
    c = lax.broadcasted_iota(jnp.int32, (128, 128), 1)
    return jnp.where((r // size == c // size) & (r < PERIOD) & (c < PERIOD), 1.0, 0.0).astype(F32)


def block_sum(x, size):
    return dot(x, same_block(size), precision=HIGH)


def lane_scalars(csum, length):
    i = lax.broadcasted_iota(jnp.int32, (GROUPS, 128), 0)
    k = lax.broadcasted_iota(jnp.int32, (GROUPS, 128), 1)
    mask = jnp.where((PERIOD * i + k < length) & (k < PERIOD), 1.0, 0.0).astype(F32)
    tok = block_sum(jnp.where(k % 2 == 0, mask, 0.0), 2)
    inv = [jnp.ones_like(mask)] + [1.0 / jnp.maximum(block_sum(mask, b), 1.0) for b in (2, 3, 4)]
    scores = [csum] + [block_sum(csum, b) * inv[b - 1] for b in (2, 3, 4)]
    top = functools.reduce(jnp.maximum, scores)
    ex = [jnp.exp(s - top) for s in scores]
    total = ex[0] + ex[1] + ex[2] + ex[3]
    rec = 1.0 / total
    chance = [e * rec for e in ex]
    mean = sum(c * s for c, s in zip(chance, scores))
    ent = mask * (top + jnp.log(total) - mean)
    alpha = [c * v for c, v in zip(chance, inv)]
    return mask, tok, inv, scores, chance, mean, ent, alpha


def gbst_fwd_body(tick, params, len_ref, bcol_ref, start_ref, conv_ref, csum_ref, ent_ref,
                  table, onehot, planes, coef, tiles):
    length = len_ref[0, 0]
    vocab = lax.broadcasted_iota(jnp.int32, (GROUPS, 256), 1)
    for k in range(PERIOD + 3):
        onehot[:, pl.ds(256 * k, 256)] = jnp.where(bcol_ref[:, k:k + 1] == vocab, 1.0, 0.0).astype(BF16)
    csum_ref[...] = jnp.zeros_like(csum_ref)
    tick("onehot", 0)
    emb, small = params()
    for j in range(4):
        table[pl.ds(256 * j, 256), :] = (emb * small[j:j + 1]).astype(BF16)
    s = small[4:5]
    tick("table", 0)
    rows = lax.broadcasted_iota(jnp.int32, (GROUPS, 1), 0)
    lane = lax.broadcasted_iota(jnp.int32, (GROUPS, 128), 1)

    def plane(k, _):
        tick("plane", k)
        lhs = onehot[:, pl.ds(pl.multiple_of(256 * k, 256), 1024)]
        out = dot(lhs, table[...])
        out = jnp.where(PERIOD * rows + k < length, out, 0.0)
        planes[k] = out
        conv_ref[k] = out.astype(BF16)
        c = jnp.sum(out * s, axis=1, keepdims=True)
        csum_ref[...] = jnp.where(lane == k, c, csum_ref[...])
        return 0

    lax.fori_loop(0, PERIOD, plane, 0)
    mask, tok, inv, scores, chance, mean, ent, alpha = lane_scalars(csum_ref[...], length)
    ent_ref[...] = jnp.sum(jnp.sum(ent, axis=0, keepdims=True), axis=1, keepdims=True) + jnp.zeros((8, 128), F32)
    half = 0.5 * tok
    coef[0] = (alpha[0] + block_sum(alpha[1], 2)) * half
    coef[1] = alpha[2] * half
    coef[2] = block_sum(alpha[2], 2) * half
    coef[3] = block_sum(alpha[3], 2) * half

    def rowblock(ib, _):
        tick("rows", ib)
        r0 = pl.multiple_of(ib * 16, 16)
        rs = pl.ds(r0, 16)
        ce, c3, c3p, c4p = [coef[n, rs, :] for n in range(4)]
        for lt in range(6):
            ls = pl.ds(128 * lt, 128)
            p = [planes[k, rs, ls] for k in range(PERIOD)]
            pair = [p[2 * m] + p[2 * m + 1] for m in range(6)]
            quad = [pair[2 * y] + pair[2 * y + 1] for y in range(3)]
            tri = [p[3 * x] + p[3 * x + 1] + p[3 * x + 2] for x in range(4)]
            for m in range(6):
                a, b = 2 * m, 2 * m + 1
                out = ce[:, a:a + 1] * p[a] + ce[:, b:b + 1] * p[b] + c4p[:, a:a + 1] * quad[m // 2]
                if a // 3 == b // 3:
                    out = out + c3p[:, a:a + 1] * tri[a // 3]
                else:
                    out = out + c3[:, a:a + 1] * tri[a // 3] + c3[:, b:b + 1] * tri[b // 3]
                tiles[lt, pl.ds(6 * r0 + m, 16, stride=6), :] = out
        return 0

    lax.fori_loop(0, GROUPS // 16, rowblock, 0)
    for lt in range(6):
        start_ref[:, pl.ds(128 * lt, 128)] = tiles[lt, pl.ds(0, start_ref.shape[0]), :]


def gbst_bwd_body(tick, len_ref, invc_ref, brow_ref, emb_ref, ck_ref, sc_ref, conv_ref, csum_ref,
                  gemb_ref, gconv_ref, gscore_ref, dm, dots, coef, dconv, onehot, tiles):
    length = len_ref[0, 0]
    at = lambda k, r0: pl.ds(pl.multiple_of(GROUPS * k + r0, 16), 16)
    invc = invc_ref[0, 0]
    mask, tok, inv, scores, chance, mean, ent, alpha = lane_scalars(csum_ref[...], length)
    half = 0.5 * tok
    coef[0] = half
    lane16 = lax.broadcasted_iota(jnp.int32, (16, 128), 1)

    def first(ib, _):
        tick("first", ib)
        r0 = pl.multiple_of(ib * 16, 16)
        rs = pl.ds(r0, 16)
        h = coef[0, rs, :]
        acc = [jnp.zeros((16, 128), F32) for _ in range(26)]
        for lt in range(6):
            ls = pl.ds(128 * lt, 128)
            p = [conv_ref[at(k, r0), ls].astype(F32) for k in range(PERIOD)]
            quad = [(p[4 * y] + p[4 * y + 1]) + (p[4 * y + 2] + p[4 * y + 3]) for y in range(3)]
            tri = [p[3 * x] + p[3 * x + 1] + p[3 * x + 2] for x in range(4)]
            n = 0
            for m in range(6):
                d = tiles[lt, pl.ds(6 * r0 + m, 16, stride=6), :] * h[:, 2 * m:2 * m + 1]
                dm[at(m, r0), ls] = d
                for q in terms(m, p, quad, tri):
                    acc[n] = acc[n] + d * q
                    n += 1
        g1 = jnp.zeros((16, 128), F32)
        g3 = jnp.zeros((16, 128), F32)
        g4 = jnp.zeros((16, 128), F32)
        n = 0
        for m in range(6):
            a, b = 2 * m, 2 * m + 1
            v = [jnp.sum(acc[n + q], axis=1, keepdims=True) for q in range(len(TERMS[m]))]
            n += len(TERMS[m])
            g1 = jnp.where(lane16 == a, v[0], jnp.where(lane16 == b, v[1], g1))
            g4 = jnp.where((lane16 == a) | (lane16 == b), v[2], g4)
            g3 = jnp.where(lane16 == a, v[3], jnp.where(lane16 == b, v[-1], g3))
        dots[0, rs, :] = g1
        dots[1, rs, :] = g3
        dots[2, rs, :] = g4
        return 0

    lax.fori_loop(0, GROUPS // 16, first, 0)
    g1 = dots[0]
    dch = [g1, block_sum(g1, 2) * inv[1], dots[1] * inv[2], dots[2] * inv[3]]
    dmean = sum(c * d for c, d in zip(chance, dch))
    dsc = [c * (d - dmean) - invc * mask * c * (s - mean) for c, d, s in zip(chance, dch, scores)]
    w = dsc[0] + sum(block_sum(dsc[b - 1], b) * inv[b - 1] for b in (2, 3, 4))
    coef[0] = (alpha[0] + block_sum(alpha[1], 2)) * mask
    coef[1] = alpha[2]
    coef[2] = block_sum(alpha[2], 2)
    coef[3] = block_sum(alpha[3], 2)
    coef[4] = w * mask
    coef[5] = mask
    s = sc_ref[...].astype(F32)
    gscore_ref[...] = jnp.zeros_like(gscore_ref)
    dconv[pl.ds(PERIOD * GROUPS, 2304 - PERIOD * GROUPS), :] = jnp.zeros((2304 - PERIOD * GROUPS, 768), BF16)

    def second(ib, _):
        tick("second", ib)
        r0 = pl.multiple_of(ib * 16, 16)
        rs = pl.ds(r0, 16)
        ce, c3, c3p, c4p, cw, mk = [coef[n, rs, :] for n in range(6)]
        for lt in range(6):
            ls = pl.ds(128 * lt, 128)
            d = [dm[at(m, r0), ls] for m in range(6)]
            tri = [c3p[:, 0:1] * d[0] + c3[:, 2:3] * d[1], c3[:, 3:4] * d[1] + c3p[:, 4:5] * d[2],
                   c3p[:, 6:7] * d[3] + c3[:, 8:9] * d[4], c3[:, 9:10] * d[4] + c3p[:, 10:11] * d[5]]
            quad = [c4p[:, 4 * y:4 * y + 1] * d[2 * y] + c4p[:, 4 * y + 2:4 * y + 3] * d[2 * y + 1] for y in range(3)]
            st = s[:, 128 * lt:128 * lt + 128]
            gs = jnp.zeros((16, 128), F32)
            for k in range(PERIOD):
                wk = cw[:, k:k + 1]
                out = ce[:, k:k + 1] * d[k // 2] + mk[:, k:k + 1] * (tri[k // 3] + quad[k // 4]) + wk * st
                gs = gs + wk * conv_ref[at(k, r0), ls].astype(F32)
                dconv[pl.ds(pl.multiple_of(GROUPS * k + r0, 16), 16), ls] = out.astype(BF16)
            gscore_ref[:, ls] += gs[:8] + gs[8:]
        return 0

    lax.fori_loop(0, GROUPS // 16, second, 0)
    vocab = lax.broadcasted_iota(jnp.int32, (256, 768), 0)
    emb = emb_ref[...].astype(F32)
    for j in range(4):
        tick("taps", j)
        g = jnp.zeros((256, 768), F32)
        for p in range(3):
            onehot[pl.ds(256 * p, 256), :] = jnp.where(brow_ref[pl.ds(j, 1), pl.ds(768 * p, 768)] == vocab, 1.0, 0.0).astype(BF16)
            g = g + dot(onehot[pl.ds(256 * p, 256), :], dconv[pl.ds(768 * p, 768), :])
        gconv_ref[pl.ds(j, 1), :] = jnp.sum(g * emb, axis=0, keepdims=True)
        part = g * ck_ref[pl.ds(j, 1), :].astype(F32)
        gemb_ref[...] = part if j == 0 else gemb_ref[...] + part


class Planes:
    def __init__(self, ref, col):
        self.ref, self.cols = ref, pl.ds(col, 128)

    def where(self, key):
        if isinstance(key, tuple):
            return pl.ds(pl.multiple_of(GROUPS * key[0] + key[1].start, 16), key[1].size), self.cols
        return pl.ds(GROUPS * key, GROUPS), self.cols

    def __getitem__(self, key):
        return self.ref[self.where(key)]

    def __setitem__(self, key, value):
        self.ref[self.where(key)] = value


TERMS = {m: (1, 1, 4, 3) if (2 * m) // 3 == (2 * m + 1) // 3 else (1, 1, 4, 3, 3) for m in range(6)}


def terms(m, p, quad, tri):
    a, b = 2 * m, 2 * m + 1
    out = [p[a], p[b], quad[m // 2], tri[a // 3]]
    if a // 3 != b // 3:
        out.append(tri[b // 3])
    return out


def byte_planes(byte_values, length):
    positions = byte_values.shape[0]
    real = jnp.where(jnp.arange(positions) < length, byte_values, -1)
    ext = jnp.pad(real, (1, PERIOD * (GROUPS + 2) - positions - 1), constant_values=-1)
    cols = ext.reshape(GROUPS + 2, PERIOD)
    wide = jnp.concatenate([cols[:GROUPS], cols[1:GROUPS + 1, :4]], axis=1)
    rows = wide.T
    brow = jnp.stack([jnp.pad(rows[j:j + PERIOD].reshape(-1), (0, 2304 - PERIOD * GROUPS), constant_values=-1)
                      for j in range(4)])
    return wide, brow

TOK = 1024
QROWS = 256
BLK = 256
NEG = -1e30


def rms_parts(x):
    return lax.rsqrt(jnp.mean(x * x, axis=1, keepdims=True) + EPS)


def head_lanes(h2, rows, dtype=BF16):
    lane = lax.broadcasted_iota(jnp.int32, (rows, 128), 1)
    return jnp.where(lane // 64 == h2, 1.0, 0.0).astype(dtype)


def split3(x):
    hi = x.astype(BF16).astype(F32)
    mid = (x - hi).astype(BF16).astype(F32)
    return hi, mid, x - hi - mid


def att_fwd_body(tick, len_ref, start_ref, gain, wq_ref, wk_ref, wv_ref, wo_ref,
                 qs_ref, k_ref, v_ref, ctx_ref, qx_ref, normed_ref, middle_ref,
                 kx, vext, kext, qxf):
    length = len_ref[0, 0]
    g = gain
    tick("project", 0)

    def project(r, _):
        rs = pl.ds(pl.multiple_of(r * BLK, BLK), BLK)
        x = start_ref[rs, :]
        n = (x * rms_parts(x) * g).astype(BF16)
        normed_ref[rs, :] = n
        qs_ref[rs, :] = (dot(n, wq_ref[...]).astype(BF16).astype(F32) * 0.125).astype(BF16)
        k_ref[rs, :] = dot(n, wk_ref[...]).astype(BF16)
        v_ref[rs, :] = dot(n, wv_ref[...]).astype(BF16)
        return 0

    lax.fori_loop(0, TOK // BLK, project, 0)
    lane = lax.broadcasted_iota(jnp.int32, (TOK, 128), 1)
    row = lax.broadcasted_iota(jnp.int32, (TOK, 128), 0)
    keep = 2 * row < length
    kx[...] = jnp.where((lane == 0) & ~keep, NEG, 0.0).astype(BF16)
    ones = jnp.where(keep, 1.0, 0.0).astype(BF16)
    for h2 in range(2):
        vext[h2, :, pl.ds(128, 128)] = ones
        kext[h2, :, pl.ds(128, 128)] = kx[...]
    qxf[...] = jnp.where(lane == 0, 1.0, 0.0).astype(F32)
    lane_b = lax.broadcasted_iota(jnp.int32, (QROWS, 128), 1)
    first = jnp.where(lane_b == 0, 1.0, 0.0).astype(BF16)

    def pair(p, _):
        ls = pl.ds(pl.multiple_of(p * 128, 128), 128)
        for h2 in range(2):
            hm = head_lanes(h2, TOK)
            vext[h2, :, pl.ds(0, 128)] = v_ref[:, ls] * hm
            kext[h2, :, pl.ds(0, 128)] = k_ref[:, ls] * hm

        def qblock(r, _):
            tick("att", 4 * p + r)
            rs = pl.ds(pl.multiple_of(r * QROWS, QROWS), QROWS)
            q = jnp.concatenate([qs_ref[rs, ls], first], axis=1)
            out = jnp.zeros((QROWS, 128), F32)
            upd = qxf[rs, :]
            for h2 in range(2):
                s = dot(q, kext[h2], ((1,), (1,)))
                m = jnp.max(s, axis=1, keepdims=True)
                e = jnp.exp(s - m).astype(BF16)
                c = dot(e, vext[h2])
                total = c[:, 128:]
                out = out + c[:, :128] * (1.0 / total)
                hi, mid, lo = split3(-(m + jnp.log(total)))
                base = 1 + 3 * (2 * p + h2)
                upd = jnp.where(lane_b == base, hi, jnp.where(lane_b == base + 1, mid,
                                jnp.where(lane_b == base + 2, lo, upd)))
            qxf[rs, :] = upd
            ctx_ref[rs, ls] = out.astype(BF16)
            return 0

        lax.fori_loop(0, TOK // QROWS, qblock, 0)
        return 0

    lax.fori_loop(0, HEADS // 2, pair, 0)
    qx_ref[...] = qxf[...].astype(BF16)

    tick("outproj", 0)

    def outproj(r, _):
        rs = pl.ds(pl.multiple_of(r * BLK, BLK), BLK)
        middle_ref[rs, :] = start_ref[rs, :] + dot(ctx_ref[rs, :], wo_ref[...])
        return 0

    lax.fori_loop(0, TOK // BLK, outproj, 0)


def rms_back(x, g, d):
    s = rms_parts(x)
    xn = x * s
    dxn = d * xn
    gg = jnp.sum(dxn.reshape(x.shape[0] // 8, 8, x.shape[1]), axis=0)
    return s * (d * g - xn * jnp.mean(dxn * g, axis=1, keepdims=True)), gg


C0 = 0.7978845608028654
C1 = 0.044715


MESH = pl.DeviceIdType.MESH
HB = pl.BlockSpec(memory_space=pl.ANY)


def bit_of(v, b):
    return (v // (1 << b)) % 2


def flip(v, b):
    return v + (1 - 2 * bit_of(v, b)) * (1 << b)


def with_bits(v, bits, e):
    for i, b in enumerate(bits):
        v = v + (((e >> i) & 1) - bit_of(v, b)) * (1 << b)
    return v


def here():
    return lax.axis_index("wide"), lax.axis_index("narrow")


def greet(wide, direct):
    w, n = here()
    sem = pltpu.get_barrier_semaphore()
    peers = [(lax.rem(w + d, wide), n) for d in range(1, wide)] if direct else [
        (flip(w, b), n) for b in range(wide.bit_length() - 1)]
    peers = peers + [(w, flip(n, 0)), (w, flip(n, 1))]
    for p in peers:
        pl.semaphore_signal(sem, inc=1, device_id=p, device_id_type=MESH)
    pl.semaphore_wait(sem, len(peers))


class Ticker:
    def __init__(self):
        self.todo = {}

    def add(self, name, index, fn):
        self.todo.setdefault((name, index), []).append(fn)

    def __call__(self, name, index):
        for (loop, at), fns in self.todo.items():
            if loop == name:
                if isinstance(index, int):
                    if at == index:
                        for fn in fns:
                            fn()
                else:
                    @pl.when(index == at)
                    def _(fns=fns):
                        for fn in fns:
                            fn()


def wide_order(order, wide):
    bits = wide.bit_length() - 1
    return order if bits == len(order) else tuple(range(bits - 1, -1, -1))


class Gather:
    def __init__(self, index, shard, out, region, order, split, sems):
        self.a, self.shard, self.out = index, shard, out
        self.row, self.nrow, self.col, self.ncol = region
        self.wide = out.shape[0]
        self.order = wide_order(order, self.wide)
        self.split = None
        if split:
            if self.ncol % 512 == 0:
                self.split = "col"
            elif self.nrow % 16 == 0:
                self.split = "row"
        self.send, self.recv, self.local = sems
        self.stages = len(self.order) + (2 if self.split else 1)

    def part(self, ref, quarter=True):
        _, n = here()
        half = self.ncol // 2
        col, ncol = self.col + bit_of(n, 0) * half, half
        row, nrow = self.row, self.nrow
        if self.split == "col" and quarter:
            ncol = half // 2
            col = col + bit_of(n, 1) * ncol
        rs = pl.ds(row, nrow)
        if self.split == "row" and quarter:
            nrow = nrow // 2
            rs = pl.ds(pl.multiple_of(row + bit_of(n, 1) * nrow, 8), nrow)
        lead = (slice(None),) * (len(ref.shape) - 2)
        return ref.at[lead + (rs, pl.ds(pl.multiple_of(col, 128), ncol))]

    def copy(self, src, dst, slot, device):
        return pltpu.make_async_remote_copy(src, dst, self.send.at[self.a, slot], self.recv.at[self.a, slot],
                                            device_id=device, device_id_type=MESH)

    def copies(self, i):
        w, n = here()
        if i < len(self.order):
            dev = (flip(w, self.order[i]), n)
            out = []
            for e in range(1 << i):
                blk = with_bits(w, self.order[:i], e)
                dst = self.part(self.out.at[blk])
                src = self.part(self.shard) if i == 0 else dst
                out.append(self.copy(src, dst, (1 << i) - 1 + e, dev))
            return out
        if self.split and i == len(self.order):
            ref = self.part(self.out)
            return [self.copy(ref, ref, self.wide - 1, (w, flip(n, 1)))]
        ref = self.part(self.out, quarter=False)
        return [self.copy(ref, ref, self.wide, (w, flip(n, 0)))]

    def own(self):
        w, _ = here()
        return pltpu.make_async_copy(self.part(self.shard), self.part(self.out.at[w]), self.local.at[self.a])

    def start(self, i):
        if i == 0:
            self.own().start()
        else:
            self.finish(i - 1)
            if i == 1:
                self.own().wait()
        for c in self.copies(i):
            c.start()

    def finish(self, i):
        for c in self.copies(i):
            c.wait_recv()

    def drain(self):
        for i in range(self.stages):
            for c in self.copies(i):
                c.wait_send()


class Total:
    def __init__(self, acc, slots, send, recv, wide, narrow):
        self.acc, self.slots, self.send, self.recv = acc, slots, send, recv
        self.bits = [("w", b) for b in range(wide.bit_length() - 1)] + [("n", b) for b in range(narrow.bit_length() - 1)]
        self.stages = len(self.bits)

    def copy(self, i):
        w, n = here()
        axis, b = self.bits[i]
        dev = (flip(w, b), n) if axis == "w" else (w, flip(n, b))
        return pltpu.make_async_remote_copy(self.acc.at[i], self.slots.at[i], self.send.at[i], self.recv.at[i],
                                            device_id=dev, device_id_type=MESH)

    def start(self, i):
        if i > 0:
            self.finish(i - 1)
        self.copy(i).start()

    def finish(self, i):
        self.copy(i).wait()
        self.acc[i + 1] = self.acc[i] + self.slots[i]


GATHERS = (
    (0, 0, (1, 2, 0), False),
    (1, 0, (2, 1, 0), True),
    (2, 0, (2, 0, 1), False),
    (3, 0, (1, 0, 2), False),
    (4, 0, (2, 1, 0), False),
    (4, 1, (1, 0, 2), True),
    (5, 0, (0, 1, 2), True),
    (5, 1, (2, 1, 0), True),
    (6, 0, (2, 1, 0), False),
    (6, 1, (2, 0, 1), False),
)
GATHER_PLAN = {
    ("begin", 0): [(1, 0), (0, 0)],
    ("onehot", 0): [(6, 0)],
    ("pre", 0): [(2, 0)],
    ("emb", 0): [(1, 1), (6, 1), (0, 1)],
    ("table", 0): [(2, 1)],
    ("plane", 6): [(7, 0)],
    ("plane", 7): [(1, 2)],
    ("plane", 10): [(6, 2)],
    ("rows", 1): [(2, 2)],
    ("rows", 5): [(0, 2)],
    ("rows", 9): [(1, 3)],
    ("project", 0): [(7, 1), (6, 3), (5, 0), (4, 0)],
    ("att", 0): [(9, 0), (3, 0), (5, 1)],
    ("att", 1): [(7, 2), (8, 0), (4, 1)],
    ("att", 3): [(6, 4)],
    ("att", 4): [(5, 2)],
    ("att", 5): [(3, 1)],
    ("att", 6): [(9, 1), (7, 3)],
    ("att", 8): [(8, 1)],
    ("att", 10): [(3, 2), (4, 2)],
    ("att", 12): [(9, 2)],
    ("att", 13): [(7, 4), (5, 3)],
    ("att", 16): [(8, 2)],
    ("att", 17): [(4, 3)],
    ("att", 20): [(5, 4)],
    ("att", 21): [(3, 3)],
    ("att", 23): [(9, 3), (8, 3)],
}


def chunk_region(weight, chunk, rows, cols):
    if weight < 4:
        return (0, rows, 0, cols)
    if weight < 6:
        return (0, rows, chunk * (cols // 2), cols // 2)
    return (chunk * (rows // 2), rows // 2, 0, cols)


def front_body(wide, narrow, len_ref, bcol_ref, emb_ref, small_ref,
               sq, sk, sv, so, sg, su, sd,
               oq, ok, ov, oo, og, ou, od,
               start_h, conv_h, csum_ref, tot_ref, smallall_ref, emball_ref,
               qs_h, k_h, v_h, ctx_h, qx_ref, normed_h, middle_h,
               start_ref, conv_ref, qs_ref, k_ref, v_ref, ctx_ref, normed_ref, middle_ref, osem,
               table, onehot, planes, coef, tiles, ent, kx, vext, kext, qxf, vq, vk, vv, vo,
               embs, smalls, tacc, tslots,
               gsend, grecv, glocal, psend, precv, tsend, trecv, wsem):
    w, n = here()
    embs[w] = emb_ref[...]
    smalls[w] = small_ref[...]
    greet(wide, True)
    shards, outs = (sq, sk, sv, so, sg, su, sd), (oq, ok, ov, oo, og, ou, od)
    gathers = [Gather(i, shards[a], outs[a], chunk_region(a, c, *shards[a].shape), order, split, (gsend, grecv, glocal))
               for i, (a, c, order, split) in enumerate(GATHERS)]
    tick = Ticker()
    started = [0] * len(gathers)

    half = emb_ref.shape[1] // 2
    hcols = pl.ds(pl.multiple_of(bit_of(n, 0) * half, 128), half)
    small_copies, emb_copies = [], []
    for d in range(1, wide):
        peer = (lax.rem(w + d, wide), n)
        emb_copies.append(pltpu.make_async_remote_copy(
            emb_ref.at[:, hcols], embs.at[w, :, hcols], psend.at[0, d], precv.at[0, d], device_id=peer, device_id_type=MESH))
        small_copies.append(pltpu.make_async_remote_copy(
            small_ref, smalls.at[w], psend.at[1, d], precv.at[1, d], device_id=peer, device_id_type=MESH))
    for c in emb_copies + small_copies:
        c.start()
    swap = pltpu.make_async_remote_copy(embs.at[:, :, hcols], embs.at[:, :, hcols], psend.at[0, 0], precv.at[0, 0],
                                        device_id=(w, flip(n, 0)), device_id_type=MESH)

    def params():
        tick("pre", 0)
        for c in emb_copies:
            c.wait_recv()
        swap.start()
        tick("emb", 0)
        for c in small_copies:
            c.wait_recv()
        per = 768 // wide
        l = lax.broadcasted_iota(jnp.int32, (128, 768), 0)
        c = lax.broadcasted_iota(jnp.int32, (128, 768), 1)
        small = sum(dot(smalls[i].astype(BF16), jnp.where((c == per * i + l) & (l < per), 1.0, 0.0).astype(BF16))
                    for i in range(wide))
        smallall_ref[...] = small
        swap.wait()
        emb = embs[...].astype(F32).reshape(256, 768)
        emball_ref[...] = emb.astype(BF16)
        return emb, small

    for (loop, at), stages in GATHER_PLAN.items():
        for g, s in stages:
            if s < gathers[g].stages:
                tick.add(loop, at, functools.partial(gathers[g].start, s))
                started[g] = s + 1
    weights = list(zip((0, 1, 2), outs[:3], (vq, vk, vv)))
    written = [pltpu.make_async_copy(s, d, osem.at[i]) for i, (s, d) in enumerate(
        ((start_ref, start_h), (conv_ref, conv_h), (normed_ref, normed_h), (qs_ref, qs_h), (k_ref, k_h), (v_ref, v_h),
         (ctx_ref, ctx_h), (middle_ref, middle_h)))]

    def write(ids):
        for i in ids:
            written[i].start()

    tick.add("project", 0, functools.partial(write, (0, 1)))
    tick.add("att", 0, functools.partial(write, (2, 3, 4, 5)))
    tick.add("outproj", 0, functools.partial(write, (6,)))

    def load(ws, sem0):
        copies = []
        for j, (_, src, dst) in enumerate(ws):
            r = src.shape[1]
            for i in range(wide):
                copies.append(pltpu.make_async_copy(src.at[i], dst.at[pl.ds(r * i, r)], wsem.at[sem0 + j, i]))
        return copies

    def ready(ids):
        for g in ids:
            for s in range(started[g], gathers[g].stages):
                gathers[g].start(s)
            gathers[g].finish(gathers[g].stages - 1)

    def qkv_ready():
        ready((0, 1, 2))
        cs = load(weights, 0)
        for c in cs:
            c.start()
        for c in cs:
            c.wait()

    tick.add("project", 0, qkv_ready)
    total = Total(tacc, tslots, tsend, trecv, wide, narrow)

    def total_begin():
        lane = lax.broadcasted_iota(jnp.int32, (8, 128), 1)
        tacc[0] = jnp.where(lane == 0, len_ref[0, 0].astype(F32), jnp.where(lane == 1, ent[...], 0.0))
        total.start(0)

    tick.add("att", 1, total_begin)
    for i in range(1, total.stages):
        tick.add("att", 1 + 2 * i, functools.partial(total.start, i))

    def out_ready():
        total.finish(total.stages - 1)
        tot_ref[...] = tacc[total.stages]
        ready((3,))
        cs = load([(3, outs[3], vo)], 3)
        for c in cs:
            c.start()
        for c in cs:
            c.wait()

    tick.add("outproj", 0, out_ready)
    tick("begin", 0)
    gbst_fwd_body(tick, params, len_ref, bcol_ref, start_ref, conv_ref, csum_ref, ent, table, onehot, planes, coef, tiles)
    att_fwd_body(tick, len_ref, start_ref, smallall_ref[pl.ds(5, 1), :], vq, vk, vv, vo,
                 qs_ref, k_ref, v_ref, ctx_ref, qx_ref, normed_ref, middle_ref, kx, vext, kext, qxf)
    write((7,))
    ready(range(4, len(gathers)))
    for c in written:
        c.wait()
    for c in emb_copies + small_copies:
        c.wait_send()
    for g in gathers:
        g.drain()


def front(wide, narrow, length, bcol, emb, small, shards):
    b = jax.ShapeDtypeStruct((TOK, 768), BF16)
    f = jax.ShapeDtypeStruct((TOK, 768), F32)
    gathered = tuple(jax.ShapeDtypeStruct((wide,) + s.shape, s.dtype) for s in shards)
    sq = pltpu.VMEM((768, 768), BF16)
    ng = len(GATHERS)
    dma = pltpu.SemaphoreType.DMA
    stages = (wide * narrow).bit_length() - 1
    return pl.pallas_call(
        functools.partial(front_body, wide, narrow),
        out_shape=gathered + (
            f, jax.ShapeDtypeStruct((PERIOD, GROUPS, 768), BF16), jax.ShapeDtypeStruct((GROUPS, 128), F32),
            jax.ShapeDtypeStruct((8, 128), F32), jax.ShapeDtypeStruct((8, 768), F32), jax.ShapeDtypeStruct((256, 768), BF16),
            b, b, b, b, jax.ShapeDtypeStruct((TOK, 128), BF16), b, f),
        in_specs=[SM] + [VM] * 10,
        out_specs=(HB,) * 9 + (VM,) * 4 + (HB,) * 4 + (VM, HB, HB),
        scratch_shapes=[
            pltpu.VMEM((TOK, 768), F32), pltpu.VMEM((PERIOD, GROUPS, 768), BF16)] + [pltpu.VMEM((TOK, 768), BF16)] * 5 + [
            pltpu.VMEM((TOK, 768), F32), dma((8,)),
            pltpu.VMEM((1024, 768), BF16), pltpu.VMEM((GROUPS, 256 * 15), BF16), pltpu.VMEM((PERIOD, GROUPS, 768), F32),
            pltpu.VMEM((4, GROUPS, 128), F32), pltpu.VMEM((6, 6 * GROUPS, 128), F32), pltpu.VMEM((8, 128), F32),
            pltpu.VMEM((TOK, 128), BF16), pltpu.VMEM((2, TOK, 256), BF16), pltpu.VMEM((2, TOK, 256), BF16),
            pltpu.VMEM((TOK, 128), F32), sq, sq, sq, sq,
            pltpu.VMEM((wide,) + emb.shape, BF16), pltpu.VMEM((wide, 8, 128), F32),
            pltpu.VMEM((stages + 1, 8, 128), F32), pltpu.VMEM((stages, 8, 128), F32),
            dma((ng, wide + 1)), dma((ng, wide + 1)), dma((ng,)), dma((2, wide)), dma((2, wide)), dma((stages,)), dma((stages,)),
            dma((4, wide))],
        compiler_params=pltpu.CompilerParams(vmem_limit_bytes=60 << 20, collective_id=0, has_side_effects=True),
        name="front",
    )(length, bcol, emb, small, *shards)


class Scatter:
    def __init__(self, index, data, out, region, order, early, bufs, sems, base=(0, 0)):
        self.a, self.data, self.out = index, data, out
        self.row, self.nrow, self.col, self.ncol = region
        self.wide = data.shape[0]
        self.order = wide_order(order, self.wide)
        self.nb = len(self.order)
        self.early = early_split(early, region)
        self.cb, self.wb, self.yb, self.fs, self.fb = bufs
        self.send, self.recv = sems
        self.base_row, self.base_col = base
        self.kinds = ["core"] + (["early"] if self.early else []) + [("wide", i) for i in range(self.nb)]
        self.kinds += ["join" if self.early else "late", "swap"]
        self.stages = len(self.kinds)

    def share(self, other=False):
        _, n = here()
        half = self.ncol // 2
        b0 = bit_of(n, 0)
        b0 = 1 - b0 if other else b0
        return pl.ds(self.row, self.nrow), pl.ds(pl.multiple_of(self.col + b0 * half, 128), half)

    def quarter(self, other=False, base=True):
        _, n = here()
        half = self.ncol // 2
        b1 = bit_of(n, 1)
        b1 = 1 - b1 if other else b1
        row, nrow, ncol = (self.row if base else 0), self.nrow, half
        col = self.col + bit_of(n, 0) * half if base else 0
        if self.early == "col":
            ncol = half // 2
            col = pl.multiple_of(col + b1 * ncol, 128)
        elif self.early == "row":
            nrow = nrow // 2
            row = pl.multiple_of(row + b1 * nrow, 8)
        if base:
            col = pl.multiple_of(col, 128)
        return pl.ds(row, nrow), pl.ds(col, ncol)

    def mine(self):
        return self.quarter() if self.early else self.share()

    def copy(self, src, dst, slot, device):
        return pltpu.make_async_remote_copy(src, dst, self.send.at[self.a, slot], self.recv.at[self.a, slot],
                                            device_id=device, device_id_type=MESH)

    def base(self, i):
        return sum(1 << (self.nb - 1 - j) for j in range(i))

    def copies(self, s):
        w, n = here()
        kind = self.kinds[s]
        W = self.wide
        if kind == "core":
            r, c = self.share(other=True)
            return [self.copy(self.data.at[:, r, c], self.cb, W - 1, (w, flip(n, 0)))]
        if kind == "early":
            r, c = self.quarter(other=True)
            return [self.copy(self.data.at[:, r, c], self.yb, W, (w, flip(n, 1)))]
        r, c = self.mine()
        if kind == "late":
            return [self.copy(self.data.at[w, r, c], self.yb, W, (w, flip(n, 1)))]
        if kind == "join":
            ref = self.fs.at[self.quarter(base=False)]
            return [self.copy(ref, ref, W + 1, (w, flip(n, 1)))]
        if kind == "swap":
            return [self.copy(self.fs, self.fb, W + 2, (w, flip(n, 0)))]
        i = kind[1]
        peer = flip(w, self.order[i])
        out = []
        for e in range(1 << (self.nb - 1 - i)):
            blk = with_bits(peer, self.order[i + 1:], e)
            out.append(self.copy(self.data.at[blk, r, c], self.wb.at[self.base(i) + e], self.base(i) + e, (peer, n)))
        return out

    def add(self, blk, where, term):
        idx = (blk,) + where
        self.data[idx] = (self.data[idx].astype(F32) + term.astype(F32)).astype(BF16)

    def combine(self, s):
        w, n = here()
        for c in self.copies(s):
            c.wait_recv()
        kind = self.kinds[s]
        if kind in ("core", "early"):
            where = self.share() if kind == "core" else self.quarter()
            if kind == "core" and self.early:
                pass
            buf = self.cb if kind == "core" else self.yb

            def block(b, _):
                self.add(b, where, buf[b])
                return 0

            lax.fori_loop(0, self.wide, block, 0)
        elif kind == "late":
            self.fs[...] = (self.data[(w,) + self.mine()].astype(F32) + self.yb[...].astype(F32)).astype(BF16)
        elif kind == "swap":
            b0, half = bit_of(n, 0), self.ncol // 2
            rows = pl.ds(self.row - self.base_row, self.nrow)
            for b, ref in ((b0, self.fs), (1 - b0, self.fb)):
                self.out[rows, pl.ds(pl.multiple_of(self.col - self.base_col + b * half, 128), half)] = ref[...]
        elif kind != "join":
            i = kind[1]
            for e in range(1 << (self.nb - 1 - i)):
                self.add(with_bits(w, self.order[i + 1:], e), self.mine(), self.wb[self.base(i) + e])
            if i == self.nb - 1 and self.early:
                self.fs[self.quarter(base=False)] = self.data[(w,) + self.mine()]

    def start(self, s):
        if s > 0:
            self.combine(s - 1)
        for c in self.copies(s):
            c.start()

    def finish(self):
        self.combine(self.stages - 1)

    def drain(self):
        for s in range(self.stages):
            for c in self.copies(s):
                c.wait_send()


def early_split(early, region):
    if not early:
        return None
    if region[3] % 512 == 0:
        return "col"
    return "row" if region[1] % 32 == 0 else None


def scatter_buffers(wide, region, early):
    _, nrow, _, ncol = region
    half = ncol // 2
    kind = early_split(early, region)
    qr, qc = (nrow // 2, half) if kind == "row" else (nrow, half // 2) if kind == "col" else (nrow, half)
    y = (wide, qr, qc) if kind else (nrow, half)
    return [pltpu.VMEM((wide, nrow, half), BF16), pltpu.VMEM((wide - 1, qr, qc), BF16), pltpu.VMEM(y, BF16),
            pltpu.VMEM((nrow, half), BF16), pltpu.VMEM((nrow, half), BF16)]


SCATTERS = (
    (0, 0, (2, 1, 0), False),
    (0, 1, (1, 0, 2), False),
    (1, 0, (1, 0, 2), False),
    (1, 1, (1, 0, 2), True),
    (2, 0, (0, 1, 2), True),
    (2, 1, (0, 1, 2), False),
    (3, 0, (1, 2, 0), False),
    (4, 0, (1, 0, 2), False),
    (5, 0, (0, 1, 2), True),
    (6, 0, (0, 1, 2), False),
    (4, 1, (0, 1, 2), False),
    (5, 1, (2, 0, 1), False),
    (6, 1, (1, 2, 0), False),
)
SCATTER_PLAN = {
    ("ffn", 8): [(2, 0), (0, 0)],
    ("ffn", 11): [(2, 1), (0, 1)],
    ("fin", 0): [(1, 0), (5, 0), (3, 0), (4, 0)],
    ("gout", 0): [(6, 0)],
    ("head", 2): [(2, 2), (0, 2)],
    ("head", 3): [(1, 1), (5, 1), (3, 1), (4, 1)],
    ("bwd", 0): [(6, 1)],
    ("bwd", 3): [(2, 3), (0, 3)],
    ("bwd", 4): [(5, 2)],
    ("bwd", 5): [(0, 4)],
    ("bwd", 6): [(3, 2), (4, 2)],
    ("bwd", 7): [(1, 2), (6, 2), (2, 4), (0, 5)],
    ("mid", 0): [(5, 3), (9, 0), (2, 5), (7, 0), (4, 3), (8, 0), (0, 6)],
    ("bwd", 9): [(1, 3), (3, 3), (6, 3), (2, 6)],
    ("bwd", 10): [(9, 1), (7, 1), (8, 1)],
    ("bwd", 11): [(5, 4), (4, 4)],
    ("wgrad", 0): [(10, 0), (11, 0), (1, 4), (3, 4), (6, 4), (12, 0)],
    ("last", 0): [(9, 2), (8, 2)],
    ("last", 1): [(5, 5), (7, 2), (4, 5)],
    ("last", 2): [(10, 1), (11, 1), (12, 1)],
    ("last", 3): [(5, 6)],
    ("first", 0): [(3, 5), (9, 3), (6, 5), (8, 3)],
    ("first", 1): [(1, 5), (4, 6)],
    ("first", 3): [(7, 3)],
    ("first", 5): [(10, 2), (6, 6)],
    ("first", 7): [(1, 6), (4, 7)],
    ("first", 8): [(11, 2), (12, 2)],
    ("first", 10): [(3, 6)],
    ("second", 0): [(9, 4), (8, 4)],
    ("second", 3): [(3, 7)],
    ("second", 4): [(7, 4)],
    ("second", 5): [(10, 3), (11, 3)],
    ("second", 8): [(12, 3)],
    ("taps", 0): [(9, 5), (8, 5)],
    ("taps", 2): [(10, 4), (11, 4), (7, 5)],
    ("taps", 3): [(12, 4)],
}
PADROWS = 6 * GROUPS
FROWS = 1024
KROWS = 512


def scatter_place(weight, chunk, wide):
    per = 768 // wide
    if weight < 2:
        return (0, per, chunk * 1024, 1024), (0, 0)
    if weight == 2:
        rows = 2048 // wide
        return (chunk * (rows // 2), rows // 2, 0, 768), (0, 0)
    if weight == 3:
        return (0, per, 0, 768), (0, 0)
    return ((0, per, 0, 512) if chunk == 0 else (0, per, 512, 256)), (0, 0)


def rest_body(wide, *refs):
    (len_ref, invc_ref, small_ref, brow_ref, csum_ref, emb_h, qx_h, middle_h, cot_h, start_h, qs_h, k_h, v_h, ctx_h,
     normed_h, conv_h, wg_h, wu_h, wd_h, wq_h, wk_h, wv_h, wo_h), refs = refs[:23], refs[23:]
    (out_h, *shard, gembs, smalls), refs = refs[:10], refs[10:]
    (f0, f1, f2, tiles, x1, x2, x3, n2t, qcat, ocat, dqt, gg, gu, gd, go, gq, gk, gv,
     gconv, gscore, gg1, gg2, lsem, wsem,
     cb, esend, eb, ysend, yb, fs, fb, sall, sb, ssum, yss), refs = refs[:35], refs[35:]
    bufs, (ssend, srecv, dsend, drecv) = refs[:-4], refs[-4:]
    w, n = here()
    greet(wide, True)
    tick = Ticker()
    datas = (gg, gu, gd, go, gq, gk, gv)
    scatters = []
    for i, (a, c, order, early) in enumerate(SCATTERS):
        region, base = scatter_place(a, c, wide)
        scatters.append(Scatter(i, datas[a], shard[a], region, order, early, bufs[5 * i:5 * i + 5], (ssend, srecv), base))
    started = [0] * len(scatters)
    for (loop, at), stages in SCATTER_PLAN.items():
        for g, s in stages:
            if s == scatters[g].stages:
                tick.add(loop, at, scatters[g].finish)
                started[g] = s + 1
            elif s < scatters[g].stages:
                tick.add(loop, at, functools.partial(scatters[g].start, s))
                started[g] = s + 1

    def complete(ids):
        for s in range(16):
            for g in ids:
                sc = scatters[g]
                if started[g] <= s < sc.stages:
                    sc.start(s)
                elif s == sc.stages and started[g] <= s:
                    sc.finish()
                    started[g] = 99

    def local(src, dst, i):
        return pltpu.make_async_copy(src, dst, lsem.at[i])

    top_rows, low_rows = pl.ds(0, TOK), pl.ds(TOK, TOK)

    g2 = small_ref[pl.ds(6, 1), :]
    n2, top = x1.at[top_rows], x1.at[low_rows]
    hdd = x2.at[top_rows]
    per = 768 // wide
    ntile = wd_h.shape[0] // BLK

    def weight_tiles(f, slot):
        fs_ = pl.ds(pl.multiple_of(f * BLK, BLK), BLK)
        return [pltpu.make_async_copy(wg_h.at[:, fs_], x3.at[pl.ds(768 * slot, 768), pl.ds(0, BLK)], wsem.at[slot, 0]),
                pltpu.make_async_copy(wu_h.at[:, fs_], x3.at[pl.ds(768 * slot, 768), pl.ds(BLK, BLK)], wsem.at[slot, 1]),
                pltpu.make_async_copy(wd_h.at[fs_, :], x2.at[pl.ds(TOK + BLK * slot, BLK), :], wsem.at[slot, 2])]

    loads = [local(middle_h, f0.at[top_rows], 0), local(cot_h, f1.at[top_rows], 1)]
    for c in loads:
        c.start()
    for c in weight_tiles(0, 0):
        c.start()
    for c in loads:
        c.wait()

    def prep(r, _):
        rs = pl.ds(pl.multiple_of(r * BLK, BLK), BLK)
        x = f0[rs, :]
        nn = x * rms_parts(x) * g2
        n2[rs, :] = nn.astype(BF16)
        n2t[:, rs] = nn.T.astype(BF16)
        top[rs, :] = f1[rs, :].astype(BF16)
        for lt in range(6):
            tiles[lt, rs, :] = x[:, 128 * lt:128 * lt + 128]
        f2[rs, :] = jnp.zeros((BLK, 768), F32)
        return 0

    lax.fori_loop(0, TOK // BLK, prep, 0)
    tick("prep", 0)

    def ffn_tile(f, slot):
        for c in weight_tiles(f, slot):
            c.wait()

        @pl.when(f + 1 < ntile)
        def _():
            for c in weight_tiles(f + 1, 1 - slot):
                c.start()

        wg = x3.at[pl.ds(768 * slot, 768), pl.ds(0, BLK)]
        wu = x3.at[pl.ds(768 * slot, 768), pl.ds(BLK, BLK)]
        wd = x2.at[pl.ds(TOK + BLK * slot, BLK), :]

        tick("ffn", 2 * f)

        def rows(r, _):
            rs = pl.ds(pl.multiple_of(r * FROWS, FROWS), FROWS)
            nn = n2[rs, :]
            v = dot(nn, wg[...])
            u = dot(nn, wu[...])
            dh = dot(top[rs, :], wd[...], ((1,), (1,)))
            v2 = v * v
            t = jnp.tanh(v * (C0 + (C0 * C1) * v2))
            hp = 0.5 + 0.5 * t
            gelu = v * hp
            slope = hp + (0.5 * v) * (1.0 - t * t) * (C0 + (3.0 * C0 * C1) * v2)
            h = (gelu * u).astype(BF16)
            a = (dh * u * slope).astype(BF16)
            b = (dh * gelu).astype(BF16)
            hdd[rs, pl.ds(0, BLK)] = h
            hdd[rs, pl.ds(BLK, BLK)] = a
            hdd[rs, pl.ds(2 * BLK, BLK)] = b
            o = dot(h, wd[...])
            for lt in range(6):
                tiles[lt, rs, :] += o[:, 128 * lt:128 * lt + 128]
            f2[rs, :] += dot(a, wg[...], ((1,), (1,))) + dot(b, wu[...], ((1,), (1,)))
            return 0

        lax.fori_loop(0, TOK // FROWS, rows, 0)
        tick("ffn", 2 * f + 1)
        cols = pl.ds(pl.multiple_of(f * BLK, BLK), BLK)
        for j, ref in ((1, gg), (2, gu)):
            res = dot(n2t[...], hdd[:, pl.ds(j * BLK, BLK)])
            for i in range(wide):
                ref[i, :, cols] = res[per * i:per * i + per].astype(BF16)
        res = dot(hdd[:, pl.ds(0, BLK)], top[...], ((0,), (0,)))
        high = 2048 // wide
        for i in range(BLK // high):
            gd[f * (BLK // high) + i] = res[high * i:high * i + high].astype(BF16)

    def tile_pair(i, _):
        ffn_tile(2 * i, 0)
        ffn_tile(2 * i + 1, 1)
        return 0

    lax.fori_loop(0, ntile // 2, tile_pair, 0)
    q, k, v, ctx, normed, low = [x.at[r] for x in (x1, x2, x3) for r in (top_rows, low_rows)]
    loads = [local(h, d, i) for i, (h, d) in enumerate(
        ((qs_h, q), (k_h, k), (v_h, v), (ctx_h, ctx), (normed_h, normed), (wo_h, n2t.at[:, pl.ds(0, 768)]),
         (qx_h, qcat.at[:, pl.ds(128, 128)])))]
    for c in loads:
        c.start()
    stores = [local(tiles.at[lt, top_rows, :], out_h.at[:, pl.ds(128 * lt, 128)], 8 + lt) for lt in range(6)]
    for c in stores:
        c.start()
    tick("fin", 0)
    gg2[...] = jnp.zeros_like(gg2)

    def fin(r, _):
        rs = pl.ds(pl.multiple_of(r * BLK, BLK), BLK)
        dxv, part = rms_back(f0[rs, :], g2, f2[rs, :])
        f1[rs, :] += dxv
        gg2[...] += part
        return 0

    lax.fori_loop(0, TOK // BLK, fin, 0)
    start_load = local(start_h, f0.at[top_rows], 7)
    start_load.start()
    for c in loads:
        c.wait()

    wo = n2t.at[:, pl.ds(0, 768)]
    length = len_ref[0, 0]

    def lower(r, _):
        rs = pl.ds(pl.multiple_of(r * BLK, BLK), BLK)
        low[rs, :] = f1[rs, :].astype(BF16)
        return 0

    lax.fori_loop(0, TOK // BLK, lower, 0)
    whole = dot(ctx[...], low[...], ((0,), (0,))).astype(BF16)
    for c in range(wide):
        go[c] = whole[per * c:per * c + per]
    tick("gout", 0)
    lane_s = lax.broadcasted_iota(jnp.int32, (768, 128), 1)
    row_s = lax.broadcasted_iota(jnp.int32, (768, 128), 0)
    sel = jnp.where(lane_s // 3 == row_s // 64, 1.0, 0.0).astype(BF16)
    lane_b = lax.broadcasted_iota(jnp.int32, (BLK, 128), 1)
    row_b = lax.broadcasted_iota(jnp.int32, (BLK, 128), 0)

    def head(r, _):
        tick("head", r)
        rs = pl.ds(pl.multiple_of(r * BLK, BLK), BLK)
        d = dot(low[rs, :], wo[...], ((1,), (1,))).astype(BF16)
        prod = d.astype(F32) * ctx[rs, :].astype(F32)
        ctx[rs, :] = d
        hi = prod.astype(BF16)
        delta = dot(hi, sel) + dot((prod - hi.astype(F32)).astype(BF16), sel)
        a, b, c = split3(-delta)
        ocat[rs, pl.ds(128, 128)] = jnp.where(lane_b % 3 == 0, a, jnp.where(lane_b % 3 == 1, b, c)).astype(BF16)
        return 0

    lax.fori_loop(0, TOK // BLK, head, 0)
    late_loads = [local(wk_h, x3.at[pl.ds(TOK, 768)], 0), local(wv_h, n2t.at[:, pl.ds(0, 768)], 1)]
    for c in late_loads:
        c.start()

    lane_k = lax.broadcasted_iota(jnp.int32, (KROWS, 128), 1)
    row_k = lax.broadcasted_iota(jnp.int32, (KROWS, 128), 0)

    def pair(p, _):
        ls = pl.ds(pl.multiple_of(p * 128, 128), 128)
        qcat[:, pl.ds(0, 128)] = q[:, ls]
        ocat[:, pl.ds(0, 128)] = ctx[:, ls]
        dqt[...] = jnp.zeros_like(dqt)

        def kblock(r, _):
            tick("bwd", 2 * p + r)
            rs = pl.ds(pl.multiple_of(r * KROWS, KROWS), KROWS)
            bias = jnp.where((lane_k == 0) & (2 * (row_k + r * KROWS) >= length), NEG, 0.0)
            dvb = jnp.zeros((KROWS, 128), F32)
            dkb = jnp.zeros((KROWS, 128), F32)
            dqb = dqt[...]
            for h2 in range(2):
                hm = head_lanes(h2, KROWS)
                hd = 3 * (2 * p + h2)
                km = k[rs, ls] * hm
                vm = v[rs, ls] * hm
                kxl = jnp.where((lane_k > hd) & (lane_k <= hd + 3), 1.0, bias).astype(BF16)
                vxl = jnp.where((lane_k >= hd) & (lane_k < hd + 3), 1.0, 0.0).astype(BF16)
                st = dot(jnp.concatenate([km, kxl], axis=1), qcat[...], ((1,), (1,)))
                dp = dot(jnp.concatenate([vm, vxl], axis=1), ocat[...], ((1,), (1,)))
                prob = jnp.exp(st)
                dsc = (prob * dp).astype(BF16)
                dvb = dvb + dot(prob.astype(BF16), ocat[:, pl.ds(0, 128)]) * hm.astype(F32)
                dkb = dkb + dot(dsc, qcat[:, pl.ds(0, 128)]) * hm.astype(F32)
                dqb = dqb + dot(km, dsc, ((0,), (0,)))
            v[rs, ls] = dvb.astype(BF16)
            k[rs, ls] = dkb.astype(BF16)
            dqt[...] = dqb
            return 0

        lax.fori_loop(0, TOK // KROWS, kblock, 0)
        q[:, ls] = (dqt[...].T * 0.125).astype(BF16)
        return 0

    def wgrad(c, _):
        cs = pl.ds(pl.multiple_of(c * BLK, BLK), BLK)
        for src, ref in ((q, gq), (k, gk), (v, gv)):
            res = dot(normed[...], src[:, cs], ((0,), (0,))).astype(BF16)
            for i in range(wide):
                ref[i, :, cs] = res[per * i:per * i + per]
        return 0

    lax.fori_loop(0, 4, pair, 0)
    lax.fori_loop(0, 2, wgrad, 0)
    tick("mid", 0)
    lax.fori_loop(4, HEADS // 2, pair, 0)
    wq_load = local(wq_h, x2.at[pl.ds(TOK, 768)], 2)
    wq_load.start()
    lax.fori_loop(2, 3, wgrad, 0)
    tick("wgrad", 0)
    start_load.wait()
    for c in late_loads + [wq_load]:
        c.wait()
    for c in stores:
        c.wait()
    gg1[...] = jnp.zeros_like(gg1)
    g1 = small_ref[pl.ds(5, 1), :]
    wq, wk, wv = x2.at[pl.ds(TOK, 768)], x3.at[pl.ds(TOK, 768)], n2t.at[:, pl.ds(0, 768)]

    def last(r, _):
        tick("last", r)
        rs = pl.ds(pl.multiple_of(r * BLK, BLK), BLK)
        d = (dot(q[rs, :], wq[...], ((1,), (1,))) + dot(k[rs, :], wk[...], ((1,), (1,)))
             + dot(v[rs, :], wv[...], ((1,), (1,))))
        dxv, part = rms_back(f0[rs, :], g1, d)
        res = f1[rs, :] + dxv
        for lt in range(6):
            tiles[lt, rs, :] = res[:, 128 * lt:128 * lt + 128]
        gg1[...] += part
        return 0

    lax.fori_loop(0, TOK // BLK, last, 0)
    conv = x3.at[pl.ds(0, PERIOD * GROUPS)]
    emb = x2.at[pl.ds(TOK, 256)]
    final_loads = [local(conv_h, conv, 14), local(emb_h, emb, 15)]
    for c in final_loads:
        c.start()
    for lt in range(6):
        tiles[lt, pl.ds(TOK, PADROWS - TOK), :] = jnp.zeros((PADROWS - TOK, 128), F32)
    for c in final_loads:
        c.wait()

    gemb = f0.at[pl.ds(0, 256)]
    gbst_bwd_body(tick, len_ref, invc_ref, brow_ref, emb, small_ref.at[pl.ds(0, 4)], small_ref.at[pl.ds(4, 1)],
                  conv, csum_ref, gemb, gconv, gscore, f2, Planes(f1, 128), Planes(f1, 0), x1, x2, tiles)

    def copy(src, dst, kk, slot, device):
        return pltpu.make_async_remote_copy(src, dst, dsend.at[kk, slot], drecv.at[kk, slot],
                                            device_id=device, device_id_type=MESH)

    half = 384
    gc = lambda b: pl.ds(pl.multiple_of(b * half, 128), half)
    b0 = bit_of(n, 0)
    esend[...] = gemb[:, gc(1 - b0)].astype(BF16).reshape(esend.shape)
    core = copy(esend, cb, 0, 0, (w, flip(n, 0)))
    core.start()
    r8 = lax.broadcasted_iota(jnp.int32, (8, 768), 0)
    total = gconv[...] * jnp.where(r8 < 4, 1.0, 0.0)
    for row, ref in ((4, gscore), (5, gg1), (6, gg2)):
        total = jnp.where(r8 == row, jnp.sum(ref[...], axis=0, keepdims=True), total)
    rl = lax.broadcasted_iota(jnp.int32, (768, 128), 0)
    cl = lax.broadcasted_iota(jnp.int32, (768, 128), 1)
    for i in range(wide):
        sall[i] = dot(total, jnp.where((rl == per * i + cl) & (cl < per), 1.0, 0.0).astype(F32), precision=HIGH)
    peers = [(lax.rem(w + d, wide), n) for d in range(1, wide)]
    small_copies = [copy(sall.at[p[0]], sb.at[w], 1, d + 1, p) for d, p in enumerate(peers)]
    for c in small_copies:
        c.start()
    core.wait()
    esend[...] = (gemb[:, gc(b0)].reshape(esend.shape) + cb[...].astype(F32)).astype(BF16)
    emb_copies = [copy(esend.at[p[0]], eb.at[w], 2, d + 1, p) for d, p in enumerate(peers)]
    for c in emb_copies:
        c.start()
    sb[w] = sall[w]
    eb[w] = esend[w]
    complete(range(len(scatters)))
    for c in small_copies + emb_copies:
        c.wait_recv()
    ysend[...] = sum(eb[i].astype(F32) for i in range(wide))
    ssum[0] = sum(sb[i] for i in range(wide))
    late = [copy(ysend, yb, 3, 0, (w, flip(n, 1))), copy(ssum.at[0], yss.at[0], 3, 1, (w, flip(n, 1)))]
    for c in late:
        c.start()
    for c in late:
        c.wait_recv()
    fs[...] = (ysend[...] + yb[...]).astype(BF16)
    ssum[1] = ssum[0] + yss[0]
    swap = [copy(fs, fb, 4, 0, (w, flip(n, 0))), copy(ssum.at[1], yss.at[1], 4, 1, (w, flip(n, 0)))]
    for c in swap:
        c.start()
    for c in swap:
        c.wait_recv()
    gembs[:, gc(b0)] = fs[...]
    gembs[:, gc(1 - b0)] = fb[...]
    smalls[...] = ssum[1] + yss[1]
    for c in small_copies + emb_copies + late + swap:
        c.wait_send()
    for g in range(len(scatters)):
        scatters[g].drain()


def rest(wide, args):
    rows, per, high = 256 // wide, 768 // wide, 2048 // wide
    bufs = []
    for a, c, _, early in SCATTERS:
        bufs += scatter_buffers(wide, scatter_place(a, c, wide)[0], early)
    v = pltpu.VMEM
    dma = pltpu.SemaphoreType.DMA
    ns = len(SCATTERS)
    shape = lambda *s: jax.ShapeDtypeStruct(s, BF16)
    return pl.pallas_call(
        functools.partial(rest_body, wide),
        out_shape=(jax.ShapeDtypeStruct((TOK, 768), F32), shape(per, 2048), shape(per, 2048), shape(high, 768),
                   shape(per, 768), shape(per, 768), shape(per, 768), shape(per, 768), shape(rows, 768),
                   jax.ShapeDtypeStruct((8, 128), F32)),
        in_specs=[SM, SM] + [VM] * 3 + [HB] * 18,
        out_specs=(HB,) + (VM,) * 9,
        scratch_shapes=[
            v((PADROWS, 768), F32), v((PADROWS, 768), F32), v((PADROWS, 768), F32), v((6, PADROWS, 128), F32),
            v((2304, 768), BF16), v((2 * TOK, 768), BF16), v((2112, 768), BF16), v((768, TOK), BF16),
            v((TOK, 256), BF16), v((TOK, 256), BF16), v((128, TOK), F32),
            v((wide, per, 2048), BF16), v((wide, per, 2048), BF16), v((wide, high, 768), BF16), v((wide, per, 768), BF16),
            v((wide, per, 768), BF16), v((wide, per, 768), BF16), v((wide, per, 768), BF16),
            v((8, 768), F32), v((8, 768), F32), v((8, 768), F32), v((8, 768), F32), dma((16,)), dma((2, 3)),
            v((wide, rows, 384), BF16), v((wide, rows, 384), BF16), v((wide, rows, 384), BF16), v((rows, 384), F32),
            v((rows, 384), F32), v((rows, 384), BF16), v((rows, 384), BF16), v((wide, 8, 128), F32), v((wide, 8, 128), F32),
            v((2, 8, 128), F32), v((2, 8, 128), F32)]
        + bufs + [dma((ns, wide + 3)), dma((ns, wide + 3)), dma((5, wide)), dma((5, wide))],
        compiler_params=pltpu.CompilerParams(vmem_limit_bytes=64 << 20, collective_id=1, has_side_effects=True),
        name="rest",
    )(*args)


def finish_body(wide, out_ref, *refs):
    shard, (gembs, smalls, tot), refs = refs[:7], refs[7:10], refs[10:]
    (res, ent, emb, conv, score, g1, g2), outs = refs[:7], refs[7:14]
    per = 768 // wide
    res[...] = out_ref[...]
    for src, dst in zip(shard, outs):
        dst[...] = src[...].astype(F32)
    emb[...] = gembs[...].astype(F32)
    ent[0, 0] = tot[0, 1] / tot[0, 0]
    conv[...] = smalls[pl.ds(0, 4), pl.ds(0, per)]
    score[...] = smalls[pl.ds(4, 1), pl.ds(0, per)]
    g1[...] = smalls[pl.ds(5, 1), pl.ds(0, per)]
    g2[...] = smalls[pl.ds(6, 1), pl.ds(0, per)]


def finish(wide, out, shards, gembs, smalls, tot):
    rows, per = 256 // wide, 768 // wide
    f = lambda *s: jax.ShapeDtypeStruct(s, F32)
    return pl.pallas_call(
        functools.partial(finish_body, wide),
        out_shape=(f(TOK, 768), f(1, 1), f(rows, 768), f(4, per), f(1, per), f(1, per), f(1, per))
        + tuple(f(*s.shape) for s in shards),
        in_specs=[VM] * 10 + [SM],
        out_specs=(VM, SM) + (VM,) * 12,
        compiler_params=pltpu.CompilerParams(vmem_limit_bytes=60 << 20),
        name="finish",
    )(out, *shards, gembs, smalls, tot)


def body(
    wide, narrow,
    byte_values, row_lengths, embedding, conv_kernel, score_vector, attn_gain, query_weight, key_weight,
    value_weight, output_weight, ffn_gain, gate_weight, up_weight, down_weight, cotangent,
):
    length = row_lengths.reshape(1, 1)
    bcol, brow = byte_planes(byte_values[0], row_lengths[0])
    small = jnp.concatenate([conv_kernel, score_vector[None], attn_gain[None], ffn_gain[None]], axis=0).astype(F32)
    small = jnp.pad(small, ((0, 8 - small.shape[0]), (0, 128 - small.shape[1])))
    shards = (query_weight, key_weight, value_weight, output_weight, gate_weight, up_weight, down_weight)
    got = front(wide, narrow, length, bcol, embedding, small, shards)
    wq, wk, wv, wo, wg, wu, wd = [x.reshape(-1, x.shape[-1]) for x in got[:7]]
    start, conv, csum, tot, smallall, emb, qs, k, v, ctx, qx, normed, middle = got[7:]
    invc = (ENT_WEIGHT / tot[0, 0]).reshape(1, 1)
    out, *rest_out = rest(wide, (length, invc, smallall, brow, csum, emb, qx, middle, cotangent[0], start, qs, k, v, ctx,
                                 normed, conv.reshape(PERIOD * GROUPS, 768), wg, wu, wd, wq, wk, wv, wo))
    shard, (gembs, smalls) = rest_out[:7], rest_out[7:]
    res, ent, ge, gc, gs, gg1, gg2, sg, su, sd, so, sq, sk, sv = finish(wide, out, shard, gembs, smalls, tot)
    flat = lambda x: x.reshape(-1)
    return (res[None], ent.reshape(()), ge, gc, flat(gs), flat(gg1), sq, sk, sv, so, flat(gg2), sg, su, sd)


def solution(mesh):
    both = ("wide", "narrow")
    row, flat = P("wide", None), P("wide")
    return jax.shard_map(
        functools.partial(body, mesh.shape["wide"], mesh.shape["narrow"]),
        mesh=mesh,
        in_specs=(P(both, None), P(both), row, P(None, "wide"), flat, flat, row, row, row, row, flat,
                  row, row, row, P(both, None, None)),
        out_specs=(P(both, None, None), P(), row, P(None, "wide"), flat, flat, row, row, row, row, flat,
                   row, row, row),
        check_vma=False,
    )
```
